32 devices in a mesh: crops: 2 (over y), row: 8 (over z, x), col: 2 (over core).
Axes of the slice: x: 2, y: 2, z: 4, core: 2. Of those that a mesh axis runs over, the one named last changes fastest.
Arguments:
- pair: bfloat16 [736, 368, 128], P(('crops', 'row'), 'col'), parts along dimension 0, may hold values from -6 to 6
- chain_lengths: int32 [10], P('crops'), parts along dimension 0, may hold values from 1 to 184, 368 in all
- in_weight: bfloat16 [128, 640], replicated, may hold values from -0.5 to 0.5
- out_weight: bfloat16 [128, 128], replicated, may hold values from -0.5 to 0.5
- trans_in: bfloat16 [128, 1024], replicated, may hold values from -0.5 to 0.5
- trans_out: bfloat16 [512, 128], replicated, may hold values from -0.25 to 0.25
Outputs:
- pair_out: bfloat16 [736, 368, 128], P(('crops', 'row'), 'col'), parts along dimension 0
The draws below stay inside these ranges and needn't reach their ends.
There are 2 independent parts, one for each index of `crops`. The reference program is written for one: setup_inputs(seed, part) draws one part's arguments, and reference() takes and returns one part's arrays. A program takes and returns all parts, laid end to end along the dimension named above; an argument that names none is the same for every part. Nothing has to cross between parts.
Inputs may be any that keep to these rules, and one draw needn't show every extreme that they name: `chain_lengths`: the entries sum to 368; the last entry counts padding tokens at the end of the crop, the others count tokens of chains.
All inputs are finite; a program needn't handle non-finite values.
Results may differ from the reference program's by a relative error of at most 0.0056.
Values may be sent and summed in bfloat16 or wider, within the bound.
No kernel may reach another device: no remote copies, remote signals or barrier semaphores. Data moves between devices by JAX's collectives and lax.ppermute only.
A program may use at most 192 MiB of HBM per device.

```python
import math
import jax
import jax.numpy as jnp
import numpy as np
from jax import lax

CH = 128
HID = 512
CHAINS = 5
N_TOK = 368


def shard_levels(stream_key, dims, cuts, smallest, largest):
    factor_of, own = 1.0, jax.random.fold_in(stream_key, 6)
    for position, parts in cuts:
        steps = jnp.exp(jax.random.uniform(jax.random.fold_in(own, position), (parts,), jnp.float32, smallest / len(cuts), largest / len(cuts)))
        factor_of = factor_of * jnp.repeat(steps, dims[position] // parts).reshape([-1 if axis == position else 1 for axis in range(len(dims))])
    return factor_of


def profile(number_of, total, reach, lean):
    loads = [(1 << 20) // math.isqrt(standing ** lean) + 1 for standing in range(2, number_of + 1)]
    spare, given = total - reach - (number_of - 1), [1] * (number_of - 1)
    while spare > 0:
        free = [i for i in range(number_of - 1) if given[i] < reach]
        mass, remaining = sum([loads[i] for i in free]), spare
        for i in free:
            extra = min(reach - given[i], max(1, remaining * loads[i] // mass), spare)
            given[i] = given[i] + extra
            spare = spare - extra
    return np.array([reach] + given)


def ragged(own_key, number_of, total, most, skew):
    if number_of == 2:
        one = jax.random.randint(own_key, (), max(1, total - most), min(most, total - 1) + 1)
        return jnp.stack([one, total - one])
    tallies = jnp.asarray(profile(number_of, total, most, skew), jnp.int32)
    couples = (number_of - 1) // 2
    source_of, sink = tallies[1:1 + 2 * couples:2], tallies[2:2 + 2 * couples:2]
    margin = jnp.minimum(source_of - 1, most - sink)
    shifted = jax.random.randint(jax.random.fold_in(own_key, 1), (couples,), 0, 1 << 20) % (margin + 1)
    tallies = tallies.at[1:1 + 2 * couples:2].set(source_of - shifted).at[2:2 + 2 * couples:2].set(sink + shifted)
    return tallies[jax.random.permutation(jax.random.fold_in(own_key, 2), number_of)]


def noise(own_key, extent, scale, reach, shards=(), kind=jnp.bfloat16):
    drawn = scale * jax.random.normal(own_key, extent, jnp.float32)
    if shards:
        drawn = drawn * shard_levels(own_key, extent, shards, -0.22, 0.18)
    return jnp.clip(drawn, -reach, reach).astype(kind)


def setup_inputs(seed: int = 0, part: int = 0) -> dict:
    splits = jax.random.split(jax.random.key(seed), 7)
    part_splits = jax.random.split(jax.random.fold_in(splits[6], part), 7)
    return {
        "pair": noise(part_splits[0], (N_TOK, N_TOK, CH), 1.0, 6.0, ((0, 8), (1, 2))),
        "chain_lengths": ragged(part_splits[1], CHAINS, N_TOK, N_TOK // 2, 0).astype(jnp.int32),
        "in_weight": noise(splits[2], (CH, 5 * CH), CH ** -0.5, 0.5),
        "out_weight": noise(splits[3], (CH, CH), CH ** -0.5, 0.5),
        "trans_in": noise(splits[4], (CH, 2 * HID), CH ** -0.5, 0.5),
        "trans_out": noise(splits[5], (HID, CH), HID ** -0.5, 0.25),
    }


def layer_norm(values):
    centered = values - lax.optimization_barrier(jnp.mean(values, axis=-1, keepdims=True))
    variance = lax.optimization_barrier(jnp.mean(centered * centered, axis=-1, keepdims=True))
    return centered * lax.rsqrt(variance + 1e-05)

def reference(pair, chain_lengths, in_weight, out_weight, trans_in, trans_out):
    tokens = pair.shape[0]
    width = pair.shape[2]
    hidden_units = trans_out.shape[0]
    valid_tokens = (jnp.arange(tokens) < tokens - chain_lengths[CHAINS - 1]).astype(jnp.float32)

    def project_row(inputs):
        row_pair, row_valid = inputs
        normed = layer_norm(row_pair.astype(jnp.float32)).astype(jnp.bfloat16)
        projected = jnp.dot(normed, in_weight, preferred_element_type=jnp.float32)
        row_mask = (row_valid * valid_tokens)[:, None]
        left_ops = (jax.nn.sigmoid(projected[:, :width]) * projected[:, width:2 * width] * row_mask).astype(jnp.bfloat16)
        right_ops = (jax.nn.sigmoid(projected[:, 2 * width:3 * width]) * projected[:, 3 * width:4 * width] * row_mask).astype(jnp.bfloat16)
        out_gate = jax.nn.sigmoid(projected[:, 4 * width:])
        return (left_ops, right_ops, out_gate)
    left_ops, right_ops, out_gate = lax.map(project_row, (pair, valid_tokens))
    triangle = jnp.einsum('ikc,jkc->ijc', left_ops.astype(jnp.float32), right_ops.astype(jnp.float32), precision=lax.Precision.HIGHEST)

    def finish_row(inputs):
        row_pair, row_tri, row_gate = inputs
        tri_normed = layer_norm(row_tri).astype(jnp.bfloat16)
        updated = row_pair.astype(jnp.float32) + row_gate * jnp.dot(tri_normed, out_weight, preferred_element_type=jnp.float32)
        trans_normed = layer_norm(updated).astype(jnp.bfloat16)
        expanded = jnp.dot(trans_normed, trans_in, preferred_element_type=jnp.float32)
        hidden = (jax.nn.silu(expanded[:, :hidden_units]) * expanded[:, hidden_units:]).astype(jnp.bfloat16)
        return (updated + jnp.dot(hidden, trans_out, preferred_element_type=jnp.float32)).astype(jnp.bfloat16)
    return lax.map(finish_row, (pair, triangle, out_gate))
```

```python
import jax
import jax.numpy as jnp
from jax import lax
from jax.sharding import PartitionSpec as P


def layer_norm(values):
    centered = values - jnp.mean(values, axis=-1, keepdims=True)
    variance = jnp.mean(centered * centered, axis=-1, keepdims=True)
    return centered * lax.rsqrt(variance + 1e-05)


def per_device(pair, chain_lengths, in_weight, out_weight, trans_in, trans_out):
    tile_rows, tile_cols, width = pair.shape
    hidden_units = trans_out.shape[0]
    row_count = lax.axis_size("row")
    col_count = lax.axis_size("col")
    outer = row_count // 2
    tokens = tile_rows * row_count
    valid_count = tokens - chain_lengths[chain_lengths.shape[0] - 1]
    row_id = lax.axis_index("row")
    col_id = lax.axis_index("col")
    line_id = row_id // 2

    def along_line(value, step, targets):
        perm = [(2 * (t - step) + b, 2 * t + b) for t in targets for b in range(2)]
        return lax.ppermute(value, "row", perm)

    row_pos = row_id * tile_rows + jnp.arange(tile_rows, dtype=jnp.int32)
    col_pos = col_id * tile_cols + jnp.arange(tile_cols, dtype=jnp.int32)
    pair_mask = ((row_pos < valid_count)[:, None] & (col_pos < valid_count)[None, :]).astype(
        jnp.float32
    )[:, :, None]
    normed = layer_norm(pair.astype(jnp.float32)).astype(jnp.bfloat16).reshape(-1, width)

    def gated(offset):
        block = jnp.dot(
            normed,
            in_weight[:, offset * width : (offset + 2) * width],
            preferred_element_type=jnp.float32,
        ).reshape(tile_rows, tile_cols, 2 * width)
        value = jax.nn.sigmoid(block[..., :width]) * block[..., width:] * pair_mask
        return value.astype(jnp.bfloat16)

    right_ops = gated(2)
    from_left, from_right = {0: right_ops}, {0: right_ops}
    for step in range(1, outer):
        from_left[step] = along_line(from_left[step - 1], 1, range(step, outer))
        from_right[step] = along_line(from_right[step - 1], -1, range(0, outer - step))
    left_ops = gated(0)
    left_other = lax.ppermute(left_ops, "row", [(i, i ^ 1) for i in range(row_count)])
    lefts = jnp.concatenate([left_ops, left_other], axis=0)

    partials = []
    for source in range(outer):
        block = right_ops
        for step in range(1, outer):
            if source + step < outer:
                block = jnp.where(line_id == source + step, from_left[step], block)
            if source - step >= 0:
                block = jnp.where(line_id == source - step, from_right[step], block)
        partials.append(
            jnp.einsum("ikc,jkc->ijc", lefts, block, preferred_element_type=jnp.float32)
        )
    partial = jnp.stack(partials)
    share = outer // col_count
    mine = lax.dynamic_slice_in_dim(partial, col_id * share, share, 0)
    for hop in range(1, col_count):
        target = (col_id + hop) % col_count
        passed = lax.dynamic_slice_in_dim(partial, target * share, share, 0)
        mine = mine + lax.ppermute(
            passed, "col", [(c, (c + hop) % col_count) for c in range(col_count)]
        )
    tri_normed = layer_norm(mine).astype(jnp.bfloat16)
    own_part = tri_normed[:, :tile_rows]
    other_part = lax.ppermute(
        tri_normed[:, tile_rows:], "row", [(i, i ^ 1) for i in range(row_count)]
    )
    even = row_id % 2 == 0
    both = jnp.stack(
        [jnp.where(even, own_part, other_part), jnp.where(even, other_part, own_part)], axis=1
    )
    tri_normed = both.transpose(2, 0, 1, 3, 4).reshape(-1, width)

    out_gate = jax.nn.sigmoid(
        jnp.dot(normed, in_weight[:, 4 * width :], preferred_element_type=jnp.float32)
    )
    update = jnp.dot(tri_normed, out_weight, preferred_element_type=jnp.float32)
    updated = pair.astype(jnp.float32).reshape(-1, width) + out_gate * update
    trans_normed = layer_norm(updated).astype(jnp.bfloat16)
    expanded = jnp.dot(trans_normed, trans_in, preferred_element_type=jnp.float32)
    hidden = (jax.nn.silu(expanded[:, :hidden_units]) * expanded[:, hidden_units:]).astype(
        jnp.bfloat16
    )
    result = updated + jnp.dot(hidden, trans_out, preferred_element_type=jnp.float32)
    return result.reshape(tile_rows, tile_cols, width).astype(jnp.bfloat16)


def solution(mesh):
    placed = (P(("crops", "row"), "col", None), P("crops"), P(), P(), P(), P())
    return jax.shard_map(
        per_device,
        mesh=mesh,
        in_specs=placed,
        out_specs=P(("crops", "row"), "col", None),
        check_vma=False,
    )
```

```python
import jax
import jax.numpy as jnp
from jax import lax
from jax.experimental import pallas as pl
from jax.experimental.pallas import tpu as pltpu
from jax.sharding import PartitionSpec as P

VMEM = pltpu.VMEM
BF16, F32 = jnp.bfloat16, jnp.float32


def norm_rows(values):
    centered = values - jnp.mean(values, axis=-1, keepdims=True)
    variance = jnp.mean(centered * centered, axis=-1, keepdims=True)
    return centered * lax.rsqrt(variance + 1e-05)


def project_kernel(where_ref, pair_ref, weight_ref, own_ref, other_ref):
    valid, row0, col0 = where_ref[0], where_ref[1], where_ref[2]
    _, half, cols, width = pair_ref.shape
    token = col0 + lax.broadcasted_iota(jnp.int32, (cols, width), 0)
    low = lax.broadcasted_iota(jnp.int32, (cols, width), 1) < width // 2

    def step(r, carry):
        rows = [pair_ref[h, r].astype(F32) for h in range(2)]
        normed = norm_rows(jnp.concatenate(rows, axis=0)).astype(BF16)
        both = jnp.dot(normed, weight_ref[...], preferred_element_type=F32)
        out = jax.nn.sigmoid(both[:, :width]) * both[:, width:]
        halves = []
        for h in range(2):
            limit = jnp.where(row0 + h * half + r < valid, valid, 0)
            halves.append(jnp.where(token < limit, out[h * cols : (h + 1) * cols], 0.0))
        first, second = halves
        own_ref[r] = jnp.where(low, first, pltpu.roll(second, width // 2, 1)).astype(BF16)
        other_ref[r] = jnp.where(low, pltpu.roll(first, width // 2, 1), second).astype(BF16)
        return carry

    lax.fori_loop(0, half, step, 0)


def project(where, pair, weight):
    _, half, cols, width = pair.shape
    piece = jax.ShapeDtypeStruct((half, cols, width), BF16)
    return pl.pallas_call(
        project_kernel,
        out_shape=(piece, piece),
        in_specs=[pl.BlockSpec(memory_space=pltpu.SMEM)] + [pl.BlockSpec(memory_space=VMEM)] * 2,
        out_specs=[pl.BlockSpec(memory_space=VMEM)] * 2,
        compiler_params=pltpu.CompilerParams(vmem_limit_bytes=48 << 20),
        name="project",
    )(where, pair, weight)


def major_kernel(start_ref, first_ref, second_ref, out_ref, work_ref):
    half, cols, width = first_ref.shape
    chans = width // 2
    pitch = work_ref.shape[1] // chans
    for ref, start in ((first_ref, start_ref[0]), (second_ref, start_ref[1])):

        def step(r, carry, ref=ref, start=start):
            turned = ref[r].astype(F32).T
            for h in range(2):
                rows = turned[h * chans : (h + 1) * chans]
                at = pl.ds(start + h * half + r, chans, stride=pitch)
                work_ref[0, at, :] = rows[:, :width]
                work_ref[1, at, : cols - width] = rows[:, width:]
            return carry

        lax.fori_loop(0, half, step, 0)

    def pack(c, carry):
        rows = pl.ds(c * pitch, out_ref.shape[1])
        out_ref[c, :, :width] = work_ref[0, rows, :].astype(BF16)
        out_ref[c, :, width:] = work_ref[1, rows, : cols - width].astype(BF16)
        return carry

    lax.fori_loop(0, chans, pack, 0, unroll=4)


def major(starts, first, second):
    half, cols, width = first.shape
    pitch = (4 * half + 7) // 8 * 8
    return pl.pallas_call(
        major_kernel,
        out_shape=jax.ShapeDtypeStruct((width // 2, 4 * half, cols), BF16),
        in_specs=[pl.BlockSpec(memory_space=pltpu.SMEM)] + [pl.BlockSpec(memory_space=VMEM)] * 2,
        out_specs=pl.BlockSpec(memory_space=VMEM),
        scratch_shapes=[VMEM((2, width // 2 * pitch, width), F32)],
        compiler_params=pltpu.CompilerParams(vmem_limit_bytes=48 << 20),
        name="major",
    )(starts, first, second)


def triangle_kernel(left_ref, right_ref, out_ref, work_ref):
    chans, rows, _ = left_ref.shape
    _, half, cols, width = out_ref.shape

    def product(c, carry):
        value = lax.dot_general(
            left_ref[c], right_ref[c], (((1,), (1,)), ((), ())), preferred_element_type=F32
        )
        work_ref[pl.ds(c, rows, stride=chans), :cols] = value
        return carry

    lax.fori_loop(0, chans, product, 0, unroll=4)
    for o in range(2):

        def turn(r, carry, o=o):
            parts = []
            for h in range(2):
                at = pl.multiple_of((o * 2 * half + h * half + r) * chans, chans)
                parts.append(work_ref[pl.ds(at, chans), :])
            out_ref[o, r] = jnp.concatenate(parts, axis=0).T[:cols]
            return carry

        lax.fori_loop(0, half, turn, 0)


def triangle(left, right):
    chans, rows, _ = left.shape
    return pl.pallas_call(
        triangle_kernel,
        out_shape=jax.ShapeDtypeStruct((2, rows // 4, right.shape[1], 2 * chans), F32),
        in_specs=[pl.BlockSpec(memory_space=VMEM)] * 2,
        out_specs=pl.BlockSpec(memory_space=VMEM),
        scratch_shapes=[VMEM((rows * chans, 128), F32)],
        compiler_params=pltpu.CompilerParams(vmem_limit_bytes=48 << 20),
        name="triangle",
    )(left, right)


def finish_kernel(order_ref, pair_ref, own_ref, other_ref, gate_ref, out_w_ref, in_ref, back_ref, out_ref):
    _, half, cols, width = pair_ref.shape
    blocks = own_ref.shape[0]
    hidden_units = back_ref.shape[0]
    low = lax.broadcasted_iota(jnp.int32, own_ref.shape[2:], 1) < width // 2
    flip = order_ref[0]

    def step(r, carry):
        tri = [[], []]
        for b in range(blocks):
            at = jnp.where(flip == 1, blocks - 1 - b, b)
            own, other = own_ref[at, r].astype(F32), other_ref[at, r].astype(F32)
            tri[0].append(jnp.where(low, own, pltpu.roll(other, width // 2, 1)))
            tri[1].append(jnp.where(low, pltpu.roll(own, width // 2, 1), other))
        tri_normed = norm_rows(jnp.concatenate(tri[0] + tri[1], axis=0)).astype(BF16)
        pair = jnp.concatenate([pair_ref[h, r].astype(F32) for h in range(2)], axis=0)
        normed = norm_rows(pair).astype(BF16)
        out_gate = jax.nn.sigmoid(jnp.dot(normed, gate_ref[...], preferred_element_type=F32))
        update = jnp.dot(tri_normed, out_w_ref[...], preferred_element_type=F32)
        updated = pair + out_gate * update
        trans_normed = norm_rows(updated).astype(BF16)
        expanded = jnp.dot(trans_normed, in_ref[...], preferred_element_type=F32)
        swish, linear = expanded[:, :hidden_units], expanded[:, hidden_units:]
        hidden = (swish * jax.nn.sigmoid(swish) * linear).astype(BF16)
        result = updated + jnp.dot(hidden, back_ref[...], preferred_element_type=F32)
        for h in range(2):
            out_ref[h, r] = result[h * cols : (h + 1) * cols].astype(BF16)
        return carry

    lax.fori_loop(0, half, step, 0)


def finish(order, pair, own, other, gate_w, out_w, trans_in, trans_out):
    return pl.pallas_call(
        finish_kernel,
        out_shape=jax.ShapeDtypeStruct(pair.shape, BF16),
        in_specs=[pl.BlockSpec(memory_space=pltpu.SMEM)] + [pl.BlockSpec(memory_space=VMEM)] * 7,
        out_specs=pl.BlockSpec(memory_space=VMEM),
        compiler_params=pltpu.CompilerParams(vmem_limit_bytes=48 << 20),
        name="finish",
    )(order, pair, own, other, gate_w, out_w, trans_in, trans_out)


def layer_norm(values):
    centered = values - jnp.mean(values, axis=-1, keepdims=True)
    variance = jnp.mean(centered * centered, axis=-1, keepdims=True)
    return centered * lax.rsqrt(variance + 1e-05)


def any_mesh(pair, chain_lengths, in_weight, out_weight, trans_in, trans_out):
    tile_rows, tile_cols, width = pair.shape
    hidden_units = trans_out.shape[0]
    row_count = lax.axis_size("row")
    col_count = lax.axis_size("col")
    outer = row_count // 2
    tokens = tile_rows * row_count
    valid_count = tokens - chain_lengths[chain_lengths.shape[0] - 1]
    row_id = lax.axis_index("row")
    col_id = lax.axis_index("col")
    line_id = row_id // 2

    def along_line(value, step, targets):
        perm = [(2 * (t - step) + b, 2 * t + b) for t in targets for b in range(2)]
        return lax.ppermute(value, "row", perm)

    row_pos = row_id * tile_rows + jnp.arange(tile_rows, dtype=jnp.int32)
    col_pos = col_id * tile_cols + jnp.arange(tile_cols, dtype=jnp.int32)
    pair_mask = ((row_pos < valid_count)[:, None] & (col_pos < valid_count)[None, :]).astype(
        jnp.float32
    )[:, :, None]
    normed = layer_norm(pair.astype(jnp.float32)).astype(jnp.bfloat16).reshape(-1, width)

    def gated(offset):
        block = jnp.dot(
            normed,
            in_weight[:, offset * width : (offset + 2) * width],
            preferred_element_type=jnp.float32,
        ).reshape(tile_rows, tile_cols, 2 * width)
        value = jax.nn.sigmoid(block[..., :width]) * block[..., width:] * pair_mask
        return value.astype(jnp.bfloat16)

    right_ops = gated(2)
    from_left, from_right = {0: right_ops}, {0: right_ops}
    for step in range(1, outer):
        from_left[step] = along_line(from_left[step - 1], 1, range(step, outer))
        from_right[step] = along_line(from_right[step - 1], -1, range(0, outer - step))
    left_ops = gated(0)
    left_other = lax.ppermute(left_ops, "row", [(i, i ^ 1) for i in range(row_count)])
    lefts = jnp.concatenate([left_ops, left_other], axis=0)

    partials = []
    for source in range(outer):
        block = right_ops
        for step in range(1, outer):
            if source + step < outer:
                block = jnp.where(line_id == source + step, from_left[step], block)
            if source - step >= 0:
                block = jnp.where(line_id == source - step, from_right[step], block)
        partials.append(
            jnp.einsum("ikc,jkc->ijc", lefts, block, preferred_element_type=jnp.float32)
        )
    partial = jnp.stack(partials)
    share = outer // col_count
    mine = lax.dynamic_slice_in_dim(partial, col_id * share, share, 0)
    for hop in range(1, col_count):
        target = (col_id + hop) % col_count
        passed = lax.dynamic_slice_in_dim(partial, target * share, share, 0)
        mine = mine + lax.ppermute(
            passed, "col", [(c, (c + hop) % col_count) for c in range(col_count)]
        )
    tri_normed = layer_norm(mine).astype(jnp.bfloat16)
    own_part = tri_normed[:, :tile_rows]
    other_part = lax.ppermute(
        tri_normed[:, tile_rows:], "row", [(i, i ^ 1) for i in range(row_count)]
    )
    even = row_id % 2 == 0
    both = jnp.stack(
        [jnp.where(even, own_part, other_part), jnp.where(even, other_part, own_part)], axis=1
    )
    tri_normed = both.transpose(2, 0, 1, 3, 4).reshape(-1, width)

    out_gate = jax.nn.sigmoid(
        jnp.dot(normed, in_weight[:, 4 * width :], preferred_element_type=jnp.float32)
    )
    update = jnp.dot(tri_normed, out_weight, preferred_element_type=jnp.float32)
    updated = pair.astype(jnp.float32).reshape(-1, width) + out_gate * update
    trans_normed = layer_norm(updated).astype(jnp.bfloat16)
    expanded = jnp.dot(trans_normed, trans_in, preferred_element_type=jnp.float32)
    hidden = (jax.nn.silu(expanded[:, :hidden_units]) * expanded[:, hidden_units:]).astype(
        jnp.bfloat16
    )
    result = updated + jnp.dot(hidden, trans_out, preferred_element_type=jnp.float32)
    return result.reshape(tile_rows, tile_cols, width).astype(jnp.bfloat16)


def per_device(pair, chain_lengths, in_weight, out_weight, trans_in, trans_out):
    if (lax.axis_size("row"), lax.axis_size("col")) != (8, 2):
        return any_mesh(pair, chain_lengths, in_weight, out_weight, trans_in, trans_out)
    return two_by_four(pair, chain_lengths, in_weight, out_weight, trans_in, trans_out)


def two_by_four(pair, chain_lengths, in_weight, out_weight, trans_in, trans_out):
    tile_rows, tile_cols, width = pair.shape
    half = tile_rows // 2
    tokens = tile_rows * lax.axis_size("row")
    valid_count = tokens - chain_lengths[chain_lengths.shape[0] - 1]
    row_id, core = lax.axis_index("row"), lax.axis_index("col")
    place, side = row_id // 2, row_id % 2
    keeper = place // 2

    def among(value, moves):
        return lax.ppermute(value, "row", [(2 * s + b, 2 * t + b) for s, t in moves for b in range(2)])

    def across(value):
        return lax.ppermute(value, "row", [(i, i ^ 1) for i in range(8)])

    def to_core(value, places, keep):
        perm = []
        for z in places:
            target = z // 2 if keep else 1 - z // 2
            perm += [(4 * z + 2 * b + 1 - target, 4 * z + 2 * b + target) for b in range(2)]
        return lax.ppermute(value, ("row", "col"), perm)

    def by_side(block, axis):
        return jnp.where(side == 0, block, jnp.roll(block, width // 2, axis))

    def gate_pair(first):
        return jnp.concatenate(
            [by_side(in_weight[:, (first + i) * width : (first + i + 1) * width], 1) for i in range(2)],
            axis=1,
        )

    where = jnp.stack([valid_count, row_id * tile_rows, core * tile_cols]).astype(jnp.int32)
    folded = pair.reshape(2, half, tile_cols, width)
    mates, cross = [(0, 1), (1, 0), (2, 3), (3, 2)], [(1, 2), (2, 1)]
    inward, outward = [(0, 1), (3, 2)], [(1, 0), (2, 3)]

    right_own, right_far = project(where, folded, gate_pair(2))
    right_beside = across(right_far)
    mate = [among(v, mates) for v in (right_own, right_beside)]
    near = [among(v, cross) for v in (right_own, right_beside)]
    far = [among(v, cross) for v in mate]
    left_own, left_far = project(where, folded, gate_pair(0))
    left_beside = across(left_far)
    guest = [among(v, inward) for v in (left_own, left_beside)]

    plain = jnp.array([0, tile_rows], jnp.int32)
    sided = jnp.stack([side * tile_rows, (1 - side) * tile_rows]).astype(jnp.int32)
    left = major(plain, left_own, left_beside)
    left_guest = major(plain, *guest)
    rights = {
        "own": major(sided, right_own, right_beside),
        "mate": major(sided, *mate),
        "near": major(sided, *near),
        "far": major(sided, *far),
    }
    home = [triangle(left, rights[k]) for k in ("own", "mate")]
    away = [triangle(left, rights[k]) for k in ("near", "far")]
    lent = [triangle(left_guest, rights[k]) for k in ("near", "far")]

    home_rest = [to_core(v, range(4), True) for v in home]
    away_rest = [to_core(v, (1, 2), False) for v in away]
    lent_rest = [to_core(v, (1, 2), False) for v in lent]
    given = [among((a + b).astype(BF16), outward) for a, b in zip(lent, lent_rest)]
    is_keeper = core == keeper
    inner = (place == 1) | (place == 2)
    blocks = []
    for i in range(2):
        total = jnp.where(is_keeper, home[i] + home_rest[i], away[i] + away_rest[i]).astype(BF16)
        blocks.append(jnp.where(is_keeper | inner, total, given[i]))
    own = jnp.stack([b[0] for b in blocks])
    other = jnp.stack([across(b[1]) for b in blocks])
    flip = jnp.where(is_keeper, place % 2, place // 2).astype(jnp.int32).reshape(1)
    result = finish(
        flip,
        folded,
        own,
        other,
        in_weight[:, 4 * width :],
        by_side(out_weight, 0),
        trans_in,
        trans_out,
    )
    return result.reshape(tile_rows, tile_cols, width)


def solution(mesh):
    placed = (P(("crops", "row"), "col", None), P("crops"), P(), P(), P(), P())
    return jax.shard_map(
        per_device,
        mesh=mesh,
        in_specs=placed,
        out_specs=P(("crops", "row"), "col", None),
        check_vma=False,
    )
```

```python
import jax
import jax.numpy as jnp
from jax import lax
from jax.experimental import pallas as pl
from jax.experimental.pallas import tpu as pltpu
from jax.sharding import PartitionSpec as P

VMEM = pltpu.VMEM
BF16, F32 = jnp.bfloat16, jnp.float32
CHUNK = 16


def whole(count):
    return [pl.BlockSpec(memory_space=VMEM)] * count


def params():
    return pltpu.CompilerParams(vmem_limit_bytes=48 << 20)


def cost(flops, moved, transcendentals=0):
    return pl.CostEstimate(flops=flops, bytes_accessed=moved, transcendentals=transcendentals)


def sigmoid(values):
    return 0.5 * jnp.tanh(0.5 * values) + 0.5


def norm_chans(values):
    centered = values - jnp.mean(values, axis=0, keepdims=True)
    variance = jnp.mean(centered * centered, axis=0, keepdims=True)
    return centered * lax.rsqrt(variance + 1e-05)


def padded(count, unit):
    return -(-count // unit) * unit


def project_kernel(where_ref, pair_ref, weight_ref, own_ref, far_ref):
    valid, row0, col0 = where_ref[0], where_ref[1], where_ref[2]
    _, half, cols, width = pair_ref.shape
    chans = width // 2
    tail = cols - width
    lane = lax.broadcasted_iota(jnp.int32, (1, 3 * width), 1)
    in_tail = lane >= 2 * width
    ends = jnp.where(in_tail, 2 * width + chans, width)
    is_first = jnp.where(lane < ends, 1, 0)
    token = jnp.where(in_tail, lane % chans + width, lane % width) + col0
    gap = jnp.zeros((chans - tail, width), F32)

    def step(r, carry):
        first, second = (pair_ref[h, r].astype(F32) for h in range(2))
        tokens = jnp.concatenate(
            [first[:width], second[:width], first[width:], gap, second[width:], gap], axis=0
        )
        normed = norm_chans(tokens.T).astype(BF16)
        both = jnp.dot(weight_ref[...], normed, preferred_element_type=F32)
        limits = [jnp.where(row0 + h * half + r < valid, valid, 0) for h in range(2)]
        keep = jnp.where(token < limits[1] + is_first * (limits[0] - limits[1]), 1.0, 0.0)
        out = (sigmoid(both[:width]) * both[width:] * keep).astype(BF16)
        own_ref[r] = out[:chans]
        far_ref[r] = out[chans:]
        return carry

    lax.fori_loop(0, half, step, 0, unroll=4)


def project(where, pair, weight):
    _, half, cols, width = pair.shape
    piece = jax.ShapeDtypeStruct((half, width // 2, 3 * width), BF16)
    return pl.pallas_call(
        project_kernel,
        out_shape=(piece, piece),
        in_specs=[pl.BlockSpec(memory_space=pltpu.SMEM)] + whole(2),
        out_specs=whole(2),
        compiler_params=params(),
        cost_estimate=cost(4 * pair.size * width, 4 * pair.size, pair.size),
        name="project",
    )(where, pair, weight)


def channel_major(pieces, clear):
    width = pieces[0].shape[2] // 3
    main, rest = [], []
    for piece in pieces:
        tail = piece[:, :, 2 * width :]
        turned = jnp.concatenate([tail[:, :, width // 2 :], tail[:, :, : width // 2]], axis=2)
        main += [piece[:, :, :width], piece[:, :, width : 2 * width]]
        rest += [tail, turned]
    rest = jnp.concatenate(rest, axis=0)
    if clear:
        low = lax.broadcasted_iota(jnp.int32, rest.shape, 2) < width // 2
        rest = jnp.where(low, rest, jnp.zeros_like(rest))
    main = jnp.swapaxes(jnp.concatenate(main, axis=0), 0, 1)
    return main, jnp.swapaxes(rest, 0, 1)


def left_kernel(own_ref, beside_ref, out_ref):
    width = own_ref.shape[2] // 3
    main, rest = channel_major([own_ref[...], beside_ref[...]], True)
    rows = main.shape[1]
    out_ref[:, :rows, :width] = main
    out_ref[:, :rows, width:] = rest
    out_ref[:, rows:] = jnp.zeros_like(out_ref[:, rows:])


def left_major(own, beside):
    half, chans, lanes = own.shape
    piece = pl.BlockSpec((half, CHUNK, lanes), lambda c: (0, c, 0))
    return pl.pallas_call(
        left_kernel,
        grid=(chans // CHUNK,),
        out_shape=jax.ShapeDtypeStruct((chans, padded(4 * half, 16), lanes // 3 * 2), BF16),
        in_specs=[piece, piece],
        out_specs=pl.BlockSpec((CHUNK, padded(4 * half, 16), lanes // 3 * 2), lambda c: (c, 0, 0)),
        compiler_params=params(),
        cost_estimate=cost(0, 8 * own.size),
        name="left_major",
    )(own, beside)


def triangle_kernel(side_ref, *refs):
    lefts = len(refs) // 2 - 1
    own, beside = refs[lefts][...], refs[lefts + 1][...]
    outs, right_ref = refs[lefts + 2 : -1], refs[-1]
    width = own.shape[2] // 3
    even = side_ref[0] == 0
    main, rest = channel_major(
        [jnp.where(even, own, beside), jnp.where(even, beside, own)], False
    )
    rows = main.shape[1]

    @pl.when(pl.program_id(0) == 0)
    def _():
        right_ref[...] = jnp.zeros_like(right_ref)

    right_ref[:, :rows, :width] = main
    right_ref[:, :rows, width:] = rest
    for c in range(CHUNK):
        for left_ref, out_ref in zip(refs[:lefts], outs):
            out_ref[c] = lax.dot_general(
                left_ref[c], right_ref[c], (((1,), (1,)), ((), ())), preferred_element_type=F32
            )


def triangle(side, lefts, own, beside):
    half, chans, lanes = own.shape
    rows, cols = padded(4 * half, 16), padded(4 * half, 128)
    piece = pl.BlockSpec((half, CHUNK, lanes), lambda c: (0, c, 0))
    left = pl.BlockSpec((CHUNK, rows, lanes // 3 * 2), lambda c: (c, 0, 0))
    out = pl.BlockSpec((CHUNK, rows, cols), lambda c: (c, 0, 0))
    return pl.pallas_call(
        triangle_kernel,
        grid=(chans // CHUNK,),
        out_shape=[jax.ShapeDtypeStruct((chans, rows, cols), F32) for _ in lefts],
        in_specs=[pl.BlockSpec(memory_space=pltpu.SMEM)] + [left] * len(lefts) + [piece, piece],
        out_specs=[out] * len(lefts),
        scratch_shapes=[VMEM((CHUNK, cols, lanes // 3 * 2), BF16)],
        compiler_params=params(),
        cost_estimate=cost(2 * len(lefts) * chans * rows * cols * lanes // 3 * 2, (4 + 8 * len(lefts)) * own.size),
        name="triangle",
    )(side, *lefts, own, beside)


def fold_kernel(role_ref, *refs):
    own_ref, beside_ref, work_ref = refs[-3:]
    half, cols, width = own_ref.shape
    chans = width // 2
    c = pl.program_id(0)
    options = len(refs[:-3]) // 2
    for option in range(options):
        mine_ref, rest_ref = refs[2 * option : 2 * option + 2]

        def gather():
            total = (mine_ref[...] + rest_ref[...]).astype(BF16)
            at = pl.ds(pl.multiple_of(c * CHUNK, CHUNK), CHUNK)
            work_ref[:, at, :] = jnp.swapaxes(total, 0, 1)

        if options == 1:
            gather()
        else:
            pl.when(role_ref[0] == option)(gather)

    @pl.when(c == pl.num_programs(0) - 1)
    def _():
        for o, out_ref in enumerate((own_ref, beside_ref)):

            def turn(r, carry, o=o, out_ref=out_ref):
                at = o * 2 * half + r
                stacked = jnp.concatenate([work_ref[at], work_ref[at + half]], axis=0)
                out_ref[r] = stacked.T[:cols]
                return carry

            lax.fori_loop(0, half, turn, 0, unroll=True)


def fold(half, role, *parts):
    chans, rows, cols = parts[0].shape
    out = jax.ShapeDtypeStruct((half, padded(4 * half, 16), 2 * chans), BF16)

    def block(option):
        if len(parts) == 2:
            return pl.BlockSpec((CHUNK, rows, cols), lambda c, role_ref: (c, 0, 0))
        return pl.BlockSpec(
            (CHUNK, rows, cols), lambda c, role_ref: (jnp.where(role_ref[0] == option, c, 0), 0, 0)
        )

    return pl.pallas_call(
        fold_kernel,
        grid_spec=pltpu.PrefetchScalarGridSpec(
            num_scalar_prefetch=1,
            grid=(chans // CHUNK,),
            in_specs=[block(i // 2) for i in range(len(parts))],
            out_specs=[pl.BlockSpec(out.shape, lambda c, role_ref: (0, 0, 0))] * 2,
            scratch_shapes=[VMEM((rows, chans, cols), BF16)],
        ),
        out_shape=(out, out),
        compiler_params=params(),
        cost_estimate=cost(0, 10 * parts[0].size),
        name="fold",
    )(role, *parts)


def finish_kernel(order_ref, pair_ref, *refs):
    owns, others = refs[0:2], refs[2:4]
    gate_ref, out_w_ref, in_ref, back_ref, out_ref = refs[4:]
    _, half, cols, width = pair_ref.shape
    hidden_units = back_ref.shape[1]
    flip = order_ref[0] == 1

    block = cols // 2
    chans = width // 2

    def step(r, carry):
        rows = [[], []]
        for own_ref, other_ref in zip(owns, others):
            own, other = (ref[r].astype(F32).T[:, :block] for ref in (own_ref, other_ref))
            for h in range(2):
                at = slice(h * chans, (h + 1) * chans)
                rows[h].append(jnp.concatenate([own[at], other[at]], axis=0))
        lanes = []
        for first, second in rows:
            lanes += [jnp.where(flip, second, first), jnp.where(flip, first, second)]
        tri_normed = norm_chans(jnp.concatenate(lanes, axis=1)).astype(BF16)
        pair = jnp.concatenate([pair_ref[h, r].astype(F32) for h in range(2)], axis=0).T
        normed = norm_chans(pair).astype(BF16)
        out_gate = sigmoid(jnp.dot(gate_ref[...], normed, preferred_element_type=F32))
        update = jnp.dot(out_w_ref[...], tri_normed, preferred_element_type=F32)
        updated = pair + out_gate * update
        trans_normed = norm_chans(updated).astype(BF16)
        expanded = jnp.dot(in_ref[...], trans_normed, preferred_element_type=F32)
        swish, linear = expanded[:hidden_units], expanded[hidden_units:]
        hidden = (swish * sigmoid(swish) * linear).astype(BF16)
        result = updated + jnp.dot(back_ref[...], hidden, preferred_element_type=F32)
        result = result.T
        for h in range(2):
            out_ref[h, r] = result[h * cols : (h + 1) * cols].astype(BF16)
        return carry

    lax.fori_loop(0, half, step, 0, unroll=2)


def finish(order, pair, owns, others, gate_w, out_w, trans_in, trans_out):
    return pl.pallas_call(
        finish_kernel,
        out_shape=jax.ShapeDtypeStruct(pair.shape, BF16),
        in_specs=[pl.BlockSpec(memory_space=pltpu.SMEM)] + whole(9),
        out_specs=pl.BlockSpec(memory_space=VMEM),
        compiler_params=params(),
        cost_estimate=cost(28 * pair.size * pair.shape[-1], 6 * pair.size, 6 * pair.size),
        name="finish",
    )(order, pair, *owns, *others, gate_w, out_w, trans_in, trans_out)


def layer_norm(values):
    centered = values - jnp.mean(values, axis=-1, keepdims=True)
    variance = jnp.mean(centered * centered, axis=-1, keepdims=True)
    return centered * lax.rsqrt(variance + 1e-05)


def any_mesh(pair, chain_lengths, in_weight, out_weight, trans_in, trans_out):
    tile_rows, tile_cols, width = pair.shape
    hidden_units = trans_out.shape[0]
    row_count = lax.axis_size("row")
    col_count = lax.axis_size("col")
    outer = row_count // 2
    tokens = tile_rows * row_count
    valid_count = tokens - chain_lengths[chain_lengths.shape[0] - 1]
    row_id = lax.axis_index("row")
    col_id = lax.axis_index("col")
    line_id = row_id // 2

    def along_line(value, step, targets):
        perm = [(2 * (t - step) + b, 2 * t + b) for t in targets for b in range(2)]
        return lax.ppermute(value, "row", perm)

    row_pos = row_id * tile_rows + jnp.arange(tile_rows, dtype=jnp.int32)
    col_pos = col_id * tile_cols + jnp.arange(tile_cols, dtype=jnp.int32)
    pair_mask = ((row_pos < valid_count)[:, None] & (col_pos < valid_count)[None, :]).astype(
        jnp.float32
    )[:, :, None]
    normed = layer_norm(pair.astype(jnp.float32)).astype(jnp.bfloat16).reshape(-1, width)

    def gated(offset):
        block = jnp.dot(
            normed,
            in_weight[:, offset * width : (offset + 2) * width],
            preferred_element_type=jnp.float32,
        ).reshape(tile_rows, tile_cols, 2 * width)
        value = jax.nn.sigmoid(block[..., :width]) * block[..., width:] * pair_mask
        return value.astype(jnp.bfloat16)

    right_ops = gated(2)
    from_left, from_right = {0: right_ops}, {0: right_ops}
    for step in range(1, outer):
        from_left[step] = along_line(from_left[step - 1], 1, range(step, outer))
        from_right[step] = along_line(from_right[step - 1], -1, range(0, outer - step))
    left_ops = gated(0)
    left_other = lax.ppermute(left_ops, "row", [(i, i ^ 1) for i in range(row_count)])
    lefts = jnp.concatenate([left_ops, left_other], axis=0)

    partials = []
    for source in range(outer):
        block = right_ops
        for step in range(1, outer):
            if source + step < outer:
                block = jnp.where(line_id == source + step, from_left[step], block)
            if source - step >= 0:
                block = jnp.where(line_id == source - step, from_right[step], block)
        partials.append(
            jnp.einsum("ikc,jkc->ijc", lefts, block, preferred_element_type=jnp.float32)
        )
    partial = jnp.stack(partials)
    share = outer // col_count
    mine = lax.dynamic_slice_in_dim(partial, col_id * share, share, 0)
    for hop in range(1, col_count):
        target = (col_id + hop) % col_count
        passed = lax.dynamic_slice_in_dim(partial, target * share, share, 0)
        mine = mine + lax.ppermute(
            passed, "col", [(c, (c + hop) % col_count) for c in range(col_count)]
        )
    tri_normed = layer_norm(mine).astype(jnp.bfloat16)
    own_part = tri_normed[:, :tile_rows]
    other_part = lax.ppermute(
        tri_normed[:, tile_rows:], "row", [(i, i ^ 1) for i in range(row_count)]
    )
    even = row_id % 2 == 0
    both = jnp.stack(
        [jnp.where(even, own_part, other_part), jnp.where(even, other_part, own_part)], axis=1
    )
    tri_normed = both.transpose(2, 0, 1, 3, 4).reshape(-1, width)

    out_gate = jax.nn.sigmoid(
        jnp.dot(normed, in_weight[:, 4 * width :], preferred_element_type=jnp.float32)
    )
    update = jnp.dot(tri_normed, out_weight, preferred_element_type=jnp.float32)
    updated = pair.astype(jnp.float32).reshape(-1, width) + out_gate * update
    trans_normed = layer_norm(updated).astype(jnp.bfloat16)
    expanded = jnp.dot(trans_normed, trans_in, preferred_element_type=jnp.float32)
    hidden = (jax.nn.silu(expanded[:, :hidden_units]) * expanded[:, hidden_units:]).astype(
        jnp.bfloat16
    )
    result = updated + jnp.dot(hidden, trans_out, preferred_element_type=jnp.float32)
    return result.reshape(tile_rows, tile_cols, width).astype(jnp.bfloat16)


def per_device(pair, chain_lengths, in_weight, out_weight, trans_in, trans_out):
    if (lax.axis_size("row"), lax.axis_size("col")) != (8, 2):
        return any_mesh(pair, chain_lengths, in_weight, out_weight, trans_in, trans_out)
    return two_by_four(pair, chain_lengths, in_weight, out_weight, trans_in, trans_out)


def two_by_four(pair, chain_lengths, in_weight, out_weight, trans_in, trans_out):
    tile_rows, tile_cols, width = pair.shape
    half = tile_rows // 2
    tokens = tile_rows * lax.axis_size("row")
    valid_count = tokens - chain_lengths[chain_lengths.shape[0] - 1]
    row_id, core = lax.axis_index("row"), lax.axis_index("col")
    place, side = row_id // 2, row_id % 2
    keeper = place // 2

    def among(value, moves):
        return lax.ppermute(value, "row", [(2 * s + b, 2 * t + b) for s, t in moves for b in range(2)])

    def across(value):
        return lax.ppermute(value, "row", [(i, i ^ 1) for i in range(8)])

    def to_core(value, places, keep):
        perm = []
        for z in places:
            target = z // 2 if keep else 1 - z // 2
            perm += [(4 * z + 2 * b + 1 - target, 4 * z + 2 * b + target) for b in range(2)]
        return lax.ppermute(value, ("row", "col"), perm)

    def by_side(block, axis):
        return jnp.where(side == 0, block, jnp.roll(block, width // 2, axis))

    def gate_pair(first):
        parts = [
            by_side(in_weight[:, (first + i) * width : (first + i + 1) * width], 1) for i in range(2)
        ]
        return jnp.concatenate(parts, axis=1).T

    where = jnp.stack([valid_count, row_id * tile_rows, core * tile_cols]).astype(jnp.int32)
    sides = side.astype(jnp.int32).reshape(1)
    is_keeper = core == keeper
    role = jnp.where(is_keeper, 0, 1).astype(jnp.int32).reshape(1)
    folded = pair.reshape(2, half, tile_cols, width)
    mates, cross = [(0, 1), (1, 0), (2, 3), (3, 2)], [(1, 2), (2, 1)]
    inward, outward = [(0, 1), (3, 2)], [(1, 0), (2, 3)]

    right_own, right_far = project(where, folded, gate_pair(2))
    right_beside = across(right_far)
    mate = [among(v, mates) for v in (right_own, right_beside)]
    near = [among(v, cross) for v in (right_own, right_beside)]
    far = [among(v, cross) for v in mate]
    left_own, left_far = project(where, folded, gate_pair(0))
    left_beside = across(left_far)
    guest = [among(v, inward) for v in (left_own, left_beside)]

    left = left_major(left_own, left_beside)
    home = [triangle(sides, [left], right_own, right_beside)[0], triangle(sides, [left], *mate)[0]]
    left_guest = left_major(*guest)
    away, lent = zip(*(triangle(sides, [left, left_guest], *v) for v in (near, far)))

    home_rest = [to_core(v, range(4), True) for v in home]
    away_rest = [to_core(v, (1, 2), False) for v in away]
    lent_rest = [to_core(v, (1, 2), False) for v in lent]
    inner = (place == 1) | (place == 2)
    owns, others = [], []
    for i in range(2):
        given = [among(v, outward) for v in fold(half, role, lent[i], lent_rest[i])]
        kept = fold(half, role, home[i], home_rest[i], away[i], away_rest[i])
        own, beside = (jnp.where(is_keeper | inner, k, g) for k, g in zip(kept, given))
        owns.append(own)
        others.append(across(beside))
    flip = jnp.where(is_keeper, place % 2, place // 2).astype(jnp.int32).reshape(1)
    result = finish(
        flip,
        folded,
        owns,
        others,
        in_weight[:, 4 * width :].T,
        by_side(out_weight, 0).T,
        trans_in.T,
        trans_out.T,
    )
    return result.reshape(tile_rows, tile_cols, width)


def solution(mesh):
    placed = (P(("crops", "row"), "col", None), P("crops"), P(), P(), P(), P())
    return jax.shard_map(
        per_device,
        mesh=mesh,
        in_specs=placed,
        out_specs=P(("crops", "row"), "col", None),
        check_vma=False,
    )
```

```python
import jax
import jax.numpy as jnp
from jax import lax
from jax.experimental import pallas as pl
from jax.experimental.pallas import tpu as pltpu
from jax.sharding import PartitionSpec as P

VMEM = pltpu.VMEM
BF16, F32 = jnp.bfloat16, jnp.float32
CHUNK = 16


def whole(count):
    return [pl.BlockSpec(memory_space=VMEM)] * count


def params():
    return pltpu.CompilerParams(vmem_limit_bytes=48 << 20)


def cost(flops, moved, transcendentals=0):
    return pl.CostEstimate(flops=flops, bytes_accessed=moved, transcendentals=transcendentals)


def sigmoid(values):
    return 0.5 * jnp.tanh(0.5 * values) + 0.5


def norm_chans(values):
    centered = values - jnp.mean(values, axis=0, keepdims=True)
    variance = jnp.mean(centered * centered, axis=0, keepdims=True)
    return centered * lax.rsqrt(variance + 1e-05)


def padded(count, unit):
    return -(-count // unit) * unit


def project_kernel(where_ref, pair_ref, weight_ref, own_ref, far_ref):
    valid, row0, col0 = where_ref[0], where_ref[1], where_ref[2]
    _, half, cols, width = pair_ref.shape
    chans = width // 2
    tail = cols - width
    lane = lax.broadcasted_iota(jnp.int32, (1, 3 * width), 1)
    in_tail = lane >= 2 * width
    ends = jnp.where(in_tail, 2 * width + chans, width)
    is_first = jnp.where(lane < ends, 1, 0)
    token = jnp.where(in_tail, lane % chans + width, lane % width) + col0
    gap = jnp.zeros((chans - tail, width), F32)

    def step(r, carry):
        first, second = (pair_ref[h, r].astype(F32) for h in range(2))
        tokens = jnp.concatenate(
            [first[:width], second[:width], first[width:], gap, second[width:], gap], axis=0
        )
        normed = norm_chans(tokens.T).astype(BF16)
        both = jnp.dot(weight_ref[...], normed, preferred_element_type=F32)
        limits = [jnp.where(row0 + h * half + r < valid, valid, 0) for h in range(2)]
        keep = jnp.where(token < limits[1] + is_first * (limits[0] - limits[1]), 1.0, 0.0)
        out = (sigmoid(both[:width]) * both[width:] * keep).astype(BF16)
        own_ref[r] = out[:chans]
        far_ref[r] = out[chans:]
        return carry

    lax.fori_loop(0, half, step, 0, unroll=4)


def project(where, pair, weight):
    _, half, cols, width = pair.shape
    piece = jax.ShapeDtypeStruct((half, width // 2, 3 * width), BF16)
    return pl.pallas_call(
        project_kernel,
        out_shape=(piece, piece),
        in_specs=[pl.BlockSpec(memory_space=pltpu.SMEM)] + whole(2),
        out_specs=whole(2),
        compiler_params=params(),
        cost_estimate=cost(4 * pair.size * width, 4 * pair.size, pair.size),
        name="project",
    )(where, pair, weight)


def channel_major(pieces, clear):
    width = pieces[0].shape[2] // 3
    main, rest = [], []
    for piece in pieces:
        tail = piece[:, :, 2 * width :]
        turned = jnp.concatenate([tail[:, :, width // 2 :], tail[:, :, : width // 2]], axis=2)
        main += [piece[:, :, :width], piece[:, :, width : 2 * width]]
        rest += [tail, turned]
    rest = jnp.concatenate(rest, axis=0)
    if clear:
        low = lax.broadcasted_iota(jnp.int32, rest.shape, 2) < width // 2
        rest = jnp.where(low, rest, jnp.zeros_like(rest))
    main = jnp.swapaxes(jnp.concatenate(main, axis=0), 0, 1)
    return main, jnp.swapaxes(rest, 0, 1)


def left_kernel(own_ref, beside_ref, out_ref):
    width = own_ref.shape[2] // 3
    main, rest = channel_major([own_ref[...], beside_ref[...]], True)
    rows = main.shape[1]
    out_ref[:, :rows, :width] = main
    out_ref[:, :rows, width:] = rest
    out_ref[:, rows:] = jnp.zeros_like(out_ref[:, rows:])


def left_major(own, beside):
    half, chans, lanes = own.shape
    piece = pl.BlockSpec((half, CHUNK, lanes), lambda c: (0, c, 0))
    return pl.pallas_call(
        left_kernel,
        grid=(chans // CHUNK,),
        out_shape=jax.ShapeDtypeStruct((chans, padded(4 * half, 16), lanes // 3 * 2), BF16),
        in_specs=[piece, piece],
        out_specs=pl.BlockSpec((CHUNK, padded(4 * half, 16), lanes // 3 * 2), lambda c: (c, 0, 0)),
        compiler_params=params(),
        cost_estimate=cost(0, 8 * own.size),
        name="left_major",
    )(own, beside)


def triangle_kernel(side_ref, *refs):
    lefts = len(refs) // 2 - 1
    own, beside = refs[lefts][...], refs[lefts + 1][...]
    outs, right_ref = refs[lefts + 2 : -1], refs[-1]
    width = own.shape[2] // 3
    even = side_ref[0] == 0
    main, rest = channel_major(
        [jnp.where(even, own, beside), jnp.where(even, beside, own)], False
    )
    rows = main.shape[1]

    @pl.when(pl.program_id(0) == 0)
    def _():
        right_ref[...] = jnp.zeros_like(right_ref)

    right_ref[:, :rows, :width] = main
    right_ref[:, :rows, width:] = rest
    for c in range(CHUNK):
        for left_ref, out_ref in zip(refs[:lefts], outs):
            out_ref[c] = lax.dot_general(
                left_ref[c], right_ref[c], (((1,), (1,)), ((), ())), preferred_element_type=F32
            ).astype(BF16)


def triangle(side, lefts, own, beside):
    half, chans, lanes = own.shape
    rows, cols = padded(4 * half, 16), padded(4 * half, 128)
    piece = pl.BlockSpec((half, CHUNK, lanes), lambda c: (0, c, 0))
    left = pl.BlockSpec((CHUNK, rows, lanes // 3 * 2), lambda c: (c, 0, 0))
    out = pl.BlockSpec((CHUNK, rows, cols), lambda c: (c, 0, 0))
    return pl.pallas_call(
        triangle_kernel,
        grid=(chans // CHUNK,),
        out_shape=[jax.ShapeDtypeStruct((chans, rows, cols), BF16) for _ in lefts],
        in_specs=[pl.BlockSpec(memory_space=pltpu.SMEM)] + [left] * len(lefts) + [piece, piece],
        out_specs=[out] * len(lefts),
        scratch_shapes=[VMEM((CHUNK, cols, lanes // 3 * 2), BF16)],
        compiler_params=params(),
        cost_estimate=cost(2 * len(lefts) * chans * rows * cols * lanes // 3 * 2, (4 + 6 * len(lefts)) * own.size),
        name="triangle",
    )(side, *lefts, own, beside)


def fold_kernel(role_ref, *refs):
    own_ref, beside_ref, work_ref = refs[-3:]
    half, cols, width = own_ref.shape
    chans = width // 2
    c = pl.program_id(0)
    options = len(refs[:-3]) // 2
    for option in range(options):
        mine_ref, rest_ref = refs[2 * option : 2 * option + 2]

        def gather():
            total = (mine_ref[...].astype(F32) + rest_ref[...].astype(F32)).astype(BF16)
            at = pl.ds(pl.multiple_of(c * CHUNK, CHUNK), CHUNK)
            work_ref[:, at, :] = jnp.swapaxes(total, 0, 1)

        if options == 1:
            gather()
        else:
            pl.when(role_ref[0] == option)(gather)

    @pl.when(c == pl.num_programs(0) - 1)
    def _():
        for o, out_ref in enumerate((own_ref, beside_ref)):

            def turn(r, carry, o=o, out_ref=out_ref):
                at = o * 2 * half + r
                stacked = jnp.concatenate([work_ref[at], work_ref[at + half]], axis=0)
                out_ref[r] = stacked.T[:cols]
                return carry

            lax.fori_loop(0, half, turn, 0, unroll=True)


def fold(half, role, *parts):
    chans, rows, cols = parts[0].shape
    out = jax.ShapeDtypeStruct((half, padded(4 * half, 16), 2 * chans), BF16)

    def block(option):
        if len(parts) == 2:
            return pl.BlockSpec((CHUNK, rows, cols), lambda c, role_ref: (c, 0, 0))
        return pl.BlockSpec(
            (CHUNK, rows, cols), lambda c, role_ref: (jnp.where(role_ref[0] == option, c, 0), 0, 0)
        )

    return pl.pallas_call(
        fold_kernel,
        grid_spec=pltpu.PrefetchScalarGridSpec(
            num_scalar_prefetch=1,
            grid=(chans // CHUNK,),
            in_specs=[block(i // 2) for i in range(len(parts))],
            out_specs=[pl.BlockSpec(out.shape, lambda c, role_ref: (0, 0, 0))] * 2,
            scratch_shapes=[VMEM((rows, chans, cols), BF16)],
        ),
        out_shape=(out, out),
        compiler_params=params(),
        cost_estimate=cost(0, 6 * parts[0].size),
        name="fold",
    )(role, *parts)


def finish_kernel(flag_ref, pair_ref, own_ref, other_ref, *refs):
    gate_ref, out_w_ref, in_ref, back_ref = refs[:4]
    earlier_ref, out_ref = refs[4] if len(refs) == 6 else None, refs[-1]
    _, half, cols, width = pair_ref.shape
    block, chans = cols // 2, width // 2
    hidden_units = back_ref.shape[1]
    front = flag_ref[0] == 0
    steps = (half + 1) // 2

    def step(i, carry):
        first = jnp.minimum(2 * i, half - 2)
        rows = [(h, first + e) for h in range(2) for e in range(2)]
        turned = [[ref[first + e].T[:, :block] for ref in (own_ref, other_ref)] for e in range(2)]
        tri = [
            jnp.concatenate([t[h * chans : (h + 1) * chans] for t in turned[e]], axis=0)
            for h in range(2)
            for e in range(2)
        ]
        tri_normed = norm_chans(jnp.concatenate(tri, axis=1).astype(F32)).astype(BF16)
        pair = []
        for h, r in rows:
            row = pair_ref[h, r].astype(F32)
            pair.append(jnp.where(front, row[:block], row[block:]))
        pair = jnp.concatenate(pair, axis=0).T
        normed = norm_chans(pair).astype(BF16)
        out_gate = sigmoid(jnp.dot(gate_ref[...], normed, preferred_element_type=F32))
        update = jnp.dot(out_w_ref[...], tri_normed, preferred_element_type=F32)
        updated = pair + out_gate * update
        trans_normed = norm_chans(updated).astype(BF16)
        expanded = jnp.dot(in_ref[...], trans_normed, preferred_element_type=F32)
        swish, linear = expanded[:hidden_units], expanded[hidden_units:]
        hidden = (swish * sigmoid(swish) * linear).astype(BF16)
        result = updated + jnp.dot(back_ref[...], hidden, preferred_element_type=F32)
        result = result.T
        for s, (h, r) in enumerate(rows):
            mine = result[s * block : (s + 1) * block]
            if earlier_ref is None:
                out_ref[h, r, :block] = mine.astype(BF16)
            else:
                past = earlier_ref[h, r].astype(F32)[:block]
                parts = [jnp.where(front, mine, past), jnp.where(front, past, mine)]
                out_ref[h, r] = jnp.concatenate(parts, axis=0).astype(BF16)
        return carry

    lax.fori_loop(0, steps, step, 0, unroll=2)


def finish(flag, pair, own, other, weights, earlier=None):
    _, half, cols, width = pair.shape
    shape = pair.shape if earlier is not None else (2, half, padded(cols // 2, 16), width)
    extra = [] if earlier is None else [earlier]
    return pl.pallas_call(
        finish_kernel,
        out_shape=jax.ShapeDtypeStruct(shape, BF16),
        in_specs=[pl.BlockSpec(memory_space=pltpu.SMEM)] + whole(7 + len(extra)),
        out_specs=pl.BlockSpec(memory_space=VMEM),
        compiler_params=params(),
        cost_estimate=cost(14 * pair.size * width, 4 * pair.size, 3 * pair.size),
        name="finish",
    )(flag, pair, own, other, *weights, *extra)


def layer_norm(values):
    centered = values - jnp.mean(values, axis=-1, keepdims=True)
    variance = jnp.mean(centered * centered, axis=-1, keepdims=True)
    return centered * lax.rsqrt(variance + 1e-05)


def any_mesh(pair, chain_lengths, in_weight, out_weight, trans_in, trans_out):
    tile_rows, tile_cols, width = pair.shape
    hidden_units = trans_out.shape[0]
    row_count = lax.axis_size("row")
    col_count = lax.axis_size("col")
    outer = row_count // 2
    tokens = tile_rows * row_count
    valid_count = tokens - chain_lengths[chain_lengths.shape[0] - 1]
    row_id = lax.axis_index("row")
    col_id = lax.axis_index("col")
    line_id = row_id // 2

    def along_line(value, step, targets):
        perm = [(2 * (t - step) + b, 2 * t + b) for t in targets for b in range(2)]
        return lax.ppermute(value, "row", perm)

    row_pos = row_id * tile_rows + jnp.arange(tile_rows, dtype=jnp.int32)
    col_pos = col_id * tile_cols + jnp.arange(tile_cols, dtype=jnp.int32)
    pair_mask = ((row_pos < valid_count)[:, None] & (col_pos < valid_count)[None, :]).astype(
        jnp.float32
    )[:, :, None]
    normed = layer_norm(pair.astype(jnp.float32)).astype(jnp.bfloat16).reshape(-1, width)

    def gated(offset):
        block = jnp.dot(
            normed,
            in_weight[:, offset * width : (offset + 2) * width],
            preferred_element_type=jnp.float32,
        ).reshape(tile_rows, tile_cols, 2 * width)
        value = jax.nn.sigmoid(block[..., :width]) * block[..., width:] * pair_mask
        return value.astype(jnp.bfloat16)

    right_ops = gated(2)
    from_left, from_right = {0: right_ops}, {0: right_ops}
    for step in range(1, outer):
        from_left[step] = along_line(from_left[step - 1], 1, range(step, outer))
        from_right[step] = along_line(from_right[step - 1], -1, range(0, outer - step))
    left_ops = gated(0)
    left_other = lax.ppermute(left_ops, "row", [(i, i ^ 1) for i in range(row_count)])
    lefts = jnp.concatenate([left_ops, left_other], axis=0)

    partials = []
    for source in range(outer):
        block = right_ops
        for step in range(1, outer):
            if source + step < outer:
                block = jnp.where(line_id == source + step, from_left[step], block)
            if source - step >= 0:
                block = jnp.where(line_id == source - step, from_right[step], block)
        partials.append(
            jnp.einsum("ikc,jkc->ijc", lefts, block, preferred_element_type=jnp.float32)
        )
    partial = jnp.stack(partials)
    share = outer // col_count
    mine = lax.dynamic_slice_in_dim(partial, col_id * share, share, 0)
    for hop in range(1, col_count):
        target = (col_id + hop) % col_count
        passed = lax.dynamic_slice_in_dim(partial, target * share, share, 0)
        mine = mine + lax.ppermute(
            passed, "col", [(c, (c + hop) % col_count) for c in range(col_count)]
        )
    tri_normed = layer_norm(mine).astype(jnp.bfloat16)
    own_part = tri_normed[:, :tile_rows]
    other_part = lax.ppermute(
        tri_normed[:, tile_rows:], "row", [(i, i ^ 1) for i in range(row_count)]
    )
    even = row_id % 2 == 0
    both = jnp.stack(
        [jnp.where(even, own_part, other_part), jnp.where(even, other_part, own_part)], axis=1
    )
    tri_normed = both.transpose(2, 0, 1, 3, 4).reshape(-1, width)

    out_gate = jax.nn.sigmoid(
        jnp.dot(normed, in_weight[:, 4 * width :], preferred_element_type=jnp.float32)
    )
    update = jnp.dot(tri_normed, out_weight, preferred_element_type=jnp.float32)
    updated = pair.astype(jnp.float32).reshape(-1, width) + out_gate * update
    trans_normed = layer_norm(updated).astype(jnp.bfloat16)
    expanded = jnp.dot(trans_normed, trans_in, preferred_element_type=jnp.float32)
    hidden = (jax.nn.silu(expanded[:, :hidden_units]) * expanded[:, hidden_units:]).astype(
        jnp.bfloat16
    )
    result = updated + jnp.dot(hidden, trans_out, preferred_element_type=jnp.float32)
    return result.reshape(tile_rows, tile_cols, width).astype(jnp.bfloat16)


def per_device(pair, chain_lengths, in_weight, out_weight, trans_in, trans_out):
    if (lax.axis_size("row"), lax.axis_size("col")) != (8, 2):
        return any_mesh(pair, chain_lengths, in_weight, out_weight, trans_in, trans_out)
    return two_by_four(pair, chain_lengths, in_weight, out_weight, trans_in, trans_out)


def two_by_four(pair, chain_lengths, in_weight, out_weight, trans_in, trans_out):
    tile_rows, tile_cols, width = pair.shape
    half = tile_rows // 2
    tokens = tile_rows * lax.axis_size("row")
    valid_count = tokens - chain_lengths[chain_lengths.shape[0] - 1]
    row_id, core = lax.axis_index("row"), lax.axis_index("col")
    place, side = row_id // 2, row_id % 2
    keeper = place // 2

    def among(value, moves):
        return lax.ppermute(value, "row", [(2 * s + b, 2 * t + b) for s, t in moves for b in range(2)])

    def across(value):
        return lax.ppermute(value, "row", [(i, i ^ 1) for i in range(8)])

    def to_core(value, places, keep):
        perm = []
        for z in places:
            target = z // 2 if keep else 1 - z // 2
            perm += [(4 * z + 2 * b + 1 - target, 4 * z + 2 * b + target) for b in range(2)]
        return lax.ppermute(value, ("row", "col"), perm)

    def by_side(block, axis):
        return jnp.where(side == 0, block, jnp.roll(block, width // 2, axis))

    def gate_pair(first):
        parts = [
            by_side(in_weight[:, (first + i) * width : (first + i + 1) * width], 1) for i in range(2)
        ]
        return jnp.concatenate(parts, axis=1).T

    where = jnp.stack([valid_count, row_id * tile_rows, core * tile_cols]).astype(jnp.int32)
    sides = side.astype(jnp.int32).reshape(1)
    is_keeper = core == keeper
    role = jnp.where(is_keeper, 0, 1).astype(jnp.int32).reshape(1)
    folded = pair.reshape(2, half, tile_cols, width)
    mates, cross = [(0, 1), (1, 0), (2, 3), (3, 2)], [(1, 2), (2, 1)]
    inward, outward = [(0, 1), (3, 2)], [(1, 0), (2, 3)]

    def after(value, *others):
        return lax.optimization_barrier((value, *others))[0]

    right_own, right_far = project(where, folded, gate_pair(2))
    mate_own, near_own = among(right_own, mates), among(right_own, cross)
    right_beside = across(right_far)
    left_own, left_far = project(where, folded, gate_pair(0))
    left_beside = across(after(left_far, right_beside))
    mate_beside, near_beside = among(right_beside, mates), among(right_beside, cross)
    far_own = among(after(mate_own, near_own), cross)
    guest_own = among(after(left_own, mate_own), inward)
    far_beside = among(after(mate_beside, near_beside), cross)
    guest_beside = among(after(left_beside, mate_beside), inward)

    left = left_major(left_own, left_beside)
    (home_own,) = triangle(sides, [left], right_own, right_beside)
    (home_mate,) = triangle(sides, [left], mate_own, mate_beside)
    left_guest = left_major(guest_own, guest_beside)
    away_near, lent_near = triangle(sides, [left, left_guest], near_own, near_beside)
    away_far, lent_far = triangle(sides, [left, left_guest], far_own, far_beside)

    inner = (place == 1) | (place == 2)
    order = jnp.where(is_keeper, place % 2, place // 2).astype(jnp.int32).reshape(1)
    weights = [w.T for w in (in_weight[:, 4 * width :], by_side(out_weight, 0), trans_in, trans_out)]
    result = None
    for i, (home, away, lent) in enumerate(
        ((home_own, away_near, lent_near), (home_mate, away_far, lent_far))
    ):
        returned = [among(v, outward) for v in fold(half, role, lent, to_core(lent, (1, 2), False))]
        kept = fold(half, role, home, to_core(home, range(4), True), away, to_core(away, (1, 2), False))
        own, beside = (jnp.where(is_keeper | inner, k, g) for k, g in zip(kept, returned))
        flag = order if i == 0 else 1 - order
        result = finish(flag, folded, own, across(beside), weights, result)
    return result.reshape(tile_rows, tile_cols, width)


def solution(mesh):
    placed = (P(("crops", "row"), "col", None), P("crops"), P(), P(), P(), P())
    return jax.shard_map(
        per_device,
        mesh=mesh,
        in_specs=placed,
        out_specs=P(("crops", "row"), "col", None),
        check_vma=False,
    )
```

```python
import functools

import jax
import jax.numpy as jnp
from jax import lax
from jax.experimental import pallas as pl
from jax.experimental.pallas import tpu as pltpu
from jax.sharding import PartitionSpec as P

VMEM = pltpu.VMEM
BF16, F32 = jnp.bfloat16, jnp.float32
CHUNK = 16


def whole(count):
    return [pl.BlockSpec(memory_space=VMEM)] * count


def params():
    return pltpu.CompilerParams(vmem_limit_bytes=48 << 20)


def cost(flops, moved, transcendentals=0):
    return pl.CostEstimate(flops=flops, bytes_accessed=moved, transcendentals=transcendentals)


def sigmoid(values):
    return 0.5 * jnp.tanh(0.5 * values) + 0.5


def norm_chans(values):
    centered = values - jnp.mean(values, axis=0, keepdims=True)
    variance = jnp.mean(centered * centered, axis=0, keepdims=True)
    return centered * lax.rsqrt(variance + 1e-05)


def padded(count, unit):
    return -(-count // unit) * unit


def project_kernel(where_ref, pair_ref, weight_ref, own_ref, far_ref):
    valid, row0, col0 = where_ref[0], where_ref[1], where_ref[2]
    _, half, cols, width = pair_ref.shape
    chans = width // 2
    tail = cols - width
    lane = lax.broadcasted_iota(jnp.int32, (1, 3 * width), 1)
    in_tail = lane >= 2 * width
    ends = jnp.where(in_tail, 2 * width + chans, width)
    is_first = jnp.where(lane < ends, 1, 0)
    token = jnp.where(in_tail, lane % chans + width, lane % width) + col0
    gap = jnp.zeros((chans - tail, width), F32)

    def step(r, carry):
        first, second = (pair_ref[h, r].astype(F32) for h in range(2))
        tokens = jnp.concatenate(
            [first[:width], second[:width], first[width:], gap, second[width:], gap], axis=0
        )
        normed = norm_chans(tokens.T).astype(BF16)
        both = jnp.dot(weight_ref[...], normed, preferred_element_type=F32)
        limits = [jnp.where(row0 + h * half + r < valid, valid, 0) for h in range(2)]
        keep = jnp.where(token < limits[1] + is_first * (limits[0] - limits[1]), 1.0, 0.0)
        out = (sigmoid(both[:width]) * both[width:] * keep).astype(BF16)
        own_ref[r] = out[:chans]
        far_ref[r] = out[chans:]
        return carry

    lax.fori_loop(0, half, step, 0, unroll=4)


def project(where, pair, weight):
    _, half, cols, width = pair.shape
    piece = jax.ShapeDtypeStruct((half, width // 2, 3 * width), BF16)
    return pl.pallas_call(
        project_kernel,
        out_shape=(piece, piece),
        in_specs=[pl.BlockSpec(memory_space=pltpu.SMEM)] + whole(2),
        out_specs=whole(2),
        compiler_params=params(),
        cost_estimate=cost(4 * pair.size * width, 4 * pair.size, pair.size),
        name="project",
    )(where, pair, weight)


def channel_major(pieces, left):
    half, chans, lanes = pieces[0].shape
    width = lanes // 3
    main, rest = [], []
    for piece in pieces:
        tail = piece[:, :, 2 * width :]
        turned = jnp.concatenate([tail[:, :, width // 2 :], tail[:, :, : width // 2]], axis=2)
        main += [piece[:, :, :width], piece[:, :, width : 2 * width]]
        rest += [tail, turned]
        if left:
            gap = jnp.zeros((padded(2 * half, 16) - 2 * half, chans, width), BF16)
            main.append(gap)
            rest.append(gap)
    rest = jnp.concatenate(rest, axis=0)
    if left:
        low = lax.broadcasted_iota(jnp.int32, rest.shape, 2) < width // 2
        rest = jnp.where(low, rest, jnp.zeros_like(rest))
    main = jnp.swapaxes(jnp.concatenate(main, axis=0), 0, 1)
    return main, jnp.swapaxes(rest, 0, 1)


def left_kernel(own_ref, beside_ref, out_ref):
    width = own_ref.shape[2] // 3
    main, rest = channel_major([own_ref[...], beside_ref[...]], True)
    out_ref[:, :, :width] = main
    out_ref[:, :, width:] = rest


def left_major(own, beside):
    half, chans, lanes = own.shape
    rows, deep = 2 * padded(2 * half, 16), lanes // 3 * 2
    piece = pl.BlockSpec((half, CHUNK, lanes), lambda c: (0, c, 0))
    return pl.pallas_call(
        left_kernel,
        grid=(chans // CHUNK,),
        out_shape=jax.ShapeDtypeStruct((chans, rows, deep), BF16),
        in_specs=[piece, piece],
        out_specs=pl.BlockSpec((CHUNK, rows, deep), lambda c: (c, 0, 0)),
        compiler_params=params(),
        cost_estimate=cost(0, 8 * own.size),
        name="left_major",
    )(own, beside)


def triangle_kernel(flag_ref, *refs, guests, options):
    lefts = refs[: 1 + guests]
    rights = refs[1 + guests : 1 + guests + 2 * options]
    outs, right_ref = refs[1 + guests + 2 * options : -1], refs[-1]
    own, beside = rights[0][...], rights[1][...]
    if options == 2:
        plain = flag_ref[1] == 0
        own = jnp.where(plain, own, rights[2][...])
        beside = jnp.where(plain, beside, rights[3][...])
    width = own.shape[2] // 3
    even = flag_ref[0] == 0
    main, rest = channel_major(
        [jnp.where(even, own, beside), jnp.where(even, beside, own)], False
    )
    rows = main.shape[1]

    @pl.when(pl.program_id(0) == 0)
    def _():
        right_ref[...] = jnp.zeros_like(right_ref)

    right_ref[:, :rows, :width] = main
    right_ref[:, :rows, width:] = rest
    for c in range(CHUNK):
        products = [
            lax.dot_general(
                left_ref[c], right_ref[c], (((1,), (1,)), ((), ())), preferred_element_type=F32
            ).astype(BF16)
            for left_ref in lefts
        ]
        outs[0][c] = products[0]
        if guests:
            part = products[1].shape[0] // 2
            outs[1][c] = products[1][:part]
            outs[2][c] = products[1][part:]


def triangle(flags, lefts, *pieces):
    half, chans, lanes = pieces[0].shape
    options, guests = len(pieces) // 2, len(lefts) - 1
    rows, cols, deep = lefts[0].shape[1], padded(4 * half, 128), lanes // 3 * 2

    def piece(option):
        if options == 1:
            return pl.BlockSpec((half, CHUNK, lanes), lambda c, flag_ref: (0, c, 0))
        return pl.BlockSpec(
            (half, CHUNK, lanes), lambda c, flag_ref: (0, jnp.where(flag_ref[1] == option, c, 0), 0)
        )

    def block(height, depth):
        return pl.BlockSpec((CHUNK, height, depth), lambda c, flag_ref: (c, 0, 0))

    heights = [rows] + [rows // 2] * (2 * guests)
    return pl.pallas_call(
        functools.partial(triangle_kernel, guests=guests, options=options),
        grid_spec=pltpu.PrefetchScalarGridSpec(
            num_scalar_prefetch=1,
            grid=(chans // CHUNK,),
            in_specs=[block(rows, deep)] * len(lefts) + [piece(i // 2) for i in range(len(pieces))],
            out_specs=[block(h, cols) for h in heights],
            scratch_shapes=[VMEM((CHUNK, cols, deep), BF16)],
        ),
        out_shape=[jax.ShapeDtypeStruct((chans, h, cols), BF16) for h in heights],
        compiler_params=params(),
        cost_estimate=cost(2 * len(lefts) * chans * rows * cols * deep, 10 * pieces[0].size),
        name="triangle",
    )(flags, *lefts, *pieces)


def fold_kernel(role_ref, *refs, outputs, half):
    outs, work_ref = refs[-1 - outputs : -1], refs[-1]
    cols = outs[0].shape[1]
    parts = refs[: -1 - outputs]
    c = pl.program_id(0)
    for option in range(2):

        @pl.when(role_ref[0] == option)
        def _(option=option):
            total = parts[2 * option][...].astype(F32) + parts[2 * option + 1][...].astype(F32)
            at = pl.ds(pl.multiple_of(c * CHUNK, CHUNK), CHUNK)
            work_ref[:, at, :] = jnp.swapaxes(total.astype(BF16), 0, 1)

    @pl.when(c == pl.num_programs(0) - 1)
    def _():
        pitch = work_ref.shape[0] // outputs
        for o, out_ref in enumerate(outs):

            def turn(r, carry, o=o, out_ref=out_ref):
                at = o * pitch + r
                stacked = jnp.concatenate([work_ref[at], work_ref[at + half]], axis=0)
                out_ref[r] = stacked.T[:cols]
                return carry

            lax.fori_loop(0, half, turn, 0, unroll=True)


def fold(half, role, *parts):
    chans, rows, cols = parts[0].shape
    outputs = rows // padded(2 * half, 16)
    out = jax.ShapeDtypeStruct((half, padded(4 * half, 16), 2 * chans), BF16)

    def block(option):
        return pl.BlockSpec(
            (CHUNK, rows, cols), lambda c, role_ref: (jnp.where(role_ref[0] == option, c, 0), 0, 0)
        )

    return pl.pallas_call(
        functools.partial(fold_kernel, outputs=outputs, half=half),
        grid_spec=pltpu.PrefetchScalarGridSpec(
            num_scalar_prefetch=1,
            grid=(chans // CHUNK,),
            in_specs=[block(i // 2) for i in range(4)],
            out_specs=[pl.BlockSpec(out.shape, lambda c, role_ref: (0, 0, 0))] * outputs,
            scratch_shapes=[VMEM((rows, chans, cols), BF16)],
        ),
        out_shape=[out] * outputs,
        compiler_params=params(),
        cost_estimate=cost(0, 6 * parts[0].size),
        name="fold",
    )(role, *parts)


def finish_kernel(flag_ref, pair_ref, own_ref, other_ref, *refs):
    gate_ref, out_w_ref, in_ref, back_ref = refs[:4]
    earlier_ref, out_ref = refs[4] if len(refs) == 6 else None, refs[-1]
    _, half, cols, width = pair_ref.shape
    block, chans = cols // 2, width // 2
    hidden_units = back_ref.shape[1]
    front = flag_ref[0] == 0
    steps = (half + 1) // 2

    def step(i, carry):
        first = jnp.minimum(2 * i, half - 2)
        rows = [(h, first + e) for h in range(2) for e in range(2)]
        turned = [[ref[first + e].T[:, :block] for ref in (own_ref, other_ref)] for e in range(2)]
        tri = [
            jnp.concatenate([t[h * chans : (h + 1) * chans] for t in turned[e]], axis=0)
            for h in range(2)
            for e in range(2)
        ]
        tri_normed = norm_chans(jnp.concatenate(tri, axis=1).astype(F32)).astype(BF16)
        pair = []
        for h, r in rows:
            row = pair_ref[h, r].astype(F32)
            pair.append(jnp.where(front, row[:block], row[block:]))
        pair = jnp.concatenate(pair, axis=0).T
        normed = norm_chans(pair).astype(BF16)
        out_gate = sigmoid(jnp.dot(gate_ref[...], normed, preferred_element_type=F32))
        update = jnp.dot(out_w_ref[...], tri_normed, preferred_element_type=F32)
        updated = pair + out_gate * update
        trans_normed = norm_chans(updated).astype(BF16)
        expanded = jnp.dot(in_ref[...], trans_normed, preferred_element_type=F32)
        swish, linear = expanded[:hidden_units], expanded[hidden_units:]
        hidden = (swish * sigmoid(swish) * linear).astype(BF16)
        result = updated + jnp.dot(back_ref[...], hidden, preferred_element_type=F32)
        result = result.T
        for s, (h, r) in enumerate(rows):
            mine = result[s * block : (s + 1) * block]
            if earlier_ref is None:
                out_ref[h, r, :block] = mine.astype(BF16)
            else:
                past = earlier_ref[h, r].astype(F32)[:block]
                parts = [jnp.where(front, mine, past), jnp.where(front, past, mine)]
                out_ref[h, r] = jnp.concatenate(parts, axis=0).astype(BF16)
        return carry

    lax.fori_loop(0, steps, step, 0, unroll=2)


def finish(flag, pair, own, other, weights, earlier=None):
    _, half, cols, width = pair.shape
    shape = pair.shape if earlier is not None else (2, half, padded(cols // 2, 16), width)
    extra = [] if earlier is None else [earlier]
    return pl.pallas_call(
        finish_kernel,
        out_shape=jax.ShapeDtypeStruct(shape, BF16),
        in_specs=[pl.BlockSpec(memory_space=pltpu.SMEM)] + whole(7 + len(extra)),
        out_specs=pl.BlockSpec(memory_space=VMEM),
        compiler_params=params(),
        cost_estimate=cost(14 * pair.size * width, 4 * pair.size, 3 * pair.size),
        name="finish",
    )(flag, pair, own, other, *weights, *extra)


def layer_norm(values):
    centered = values - jnp.mean(values, axis=-1, keepdims=True)
    variance = jnp.mean(centered * centered, axis=-1, keepdims=True)
    return centered * lax.rsqrt(variance + 1e-05)


def any_mesh(pair, chain_lengths, in_weight, out_weight, trans_in, trans_out):
    tile_rows, tile_cols, width = pair.shape
    hidden_units = trans_out.shape[0]
    row_count = lax.axis_size("row")
    col_count = lax.axis_size("col")
    outer = row_count // 2
    tokens = tile_rows * row_count
    valid_count = tokens - chain_lengths[chain_lengths.shape[0] - 1]
    row_id = lax.axis_index("row")
    col_id = lax.axis_index("col")
    line_id = row_id // 2

    def along_line(value, step, targets):
        perm = [(2 * (t - step) + b, 2 * t + b) for t in targets for b in range(2)]
        return lax.ppermute(value, "row", perm)

    row_pos = row_id * tile_rows + jnp.arange(tile_rows, dtype=jnp.int32)
    col_pos = col_id * tile_cols + jnp.arange(tile_cols, dtype=jnp.int32)
    pair_mask = ((row_pos < valid_count)[:, None] & (col_pos < valid_count)[None, :]).astype(
        jnp.float32
    )[:, :, None]
    normed = layer_norm(pair.astype(jnp.float32)).astype(jnp.bfloat16).reshape(-1, width)

    def gated(offset):
        block = jnp.dot(
            normed,
            in_weight[:, offset * width : (offset + 2) * width],
            preferred_element_type=jnp.float32,
        ).reshape(tile_rows, tile_cols, 2 * width)
        value = jax.nn.sigmoid(block[..., :width]) * block[..., width:] * pair_mask
        return value.astype(jnp.bfloat16)

    right_ops = gated(2)
    from_left, from_right = {0: right_ops}, {0: right_ops}
    for step in range(1, outer):
        from_left[step] = along_line(from_left[step - 1], 1, range(step, outer))
        from_right[step] = along_line(from_right[step - 1], -1, range(0, outer - step))
    left_ops = gated(0)
    left_other = lax.ppermute(left_ops, "row", [(i, i ^ 1) for i in range(row_count)])
    lefts = jnp.concatenate([left_ops, left_other], axis=0)

    partials = []
    for source in range(outer):
        block = right_ops
        for step in range(1, outer):
            if source + step < outer:
                block = jnp.where(line_id == source + step, from_left[step], block)
            if source - step >= 0:
                block = jnp.where(line_id == source - step, from_right[step], block)
        partials.append(
            jnp.einsum("ikc,jkc->ijc", lefts, block, preferred_element_type=jnp.float32)
        )
    partial = jnp.stack(partials)
    share = outer // col_count
    mine = lax.dynamic_slice_in_dim(partial, col_id * share, share, 0)
    for hop in range(1, col_count):
        target = (col_id + hop) % col_count
        passed = lax.dynamic_slice_in_dim(partial, target * share, share, 0)
        mine = mine + lax.ppermute(
            passed, "col", [(c, (c + hop) % col_count) for c in range(col_count)]
        )
    tri_normed = layer_norm(mine).astype(jnp.bfloat16)
    own_part = tri_normed[:, :tile_rows]
    other_part = lax.ppermute(
        tri_normed[:, tile_rows:], "row", [(i, i ^ 1) for i in range(row_count)]
    )
    even = row_id % 2 == 0
    both = jnp.stack(
        [jnp.where(even, own_part, other_part), jnp.where(even, other_part, own_part)], axis=1
    )
    tri_normed = both.transpose(2, 0, 1, 3, 4).reshape(-1, width)

    out_gate = jax.nn.sigmoid(
        jnp.dot(normed, in_weight[:, 4 * width :], preferred_element_type=jnp.float32)
    )
    update = jnp.dot(tri_normed, out_weight, preferred_element_type=jnp.float32)
    updated = pair.astype(jnp.float32).reshape(-1, width) + out_gate * update
    trans_normed = layer_norm(updated).astype(jnp.bfloat16)
    expanded = jnp.dot(trans_normed, trans_in, preferred_element_type=jnp.float32)
    hidden = (jax.nn.silu(expanded[:, :hidden_units]) * expanded[:, hidden_units:]).astype(
        jnp.bfloat16
    )
    result = updated + jnp.dot(hidden, trans_out, preferred_element_type=jnp.float32)
    return result.reshape(tile_rows, tile_cols, width).astype(jnp.bfloat16)


def per_device(pair, chain_lengths, in_weight, out_weight, trans_in, trans_out):
    if (lax.axis_size("row"), lax.axis_size("col")) != (8, 2):
        return any_mesh(pair, chain_lengths, in_weight, out_weight, trans_in, trans_out)
    return two_by_four(pair, chain_lengths, in_weight, out_weight, trans_in, trans_out)


def two_by_four(pair, chain_lengths, in_weight, out_weight, trans_in, trans_out):
    tile_rows, tile_cols, width = pair.shape
    half = tile_rows // 2
    tokens = tile_rows * lax.axis_size("row")
    valid_count = tokens - chain_lengths[chain_lengths.shape[0] - 1]
    row_id, core = lax.axis_index("row"), lax.axis_index("col")
    place, side = row_id // 2, row_id % 2
    keeper = place // 2

    def among(value, moves):
        return lax.ppermute(value, "row", [(2 * s + b, 2 * t + b) for s, t in moves for b in range(2)])

    def across(value):
        return lax.ppermute(value, "row", [(i, i ^ 1) for i in range(8)])

    def to_core(value, places, keep):
        perm = []
        for z, towards in zip(places, keep):
            target = z // 2 if towards else 1 - z // 2
            perm += [(4 * z + 2 * b + 1 - target, 4 * z + 2 * b + target) for b in range(2)]
        return lax.ppermute(value, ("row", "col"), perm)

    def give_back(value, swap):
        perm = []
        for s, t in ((1, 0), (2, 3)):
            away = 1 - t // 2
            source = 1 - away if swap else away
            perm += [(4 * s + 2 * b + source, 4 * t + 2 * (b ^ swap) + away) for b in range(2)]
        return lax.ppermute(value, ("row", "col"), perm)

    def by_side(block, axis):
        return jnp.where(side == 0, block, jnp.roll(block, width // 2, axis))

    def gate_pair(first):
        parts = [
            by_side(in_weight[:, (first + i) * width : (first + i + 1) * width], 1) for i in range(2)
        ]
        return jnp.concatenate(parts, axis=1).T

    def after(value, *others):
        return lax.optimization_barrier((value, *others))[0]

    def scalars(*values):
        return jnp.stack([jnp.asarray(v).astype(jnp.int32) for v in values])

    is_keeper = core == keeper
    inner = (place == 1) | (place == 2)
    where = scalars(valid_count, row_id * tile_rows, core * tile_cols)
    folded = pair.reshape(2, half, tile_cols, width)
    cross, inward, outward = [(1, 2), (2, 1)], [(0, 1), (3, 2)], [(1, 0), (2, 3)]
    everyone, inners = range(4), (1, 2)

    right_own, right_far = project(where, folded, gate_pair(2))
    from_end, near, from_inner = ([among(right_own, m)] for m in (inward, cross, outward))
    right_beside = across(right_far)
    left_own, left_far = project(where, folded, gate_pair(0))
    left_beside = across(after(left_far, right_beside))
    from_end.append(among(right_beside, inward))
    near.append(among(right_beside, cross))
    relay = [among(after(near[0], from_inner[0]), outward)]
    far = [among(after(from_end[0], near[0]), cross)]
    relay.append(among(after(near[1], from_inner[0]), outward))
    guest = [among(after(left_own, from_end[0]), inward)]
    far.append(among(after(from_end[1], near[1]), cross))
    from_inner.append(among(after(right_beside, relay[0]), outward))
    guest.append(among(after(left_beside, from_end[1]), inward))

    left = left_major(left_own, left_beside)
    (home,) = triangle(scalars(side, 0), [left], right_own, right_beside)
    home_rest = to_core(home, everyone, [True] * 4)
    (mate,) = triangle(scalars(side, 0), [left], *from_end)
    mate_rest = to_core(mate, inners, [True] * 2)
    (away,) = triangle(scalars(side, jnp.where(inner, 0, 1)), [left], *near, *relay)
    away_rest = to_core(away, everyone, [False] * 4)
    first = fold(half, scalars(jnp.where(is_keeper, 0, 1)), home, home_rest, away, away_rest)

    left_guest = left_major(after(guest[0], *first), guest[1])
    late, lent_own, lent_beside = triangle(
        scalars(side, jnp.where(inner, 0, 1)), [left, left_guest], *far, *from_inner
    )
    lent_rest = to_core(lent_own, inners, [False] * 2), to_core(lent_beside, inners, [True] * 2)
    late_rest = to_core(late, everyone, [True, False, False, True])
    (lent,) = fold(
        half, scalars(jnp.where(is_keeper, 0, 1)), lent_beside, lent_rest[1], lent_own, lent_rest[0]
    )
    given = give_back(lent, 0), give_back(lent, 1)
    second = fold(half, scalars(jnp.where(is_keeper & inner, 0, 1)), mate, mate_rest, late, late_rest)

    order = jnp.where(is_keeper, place % 2, place // 2)
    weights = [w.T for w in (in_weight[:, 4 * width :], by_side(out_weight, 0), trans_in, trans_out)]
    earlier = finish(scalars(order), folded, after(first[0], lent), across(first[1]), weights)
    kept = is_keeper | inner
    own = jnp.where(kept, second[0], given[0])
    other = jnp.where(kept, across(second[1]), given[1])
    result = finish(scalars(1 - order), folded, own, other, weights, earlier)
    return result.reshape(tile_rows, tile_cols, width)


def solution(mesh):
    placed = (P(("crops", "row"), "col", None), P("crops"), P(), P(), P(), P())
    return jax.shard_map(
        per_device,
        mesh=mesh,
        in_specs=placed,
        out_specs=P(("crops", "row"), "col", None),
        check_vma=False,
    )
```

```python
import functools

import jax
import jax.numpy as jnp
from jax import lax
from jax.experimental import pallas as pl
from jax.experimental.pallas import tpu as pltpu
from jax.sharding import PartitionSpec as P

VMEM = pltpu.VMEM
BF16, F32 = jnp.bfloat16, jnp.float32
CHUNK = 16


def whole(count):
    return [pl.BlockSpec(memory_space=VMEM)] * count


def params():
    return pltpu.CompilerParams(vmem_limit_bytes=48 << 20)


def cost(flops, moved, transcendentals=0):
    return pl.CostEstimate(flops=flops, bytes_accessed=moved, transcendentals=transcendentals)


def sigmoid(values):
    return 0.5 * jnp.tanh(0.5 * values) + 0.5


def norm_chans(values):
    centered = values - jnp.mean(values, axis=0, keepdims=True)
    variance = jnp.mean(centered * centered, axis=0, keepdims=True)
    return centered * lax.rsqrt(variance + 1e-05)


def padded(count, unit):
    return -(-count // unit) * unit


def project_kernel(where_ref, pair_ref, weight_ref, own_ref, far_ref):
    valid, row0, col0 = where_ref[0], where_ref[1], where_ref[2]
    _, half, cols, width = pair_ref.shape
    chans = width // 2
    tail = cols - width
    lane = lax.broadcasted_iota(jnp.int32, (1, 3 * width), 1)
    in_tail = lane >= 2 * width
    ends = jnp.where(in_tail, 2 * width + chans, width)
    is_first = jnp.where(lane < ends, 1, 0)
    token = jnp.where(in_tail, lane % chans + width, lane % width) + col0
    gap = jnp.zeros((chans - tail, width), F32)

    def step(r, carry):
        first, second = (pair_ref[h, r].astype(F32) for h in range(2))
        tokens = jnp.concatenate(
            [first[:width], second[:width], first[width:], gap, second[width:], gap], axis=0
        )
        normed = norm_chans(tokens.T).astype(BF16)
        both = jnp.dot(weight_ref[...], normed, preferred_element_type=F32)
        limits = [jnp.where(row0 + h * half + r < valid, valid, 0) for h in range(2)]
        keep = jnp.where(token < limits[1] + is_first * (limits[0] - limits[1]), 1.0, 0.0)
        out = (sigmoid(both[:width]) * both[width:] * keep).astype(BF16)
        own_ref[r] = out[:chans]
        far_ref[r] = out[chans:]
        return carry

    lax.fori_loop(0, half, step, 0, unroll=4)


def project(where, pair, weight):
    _, half, cols, width = pair.shape
    piece = jax.ShapeDtypeStruct((half, width // 2, 3 * width), BF16)
    return pl.pallas_call(
        project_kernel,
        out_shape=(piece, piece),
        in_specs=[pl.BlockSpec(memory_space=pltpu.SMEM)] + whole(2),
        out_specs=whole(2),
        compiler_params=params(),
        cost_estimate=cost(4 * pair.size * width, 4 * pair.size, pair.size),
        name="project",
    )(where, pair, weight)


def channel_major(pieces, left):
    half, chans, lanes = pieces[0].shape
    width = lanes // 3
    main, rest = [], []
    for piece in pieces:
        tail = piece[:, :, 2 * width :]
        turned = jnp.concatenate([tail[:, :, width // 2 :], tail[:, :, : width // 2]], axis=2)
        main += [piece[:, :, :width], piece[:, :, width : 2 * width]]
        rest += [tail, turned]
        if left:
            gap = jnp.zeros((padded(2 * half, 16) - 2 * half, chans, width), BF16)
            main.append(gap)
            rest.append(gap)
    rest = jnp.concatenate(rest, axis=0)
    if left:
        low = lax.broadcasted_iota(jnp.int32, rest.shape, 2) < width // 2
        rest = jnp.where(low, rest, jnp.zeros_like(rest))
    main = jnp.swapaxes(jnp.concatenate(main, axis=0), 0, 1)
    return main, jnp.swapaxes(rest, 0, 1)


def left_kernel(own_ref, beside_ref, out_ref):
    width = own_ref.shape[2] // 3
    main, rest = channel_major([own_ref[...], beside_ref[...]], True)
    out_ref[:, :, :width] = main
    out_ref[:, :, width:] = rest


def left_major(own, beside):
    half, chans, lanes = own.shape
    rows, deep = 2 * padded(2 * half, 16), lanes // 3 * 2
    piece = pl.BlockSpec((half, CHUNK, lanes), lambda c: (0, c, 0))
    return pl.pallas_call(
        left_kernel,
        grid=(chans // CHUNK,),
        out_shape=jax.ShapeDtypeStruct((chans, rows, deep), BF16),
        in_specs=[piece, piece],
        out_specs=pl.BlockSpec((CHUNK, rows, deep), lambda c: (c, 0, 0)),
        compiler_params=params(),
        cost_estimate=cost(0, 8 * own.size),
        name="left_major",
    )(own, beside)


def triangle_kernel(flag_ref, *refs, guests, options):
    lefts = refs[: 1 + guests]
    rights = refs[1 + guests : 1 + guests + 2 * options]
    outs, right_ref = refs[1 + guests + 2 * options : -1], refs[-1]
    own, beside = rights[0][...], rights[1][...]
    if options == 2:
        plain = flag_ref[1] == 0
        own = jnp.where(plain, own, rights[2][...])
        beside = jnp.where(plain, beside, rights[3][...])
    width = own.shape[2] // 3
    even = flag_ref[0] == 0
    main, rest = channel_major(
        [jnp.where(even, own, beside), jnp.where(even, beside, own)], False
    )
    rows = main.shape[1]

    @pl.when(pl.program_id(0) == 0)
    def _():
        right_ref[...] = jnp.zeros_like(right_ref)

    right_ref[:, :rows, :width] = main
    right_ref[:, :rows, width:] = rest
    for c in range(CHUNK):
        products = [
            lax.dot_general(
                left_ref[c], right_ref[c], (((1,), (1,)), ((), ())), preferred_element_type=F32
            ).astype(BF16)
            for left_ref in lefts
        ]
        outs[0][c] = products[0]
        if guests:
            part = products[1].shape[0] // 2
            outs[1][c] = products[1][:part]
            outs[2][c] = products[1][part:]


def triangle(flags, lefts, *pieces):
    half, chans, lanes = pieces[0].shape
    options, guests = len(pieces) // 2, len(lefts) - 1
    rows, cols, deep = lefts[0].shape[1], padded(4 * half, 128), lanes // 3 * 2

    def piece(option):
        if options == 1:
            return pl.BlockSpec((half, CHUNK, lanes), lambda c, flag_ref: (0, c, 0))
        return pl.BlockSpec(
            (half, CHUNK, lanes), lambda c, flag_ref: (0, jnp.where(flag_ref[1] == option, c, 0), 0)
        )

    def block(height, depth):
        return pl.BlockSpec((CHUNK, height, depth), lambda c, flag_ref: (c, 0, 0))

    heights = [rows] + [rows // 2] * (2 * guests)
    return pl.pallas_call(
        functools.partial(triangle_kernel, guests=guests, options=options),
        grid_spec=pltpu.PrefetchScalarGridSpec(
            num_scalar_prefetch=1,
            grid=(chans // CHUNK,),
            in_specs=[block(rows, deep)] * len(lefts) + [piece(i // 2) for i in range(len(pieces))],
            out_specs=[block(h, cols) for h in heights],
            scratch_shapes=[VMEM((CHUNK, cols, deep), BF16)],
        ),
        out_shape=[jax.ShapeDtypeStruct((chans, h, cols), BF16) for h in heights],
        compiler_params=params(),
        cost_estimate=cost(2 * len(lefts) * chans * rows * cols * deep, 10 * pieces[0].size),
        name="triangle",
    )(flags, *lefts, *pieces)


def fold_kernel(role_ref, *refs, outputs, half):
    outs, work_ref = refs[-1 - outputs : -1], refs[-1]
    cols = outs[0].shape[1]
    parts = refs[: -1 - outputs]
    c = pl.program_id(0)
    for option in range(2):

        @pl.when(role_ref[0] == option)
        def _(option=option):
            total = parts[2 * option][...].astype(F32) + parts[2 * option + 1][...].astype(F32)
            at = pl.ds(pl.multiple_of(c * CHUNK, CHUNK), CHUNK)
            work_ref[:, at, :] = jnp.swapaxes(total.astype(BF16), 0, 1)

    @pl.when(c == pl.num_programs(0) - 1)
    def _():
        pitch = work_ref.shape[0] // outputs
        for o, out_ref in enumerate(outs):

            def turn(r, carry, o=o, out_ref=out_ref):
                at = o * pitch + r
                stacked = jnp.concatenate([work_ref[at], work_ref[at + half]], axis=0)
                out_ref[r] = stacked.T[:cols]
                return carry

            lax.fori_loop(0, half, turn, 0, unroll=True)


def fold(half, role, *parts):
    chans, rows, cols = parts[0].shape
    outputs = rows // padded(2 * half, 16)
    out = jax.ShapeDtypeStruct((half, padded(4 * half, 16), 2 * chans), BF16)

    def block(option):
        return pl.BlockSpec(
            (CHUNK, rows, cols), lambda c, role_ref: (jnp.where(role_ref[0] == option, c, 0), 0, 0)
        )

    return pl.pallas_call(
        functools.partial(fold_kernel, outputs=outputs, half=half),
        grid_spec=pltpu.PrefetchScalarGridSpec(
            num_scalar_prefetch=1,
            grid=(chans // CHUNK,),
            in_specs=[block(i // 2) for i in range(4)],
            out_specs=[pl.BlockSpec(out.shape, lambda c, role_ref: (0, 0, 0))] * outputs,
            scratch_shapes=[VMEM((rows, chans, cols), BF16)],
        ),
        out_shape=[out] * outputs,
        compiler_params=params(),
        cost_estimate=cost(0, 6 * parts[0].size),
        name="fold",
    )(role, *parts)


def finish_kernel(flag_ref, pair_ref, own_ref, other_ref, *refs):
    gate_ref, out_w_ref, in_ref, back_ref = refs[:4]
    earlier_ref, out_ref = refs[4] if len(refs) == 6 else None, refs[-1]
    _, half, cols, width = pair_ref.shape
    block, chans = cols // 2, width // 2
    hidden_units = back_ref.shape[1]
    front = flag_ref[0] == 0
    steps = (half + 1) // 2

    def step(i, carry):
        first = jnp.minimum(2 * i, half - 2)
        rows = [(h, first + e) for h in range(2) for e in range(2)]
        turned = [[ref[first + e].T[:, :block] for ref in (own_ref, other_ref)] for e in range(2)]
        tri = [
            jnp.concatenate([t[h * chans : (h + 1) * chans] for t in turned[e]], axis=0)
            for h in range(2)
            for e in range(2)
        ]
        tri_normed = norm_chans(jnp.concatenate(tri, axis=1).astype(F32)).astype(BF16)
        pair = []
        for h, r in rows:
            row = pair_ref[h, r].astype(F32)
            pair.append(jnp.where(front, row[:block], row[block:]))
        pair = jnp.concatenate(pair, axis=0).T
        normed = norm_chans(pair).astype(BF16)
        out_gate = sigmoid(jnp.dot(gate_ref[...], normed, preferred_element_type=F32))
        update = jnp.dot(out_w_ref[...], tri_normed, preferred_element_type=F32)
        updated = pair + out_gate * update
        trans_normed = norm_chans(updated).astype(BF16)
        expanded = jnp.dot(in_ref[...], trans_normed, preferred_element_type=F32)
        swish, linear = expanded[:hidden_units], expanded[hidden_units:]
        hidden = (swish * sigmoid(swish) * linear).astype(BF16)
        result = updated + jnp.dot(back_ref[...], hidden, preferred_element_type=F32)
        result = result.T
        for s, (h, r) in enumerate(rows):
            mine = result[s * block : (s + 1) * block]
            if earlier_ref is None:
                out_ref[h, r, :block] = mine.astype(BF16)
            else:
                past = earlier_ref[h, r].astype(F32)[:block]
                parts = [jnp.where(front, mine, past), jnp.where(front, past, mine)]
                out_ref[h, r] = jnp.concatenate(parts, axis=0).astype(BF16)
        return carry

    lax.fori_loop(0, steps, step, 0, unroll=2)


def finish(flag, pair, own, other, weights, earlier=None):
    _, half, cols, width = pair.shape
    shape = pair.shape if earlier is not None else (2, half, padded(cols // 2, 16), width)
    extra = [] if earlier is None else [earlier]
    return pl.pallas_call(
        finish_kernel,
        out_shape=jax.ShapeDtypeStruct(shape, BF16),
        in_specs=[pl.BlockSpec(memory_space=pltpu.SMEM)] + whole(7 + len(extra)),
        out_specs=pl.BlockSpec(memory_space=VMEM),
        compiler_params=params(),
        cost_estimate=cost(14 * pair.size * width, 4 * pair.size, 3 * pair.size),
        name="finish",
    )(flag, pair, own, other, *weights, *extra)


def layer_norm(values):
    centered = values - jnp.mean(values, axis=-1, keepdims=True)
    variance = jnp.mean(centered * centered, axis=-1, keepdims=True)
    return centered * lax.rsqrt(variance + 1e-05)


def any_mesh(pair, chain_lengths, in_weight, out_weight, trans_in, trans_out):
    tile_rows, tile_cols, width = pair.shape
    hidden_units = trans_out.shape[0]
    row_count = lax.axis_size("row")
    col_count = lax.axis_size("col")
    outer = row_count // 2
    tokens = tile_rows * row_count
    valid_count = tokens - chain_lengths[chain_lengths.shape[0] - 1]
    row_id = lax.axis_index("row")
    col_id = lax.axis_index("col")
    line_id = row_id // 2

    def along_line(value, step, targets):
        perm = [(2 * (t - step) + b, 2 * t + b) for t in targets for b in range(2)]
        return lax.ppermute(value, "row", perm)

    row_pos = row_id * tile_rows + jnp.arange(tile_rows, dtype=jnp.int32)
    col_pos = col_id * tile_cols + jnp.arange(tile_cols, dtype=jnp.int32)
    pair_mask = ((row_pos < valid_count)[:, None] & (col_pos < valid_count)[None, :]).astype(
        jnp.float32
    )[:, :, None]
    normed = layer_norm(pair.astype(jnp.float32)).astype(jnp.bfloat16).reshape(-1, width)

    def gated(offset):
        block = jnp.dot(
            normed,
            in_weight[:, offset * width : (offset + 2) * width],
            preferred_element_type=jnp.float32,
        ).reshape(tile_rows, tile_cols, 2 * width)
        value = jax.nn.sigmoid(block[..., :width]) * block[..., width:] * pair_mask
        return value.astype(jnp.bfloat16)

    right_ops = gated(2)
    from_left, from_right = {0: right_ops}, {0: right_ops}
    for step in range(1, outer):
        from_left[step] = along_line(from_left[step - 1], 1, range(step, outer))
        from_right[step] = along_line(from_right[step - 1], -1, range(0, outer - step))
    left_ops = gated(0)
    left_other = lax.ppermute(left_ops, "row", [(i, i ^ 1) for i in range(row_count)])
    lefts = jnp.concatenate([left_ops, left_other], axis=0)

    partials = []
    for source in range(outer):
        block = right_ops
        for step in range(1, outer):
            if source + step < outer:
                block = jnp.where(line_id == source + step, from_left[step], block)
            if source - step >= 0:
                block = jnp.where(line_id == source - step, from_right[step], block)
        partials.append(
            jnp.einsum("ikc,jkc->ijc", lefts, block, preferred_element_type=jnp.float32)
        )
    partial = jnp.stack(partials)
    share = outer // col_count
    mine = lax.dynamic_slice_in_dim(partial, col_id * share, share, 0)
    for hop in range(1, col_count):
        target = (col_id + hop) % col_count
        passed = lax.dynamic_slice_in_dim(partial, target * share, share, 0)
        mine = mine + lax.ppermute(
            passed, "col", [(c, (c + hop) % col_count) for c in range(col_count)]
        )
    tri_normed = layer_norm(mine).astype(jnp.bfloat16)
    own_part = tri_normed[:, :tile_rows]
    other_part = lax.ppermute(
        tri_normed[:, tile_rows:], "row", [(i, i ^ 1) for i in range(row_count)]
    )
    even = row_id % 2 == 0
    both = jnp.stack(
        [jnp.where(even, own_part, other_part), jnp.where(even, other_part, own_part)], axis=1
    )
    tri_normed = both.transpose(2, 0, 1, 3, 4).reshape(-1, width)

    out_gate = jax.nn.sigmoid(
        jnp.dot(normed, in_weight[:, 4 * width :], preferred_element_type=jnp.float32)
    )
    update = jnp.dot(tri_normed, out_weight, preferred_element_type=jnp.float32)
    updated = pair.astype(jnp.float32).reshape(-1, width) + out_gate * update
    trans_normed = layer_norm(updated).astype(jnp.bfloat16)
    expanded = jnp.dot(trans_normed, trans_in, preferred_element_type=jnp.float32)
    hidden = (jax.nn.silu(expanded[:, :hidden_units]) * expanded[:, hidden_units:]).astype(
        jnp.bfloat16
    )
    result = updated + jnp.dot(hidden, trans_out, preferred_element_type=jnp.float32)
    return result.reshape(tile_rows, tile_cols, width).astype(jnp.bfloat16)


def per_device(pair, chain_lengths, in_weight, out_weight, trans_in, trans_out):
    if (lax.axis_size("row"), lax.axis_size("col")) != (8, 2):
        return any_mesh(pair, chain_lengths, in_weight, out_weight, trans_in, trans_out)
    return two_by_four(pair, chain_lengths, in_weight, out_weight, trans_in, trans_out)


def two_by_four(pair, chain_lengths, in_weight, out_weight, trans_in, trans_out):
    tile_rows, tile_cols, width = pair.shape
    half = tile_rows // 2
    tokens = tile_rows * lax.axis_size("row")
    valid_count = tokens - chain_lengths[chain_lengths.shape[0] - 1]
    row_id, core = lax.axis_index("row"), lax.axis_index("col")
    place, side = row_id // 2, row_id % 2
    keeper = place // 2

    def among(value, moves):
        return lax.ppermute(value, "row", [(2 * s + b, 2 * t + b) for s, t in moves for b in range(2)])

    def across(value):
        return lax.ppermute(value, "row", [(i, i ^ 1) for i in range(8)])

    def to_core(value, places, keep):
        perm = []
        for z, towards in zip(places, keep):
            target = z // 2 if towards else 1 - z // 2
            perm += [(4 * z + 2 * b + 1 - target, 4 * z + 2 * b + target) for b in range(2)]
        return lax.ppermute(value, ("row", "col"), perm)

    def give_back(value, swap):
        perm = []
        for s, t in ((1, 0), (2, 3)):
            away = 1 - t // 2
            source = 1 - away if swap else away
            perm += [(4 * s + 2 * b + source, 4 * t + 2 * (b ^ swap) + away) for b in range(2)]
        return lax.ppermute(value, ("row", "col"), perm)

    def by_side(block, axis):
        return jnp.where(side == 0, block, jnp.roll(block, width // 2, axis))

    def gate_pair(first):
        parts = [
            by_side(in_weight[:, (first + i) * width : (first + i + 1) * width], 1) for i in range(2)
        ]
        return jnp.concatenate(parts, axis=1).T

    def after(value, *others):
        return lax.optimization_barrier((value, *others))[0]

    def scalars(*values):
        return jnp.stack([jnp.asarray(v).astype(jnp.int32) for v in values])

    is_keeper = core == keeper
    inner = (place == 1) | (place == 2)
    where = scalars(valid_count, row_id * tile_rows, core * tile_cols)
    folded = pair.reshape(2, half, tile_cols, width)
    cross, inward, outward = [(1, 2), (2, 1)], [(0, 1), (3, 2)], [(1, 0), (2, 3)]
    everyone, inners = range(4), (1, 2)

    def phase(moves, finished):
        values = lax.optimization_barrier(tuple(v for _, v in moves) + tuple(finished))
        return [send(v) for (send, _), v in zip(moves, values)]

    def hop(moves):
        return lambda value: among(value, moves)

    right_own, right_far = project(where, folded, gate_pair(2))
    one = phase(
        [(hop(inward), right_own), (hop(cross), right_own), (hop(outward), right_own), (across, right_far)],
        (),
    )
    end_own, near_own, inner_own, right_beside = one
    left_own, left_far = project(where, folded, gate_pair(0))
    two = phase(
        [(hop(inward), right_beside), (hop(cross), right_beside), (hop(outward), near_own), (across, left_far)],
        one,
    )
    end_beside, near_beside, relay_own, left_beside = two
    three = phase([(hop(cross), end_own), (hop(inward), left_own), (hop(outward), near_beside)], two)
    far_own, guest_own, relay_beside = three
    four = phase(
        [(hop(cross), end_beside), (hop(inward), left_beside), (hop(outward), right_beside)], three
    )
    far_beside, guest_beside, inner_beside = four

    left = left_major(left_own, left_beside)
    (home,) = triangle(scalars(side, 0), [left], right_own, right_beside)
    home_rest = to_core(home, everyone, [True] * 4)
    (mate,) = triangle(scalars(side, 0), [left], end_own, end_beside)
    mate_rest = to_core(mate, inners, [True] * 2)
    outer = scalars(side, jnp.where(inner, 0, 1))
    (away,) = triangle(outer, [left], near_own, near_beside, relay_own, relay_beside)
    away_rest = to_core(away, everyone, [False] * 4)
    first = fold(half, scalars(jnp.where(is_keeper, 0, 1)), home, home_rest, away, away_rest)

    first_other = across(first[1])
    left_guest = left_major(after(guest_own, first_other, mate_rest), guest_beside)
    late, lent_own, lent_beside = triangle(
        outer, [left, left_guest], far_own, far_beside, inner_own, inner_beside
    )
    lent_rest = to_core(lent_own, inners, [False] * 2), to_core(lent_beside, inners, [True] * 2)
    late_rest = to_core(late, everyone, [True, False, False, True])
    (lent,) = fold(
        half, scalars(jnp.where(is_keeper, 0, 1)), lent_beside, lent_rest[1], lent_own, lent_rest[0]
    )
    given = give_back(lent, 0), give_back(lent, 1)
    second = fold(half, scalars(jnp.where(is_keeper & inner, 0, 1)), mate, mate_rest, late, late_rest)

    order = jnp.where(is_keeper, place % 2, place // 2)
    weights = [w.T for w in (in_weight[:, 4 * width :], by_side(out_weight, 0), trans_in, trans_out)]
    earlier = finish(scalars(order), folded, after(first[0], lent), first_other, weights)
    kept = is_keeper | inner
    own = jnp.where(kept, second[0], given[0])
    other = jnp.where(kept, across(second[1]), given[1])
    result = finish(scalars(1 - order), folded, own, other, weights, earlier)
    return result.reshape(tile_rows, tile_cols, width)


def solution(mesh):
    placed = (P(("crops", "row"), "col", None), P("crops"), P(), P(), P(), P())
    return jax.shard_map(
        per_device,
        mesh=mesh,
        in_specs=placed,
        out_specs=P(("crops", "row"), "col", None),
        check_vma=False,
    )
```

```python
import functools

import jax
import jax.numpy as jnp
from jax import lax
from jax.experimental import pallas as pl
from jax.experimental.pallas import tpu as pltpu
from jax.sharding import PartitionSpec as P

VMEM = pltpu.VMEM
BF16, F32 = jnp.bfloat16, jnp.float32
CHUNK = 16


def whole(count):
    return [pl.BlockSpec(memory_space=VMEM)] * count


def params():
    return pltpu.CompilerParams(vmem_limit_bytes=48 << 20)


def cost(flops, moved, transcendentals=0):
    return pl.CostEstimate(flops=flops, bytes_accessed=moved, transcendentals=transcendentals)


def sigmoid(values):
    return 0.5 * jnp.tanh(0.5 * values) + 0.5


def norm_chans(values):
    centered = values - jnp.mean(values, axis=0, keepdims=True)
    variance = jnp.mean(centered * centered, axis=0, keepdims=True)
    return centered * lax.rsqrt(variance + 1e-05)


def padded(count, unit):
    return -(-count // unit) * unit


def project_kernel(where_ref, pair_ref, weight_ref, own_ref, far_ref):
    valid, row0, col0 = where_ref[0], where_ref[1], where_ref[2]
    _, half, cols, width = pair_ref.shape
    chans = width // 2
    tail = cols - width
    lane = lax.broadcasted_iota(jnp.int32, (1, 3 * width), 1)
    in_tail = lane >= 2 * width
    ends = jnp.where(in_tail, 2 * width + chans, width)
    is_first = jnp.where(lane < ends, 1, 0)
    token = jnp.where(in_tail, lane % chans + width, lane % width) + col0
    gap = jnp.zeros((chans - tail, width), F32)

    def step(r, carry):
        first, second = (pair_ref[h, r].astype(F32) for h in range(2))
        tokens = jnp.concatenate(
            [first[:width], second[:width], first[width:], gap, second[width:], gap], axis=0
        )
        normed = norm_chans(tokens.T).astype(BF16)
        both = jnp.dot(weight_ref[...], normed, preferred_element_type=F32)
        limits = [jnp.where(row0 + h * half + r < valid, valid, 0) for h in range(2)]
        keep = jnp.where(token < limits[1] + is_first * (limits[0] - limits[1]), 1.0, 0.0)
        out = (sigmoid(both[:width]) * both[width:] * keep).astype(BF16)
        own_ref[r] = out[:chans]
        far_ref[r] = out[chans:]
        return carry

    lax.fori_loop(0, half, step, 0, unroll=4)


def project(where, pair, weight):
    _, half, cols, width = pair.shape
    piece = jax.ShapeDtypeStruct((half, width // 2, 3 * width), BF16)
    return pl.pallas_call(
        project_kernel,
        out_shape=(piece, piece),
        in_specs=[pl.BlockSpec(memory_space=pltpu.SMEM)] + whole(2),
        out_specs=whole(2),
        compiler_params=params(),
        cost_estimate=cost(4 * pair.size * width, 4 * pair.size, pair.size),
        name="project",
    )(where, pair, weight)


def channel_major(pieces, left):
    half, chans, lanes = pieces[0].shape
    width = lanes // 3
    main, rest = [], []
    for piece in pieces:
        tail = piece[:, :, 2 * width :]
        turned = jnp.concatenate([tail[:, :, width // 2 :], tail[:, :, : width // 2]], axis=2)
        main += [piece[:, :, :width], piece[:, :, width : 2 * width]]
        rest += [tail, turned]
        if left:
            gap = jnp.zeros((padded(2 * half, 16) - 2 * half, chans, width), BF16)
            main.append(gap)
            rest.append(gap)
    rest = jnp.concatenate(rest, axis=0)
    if left:
        low = lax.broadcasted_iota(jnp.int32, rest.shape, 2) < width // 2
        rest = jnp.where(low, rest, jnp.zeros_like(rest))
    main = jnp.swapaxes(jnp.concatenate(main, axis=0), 0, 1)
    return main, jnp.swapaxes(rest, 0, 1)


def left_kernel(own_ref, beside_ref, out_ref):
    width = own_ref.shape[2] // 3
    main, rest = channel_major([own_ref[...], beside_ref[...]], True)
    out_ref[:, :, :width] = main
    out_ref[:, :, width:] = rest


def left_major(own, beside):
    half, chans, lanes = own.shape
    rows, deep = 2 * padded(2 * half, 16), lanes // 3 * 2
    piece = pl.BlockSpec((half, CHUNK, lanes), lambda c: (0, c, 0))
    return pl.pallas_call(
        left_kernel,
        grid=(chans // CHUNK,),
        out_shape=jax.ShapeDtypeStruct((chans, rows, deep), BF16),
        in_specs=[piece, piece],
        out_specs=pl.BlockSpec((CHUNK, rows, deep), lambda c: (c, 0, 0)),
        compiler_params=params(),
        cost_estimate=cost(0, 8 * own.size),
        name="left_major",
    )(own, beside)


def triangle_kernel(flag_ref, *refs, guests, options):
    lefts = refs[: 1 + guests]
    rights = refs[1 + guests : 1 + guests + 2 * options]
    outs, right_ref = refs[1 + guests + 2 * options : -1], refs[-1]
    own, beside = rights[0][...], rights[1][...]
    if options == 2:
        plain = flag_ref[1] == 0
        own = jnp.where(plain, own, rights[2][...])
        beside = jnp.where(plain, beside, rights[3][...])
    width = own.shape[2] // 3
    even = flag_ref[0] == 0
    main, rest = channel_major(
        [jnp.where(even, own, beside), jnp.where(even, beside, own)], False
    )
    rows = main.shape[1]

    @pl.when(pl.program_id(0) == 0)
    def _():
        right_ref[...] = jnp.zeros_like(right_ref)

    right_ref[:, :rows, :width] = main
    right_ref[:, :rows, width:] = rest
    for c in range(CHUNK):
        products = [
            lax.dot_general(
                left_ref[c], right_ref[c], (((1,), (1,)), ((), ())), preferred_element_type=F32
            ).astype(BF16)
            for left_ref in lefts
        ]
        outs[0][c] = products[0]
        if guests:
            part = products[1].shape[0] // 2
            outs[1][c] = products[1][:part]
            outs[2][c] = products[1][part:]


def triangle(flags, lefts, *pieces):
    half, chans, lanes = pieces[0].shape
    options, guests = len(pieces) // 2, len(lefts) - 1
    rows, cols, deep = lefts[0].shape[1], padded(4 * half, 128), lanes // 3 * 2

    def piece(option):
        if options == 1:
            return pl.BlockSpec((half, CHUNK, lanes), lambda c, flag_ref: (0, c, 0))
        return pl.BlockSpec(
            (half, CHUNK, lanes), lambda c, flag_ref: (0, jnp.where(flag_ref[1] == option, c, 0), 0)
        )

    def block(height, depth):
        return pl.BlockSpec((CHUNK, height, depth), lambda c, flag_ref: (c, 0, 0))

    heights = [rows] + [rows // 2] * (2 * guests)
    return pl.pallas_call(
        functools.partial(triangle_kernel, guests=guests, options=options),
        grid_spec=pltpu.PrefetchScalarGridSpec(
            num_scalar_prefetch=1,
            grid=(chans // CHUNK,),
            in_specs=[block(rows, deep)] * len(lefts) + [piece(i // 2) for i in range(len(pieces))],
            out_specs=[block(h, cols) for h in heights],
            scratch_shapes=[VMEM((CHUNK, cols, deep), BF16)],
        ),
        out_shape=[jax.ShapeDtypeStruct((chans, h, cols), BF16) for h in heights],
        compiler_params=params(),
        cost_estimate=cost(2 * len(lefts) * chans * rows * cols * deep, 10 * pieces[0].size),
        name="triangle",
    )(flags, *lefts, *pieces)


def fold_kernel(role_ref, *refs, outputs, half):
    outs, work_ref = refs[-1 - outputs : -1], refs[-1]
    cols = outs[0].shape[1]
    parts = refs[: -1 - outputs]
    c = pl.program_id(0)
    for option in range(2):

        @pl.when(role_ref[0] == option)
        def _(option=option):
            total = parts[2 * option][...].astype(F32) + parts[2 * option + 1][...].astype(F32)
            at = pl.ds(pl.multiple_of(c * CHUNK, CHUNK), CHUNK)
            work_ref[:, at, :] = jnp.swapaxes(total.astype(BF16), 0, 1)

    @pl.when(c == pl.num_programs(0) - 1)
    def _():
        pitch = work_ref.shape[0] // outputs
        for o, out_ref in enumerate(outs):

            def turn(r, carry, o=o, out_ref=out_ref):
                at = o * pitch + r
                stacked = jnp.concatenate([work_ref[at], work_ref[at + half]], axis=0)
                out_ref[r] = stacked.T[:cols]
                return carry

            lax.fori_loop(0, half, turn, 0, unroll=True)


def fold(half, role, *parts):
    chans, rows, cols = parts[0].shape
    outputs = rows // padded(2 * half, 16)
    out = jax.ShapeDtypeStruct((half, padded(4 * half, 16), 2 * chans), BF16)

    def block(option):
        return pl.BlockSpec(
            (CHUNK, rows, cols), lambda c, role_ref: (jnp.where(role_ref[0] == option, c, 0), 0, 0)
        )

    return pl.pallas_call(
        functools.partial(fold_kernel, outputs=outputs, half=half),
        grid_spec=pltpu.PrefetchScalarGridSpec(
            num_scalar_prefetch=1,
            grid=(chans // CHUNK,),
            in_specs=[block(i // 2) for i in range(4)],
            out_specs=[pl.BlockSpec(out.shape, lambda c, role_ref: (0, 0, 0))] * outputs,
            scratch_shapes=[VMEM((rows, chans, cols), BF16)],
        ),
        out_shape=[out] * outputs,
        compiler_params=params(),
        cost_estimate=cost(0, 6 * parts[0].size),
        name="fold",
    )(role, *parts)


def finish_kernel(flag_ref, pair_ref, own_ref, other_ref, *refs):
    gate_ref, out_w_ref, in_ref, back_ref = refs[:4]
    earlier_ref, out_ref = refs[4] if len(refs) == 6 else None, refs[-1]
    _, half, cols, width = pair_ref.shape
    block, chans = cols // 2, width // 2
    hidden_units = back_ref.shape[1]
    front = flag_ref[0] == 0
    steps = (half + 1) // 2

    def step(i, carry):
        first = jnp.minimum(2 * i, half - 2)
        rows = [(h, first + e) for h in range(2) for e in range(2)]
        turned = [[ref[first + e].T[:, :block] for ref in (own_ref, other_ref)] for e in range(2)]
        tri = [
            jnp.concatenate([t[h * chans : (h + 1) * chans] for t in turned[e]], axis=0)
            for h in range(2)
            for e in range(2)
        ]
        tri_normed = norm_chans(jnp.concatenate(tri, axis=1).astype(F32)).astype(BF16)
        pair = []
        for h, r in rows:
            row = pair_ref[h, r].astype(F32)
            pair.append(jnp.where(front, row[:block], row[block:]))
        pair = jnp.concatenate(pair, axis=0).T
        normed = norm_chans(pair).astype(BF16)
        out_gate = sigmoid(jnp.dot(gate_ref[...], normed, preferred_element_type=F32))
        update = jnp.dot(out_w_ref[...], tri_normed, preferred_element_type=F32)
        updated = pair + out_gate * update
        trans_normed = norm_chans(updated).astype(BF16)
        expanded = jnp.dot(in_ref[...], trans_normed, preferred_element_type=F32)
        swish, linear = expanded[:hidden_units], expanded[hidden_units:]
        hidden = (swish * sigmoid(swish) * linear).astype(BF16)
        result = updated + jnp.dot(back_ref[...], hidden, preferred_element_type=F32)
        result = result.T
        for s, (h, r) in enumerate(rows):
            mine = result[s * block : (s + 1) * block]
            if earlier_ref is None:
                out_ref[h, r, :block] = mine.astype(BF16)
            else:
                past = earlier_ref[h, r].astype(F32)[:block]
                parts = [jnp.where(front, mine, past), jnp.where(front, past, mine)]
                out_ref[h, r] = jnp.concatenate(parts, axis=0).astype(BF16)
        return carry

    lax.fori_loop(0, steps, step, 0, unroll=2)


def finish(flag, pair, own, other, weights, earlier=None):
    _, half, cols, width = pair.shape
    shape = pair.shape if earlier is not None else (2, half, padded(cols // 2, 16), width)
    extra = [] if earlier is None else [earlier]
    return pl.pallas_call(
        finish_kernel,
        out_shape=jax.ShapeDtypeStruct(shape, BF16),
        in_specs=[pl.BlockSpec(memory_space=pltpu.SMEM)] + whole(7 + len(extra)),
        out_specs=pl.BlockSpec(memory_space=VMEM),
        compiler_params=params(),
        cost_estimate=cost(14 * pair.size * width, 4 * pair.size, 3 * pair.size),
        name="finish",
    )(flag, pair, own, other, *weights, *extra)


def layer_norm(values):
    centered = values - jnp.mean(values, axis=-1, keepdims=True)
    variance = jnp.mean(centered * centered, axis=-1, keepdims=True)
    return centered * lax.rsqrt(variance + 1e-05)


def any_mesh(pair, chain_lengths, in_weight, out_weight, trans_in, trans_out):
    tile_rows, tile_cols, width = pair.shape
    hidden_units = trans_out.shape[0]
    row_count = lax.axis_size("row")
    col_count = lax.axis_size("col")
    outer = row_count // 2
    tokens = tile_rows * row_count
    valid_count = tokens - chain_lengths[chain_lengths.shape[0] - 1]
    row_id = lax.axis_index("row")
    col_id = lax.axis_index("col")
    line_id = row_id // 2

    def along_line(value, step, targets):
        perm = [(2 * (t - step) + b, 2 * t + b) for t in targets for b in range(2)]
        return lax.ppermute(value, "row", perm)

    row_pos = row_id * tile_rows + jnp.arange(tile_rows, dtype=jnp.int32)
    col_pos = col_id * tile_cols + jnp.arange(tile_cols, dtype=jnp.int32)
    pair_mask = ((row_pos < valid_count)[:, None] & (col_pos < valid_count)[None, :]).astype(
        jnp.float32
    )[:, :, None]
    normed = layer_norm(pair.astype(jnp.float32)).astype(jnp.bfloat16).reshape(-1, width)

    def gated(offset):
        block = jnp.dot(
            normed,
            in_weight[:, offset * width : (offset + 2) * width],
            preferred_element_type=jnp.float32,
        ).reshape(tile_rows, tile_cols, 2 * width)
        value = jax.nn.sigmoid(block[..., :width]) * block[..., width:] * pair_mask
        return value.astype(jnp.bfloat16)

    right_ops = gated(2)
    from_left, from_right = {0: right_ops}, {0: right_ops}
    for step in range(1, outer):
        from_left[step] = along_line(from_left[step - 1], 1, range(step, outer))
        from_right[step] = along_line(from_right[step - 1], -1, range(0, outer - step))
    left_ops = gated(0)
    left_other = lax.ppermute(left_ops, "row", [(i, i ^ 1) for i in range(row_count)])
    lefts = jnp.concatenate([left_ops, left_other], axis=0)

    partials = []
    for source in range(outer):
        block = right_ops
        for step in range(1, outer):
            if source + step < outer:
                block = jnp.where(line_id == source + step, from_left[step], block)
            if source - step >= 0:
                block = jnp.where(line_id == source - step, from_right[step], block)
        partials.append(
            jnp.einsum("ikc,jkc->ijc", lefts, block, preferred_element_type=jnp.float32)
        )
    partial = jnp.stack(partials)
    share = outer // col_count
    mine = lax.dynamic_slice_in_dim(partial, col_id * share, share, 0)
    for hop in range(1, col_count):
        target = (col_id + hop) % col_count
        passed = lax.dynamic_slice_in_dim(partial, target * share, share, 0)
        mine = mine + lax.ppermute(
            passed, "col", [(c, (c + hop) % col_count) for c in range(col_count)]
        )
    tri_normed = layer_norm(mine).astype(jnp.bfloat16)
    own_part = tri_normed[:, :tile_rows]
    other_part = lax.ppermute(
        tri_normed[:, tile_rows:], "row", [(i, i ^ 1) for i in range(row_count)]
    )
    even = row_id % 2 == 0
    both = jnp.stack(
        [jnp.where(even, own_part, other_part), jnp.where(even, other_part, own_part)], axis=1
    )
    tri_normed = both.transpose(2, 0, 1, 3, 4).reshape(-1, width)

    out_gate = jax.nn.sigmoid(
        jnp.dot(normed, in_weight[:, 4 * width :], preferred_element_type=jnp.float32)
    )
    update = jnp.dot(tri_normed, out_weight, preferred_element_type=jnp.float32)
    updated = pair.astype(jnp.float32).reshape(-1, width) + out_gate * update
    trans_normed = layer_norm(updated).astype(jnp.bfloat16)
    expanded = jnp.dot(trans_normed, trans_in, preferred_element_type=jnp.float32)
    hidden = (jax.nn.silu(expanded[:, :hidden_units]) * expanded[:, hidden_units:]).astype(
        jnp.bfloat16
    )
    result = updated + jnp.dot(hidden, trans_out, preferred_element_type=jnp.float32)
    return result.reshape(tile_rows, tile_cols, width).astype(jnp.bfloat16)


def per_device(pair, chain_lengths, in_weight, out_weight, trans_in, trans_out):
    if (lax.axis_size("row"), lax.axis_size("col")) != (8, 2):
        return any_mesh(pair, chain_lengths, in_weight, out_weight, trans_in, trans_out)
    return two_by_four(pair, chain_lengths, in_weight, out_weight, trans_in, trans_out)


def two_by_four(pair, chain_lengths, in_weight, out_weight, trans_in, trans_out):
    tile_rows, tile_cols, width = pair.shape
    half = tile_rows // 2
    tokens = tile_rows * lax.axis_size("row")
    valid_count = tokens - chain_lengths[chain_lengths.shape[0] - 1]
    row_id, core = lax.axis_index("row"), lax.axis_index("col")
    place, side = row_id // 2, row_id % 2
    keeper = place // 2

    def among(value, moves):
        return lax.ppermute(value, "row", [(2 * s + b, 2 * t + b) for s, t in moves for b in range(2)])

    def across(value):
        return lax.ppermute(value, "row", [(i, i ^ 1) for i in range(8)])

    def to_core(value, places, keep):
        perm = []
        for z, towards in zip(places, keep):
            target = z // 2 if towards else 1 - z // 2
            perm += [(4 * z + 2 * b + 1 - target, 4 * z + 2 * b + target) for b in range(2)]
        return lax.ppermute(value, ("row", "col"), perm)

    def give_back(value, swap):
        perm = []
        for s, t in ((1, 0), (2, 3)):
            away = 1 - t // 2
            source = 1 - away if swap else away
            perm += [(4 * s + 2 * b + source, 4 * t + 2 * (b ^ swap) + away) for b in range(2)]
        return lax.ppermute(value, ("row", "col"), perm)

    def by_side(block, axis):
        return jnp.where(side == 0, block, jnp.roll(block, width // 2, axis))

    def gate_pair(first):
        parts = [
            by_side(in_weight[:, (first + i) * width : (first + i + 1) * width], 1) for i in range(2)
        ]
        return jnp.concatenate(parts, axis=1).T

    def after(value, *others):
        return lax.optimization_barrier((value, *others))[0]

    def scalars(*values):
        return jnp.stack([jnp.asarray(v).astype(jnp.int32) for v in values])

    is_keeper = core == keeper
    inner = (place == 1) | (place == 2)
    where = scalars(valid_count, row_id * tile_rows, core * tile_cols)
    folded = pair.reshape(2, half, tile_cols, width)
    cross = [(1, 2), (2, 1)]
    everyone, inners = range(4), (1, 2)

    def phase(moves, finished):
        values = lax.optimization_barrier(tuple(v for _, v in moves) + tuple(finished))
        return [send(v) for (send, _), v in zip(moves, values)]

    def hop(moves):
        return lambda value: among(value, moves)

    def either(at_inner, at_end):
        return jnp.where(inner, at_inner, at_end)

    swap = hop([(0, 1), (1, 0), (2, 3), (3, 2)])
    right_own, right_far = project(where, folded, gate_pair(2))
    one = phase([(swap, right_own), (hop(cross), right_own), (across, right_far)], ())
    mate_own, near_own, right_beside = one
    left_own, left_far = project(where, folded, gate_pair(0))
    two = phase(
        [(swap, either(near_own, right_beside)), (hop(cross), right_beside), (across, left_far)], one
    )
    mate_beside, near_beside, left_beside = two
    three = phase([(swap, either(near_beside, left_own)), (hop(cross), mate_own)], two)
    guest_own, far_own = three
    left = left_major(left_own, left_beside)
    (home,) = triangle(scalars(side, 0), [left], right_own, right_beside)
    home_rest = to_core(home, everyone, [True] * 4)
    (mate,) = triangle(scalars(side, 0), [left], mate_own, mate_beside)
    mate_rest = to_core(mate, inners, [True] * 2)
    four = phase([(swap, either(right_beside, left_beside)), (hop(cross), mate_beside)], three + [home, mate])
    guest_beside, far_beside = four

    outer = scalars(side, jnp.where(inner, 0, 1))
    (away,) = triangle(
        outer, [left], after(near_own, far_own, mate), near_beside, mate_beside, guest_own
    )
    away_rest = to_core(away, everyone, [False] * 4)
    first = fold(half, scalars(jnp.where(is_keeper, 0, 1)), home, home_rest, away, away_rest)

    first_other = across(first[1])
    left_guest = left_major(after(guest_own, first_other, mate_rest), guest_beside)
    late, lent_own, lent_beside = triangle(
        outer, [left, left_guest], far_own, far_beside, mate_own, guest_beside
    )
    lent_rest = to_core(lent_own, inners, [False] * 2), to_core(lent_beside, inners, [True] * 2)
    late_rest = to_core(late, everyone, [True, False, False, True])
    (lent,) = fold(
        half, scalars(jnp.where(is_keeper, 0, 1)), lent_beside, lent_rest[1], lent_own, lent_rest[0]
    )
    given = give_back(lent, 0), give_back(lent, 1)
    second = fold(half, scalars(jnp.where(is_keeper & inner, 0, 1)), mate, mate_rest, late, late_rest)

    order = jnp.where(is_keeper, place % 2, place // 2)
    weights = [w.T for w in (in_weight[:, 4 * width :], by_side(out_weight, 0), trans_in, trans_out)]
    earlier = finish(scalars(order), folded, after(first[0], lent), first_other, weights)
    kept = is_keeper | inner
    own = jnp.where(kept, second[0], given[0])
    other = jnp.where(kept, across(second[1]), given[1])
    result = finish(scalars(1 - order), folded, own, other, weights, earlier)
    return result.reshape(tile_rows, tile_cols, width)


def solution(mesh):
    placed = (P(("crops", "row"), "col", None), P("crops"), P(), P(), P(), P())
    return jax.shard_map(
        per_device,
        mesh=mesh,
        in_specs=placed,
        out_specs=P(("crops", "row"), "col", None),
        check_vma=False,
    )
```

```python
import functools

import jax
import jax.numpy as jnp
from jax import lax
from jax.experimental import pallas as pl
from jax.experimental.pallas import tpu as pltpu
from jax.sharding import PartitionSpec as P

VMEM = pltpu.VMEM
BF16, F32 = jnp.bfloat16, jnp.float32
CHUNK = 16


def whole(count):
    return [pl.BlockSpec(memory_space=VMEM)] * count


def params():
    return pltpu.CompilerParams(vmem_limit_bytes=48 << 20)


def cost(flops, moved, transcendentals=0):
    return pl.CostEstimate(flops=flops, bytes_accessed=moved, transcendentals=transcendentals)


def twice_sigmoid(halved):
    return jnp.tanh(halved) + 1.0


def norm_chans(values):
    centered = values - jnp.mean(values, axis=0, keepdims=True)
    variance = jnp.mean(centered * centered, axis=0, keepdims=True)
    return centered * lax.rsqrt(variance + 1e-05)


def padded(count, unit):
    return -(-count // unit) * unit


def project_kernel(where_ref, pair_ref, weight_ref, own_ref, far_ref):
    valid, row0, col0 = where_ref[0], where_ref[1], where_ref[2]
    _, half, cols, width = pair_ref.shape
    chans = width // 2
    tail = cols - width
    lane = lax.broadcasted_iota(jnp.int32, (1, 3 * width), 1)
    in_tail = lane >= 2 * width
    ends = jnp.where(in_tail, 2 * width + chans, width)
    is_first = jnp.where(lane < ends, 1, 0)
    token = jnp.where(in_tail, lane % chans + width, lane % width) + col0
    gap = jnp.zeros((chans - tail, width), F32)

    def step(r, carry):
        first, second = (pair_ref[h, r].astype(F32) for h in range(2))
        tokens = jnp.concatenate(
            [first[:width], second[:width], first[width:], gap, second[width:], gap], axis=0
        )
        normed = norm_chans(tokens.T).astype(BF16)
        both = jnp.dot(weight_ref[...], normed, preferred_element_type=F32)
        limits = [jnp.where(row0 + h * half + r < valid, valid, 0) for h in range(2)]
        keep = jnp.where(token < limits[1] + is_first * (limits[0] - limits[1]), 1.0, 0.0)
        out = (twice_sigmoid(both[:width]) * both[width:] * keep).astype(BF16)
        own_ref[r] = out[:chans]
        far_ref[r] = out[chans:]
        return carry

    lax.fori_loop(0, half, step, 0, unroll=4)


def project(where, pair, weight):
    _, half, cols, width = pair.shape
    piece = jax.ShapeDtypeStruct((half, width // 2, 3 * width), BF16)
    return pl.pallas_call(
        project_kernel,
        out_shape=(piece, piece),
        in_specs=[pl.BlockSpec(memory_space=pltpu.SMEM)] + whole(2),
        out_specs=whole(2),
        compiler_params=params(),
        cost_estimate=cost(4 * pair.size * width, 4 * pair.size, pair.size),
        name="project",
    )(where, pair, weight)


def channel_major(pieces, left):
    half, chans, lanes = pieces[0].shape
    width = lanes // 3
    main, rest = [], []
    for piece in pieces:
        tail = piece[:, :, 2 * width :]
        turned = jnp.concatenate([tail[:, :, width // 2 :], tail[:, :, : width // 2]], axis=2)
        main += [piece[:, :, :width], piece[:, :, width : 2 * width]]
        rest += [tail, turned]
        if left:
            gap = jnp.zeros((padded(2 * half, 16) - 2 * half, chans, width), BF16)
            main.append(gap)
            rest.append(gap)
    rest = jnp.concatenate(rest, axis=0)
    if left:
        low = lax.broadcasted_iota(jnp.int32, rest.shape, 2) < width // 2
        rest = jnp.where(low, rest, jnp.zeros_like(rest))
    main = jnp.swapaxes(jnp.concatenate(main, axis=0), 0, 1)
    return main, jnp.swapaxes(rest, 0, 1)


def left_kernel(own_ref, beside_ref, out_ref):
    width = own_ref.shape[2] // 3
    main, rest = channel_major([own_ref[...], beside_ref[...]], True)
    out_ref[:, :, :width] = main
    out_ref[:, :, width:] = rest


def left_major(own, beside):
    half, chans, lanes = own.shape
    rows, deep = 2 * padded(2 * half, 16), lanes // 3 * 2
    piece = pl.BlockSpec((half, CHUNK, lanes), lambda c: (0, c, 0))
    return pl.pallas_call(
        left_kernel,
        grid=(chans // CHUNK,),
        out_shape=jax.ShapeDtypeStruct((chans, rows, deep), BF16),
        in_specs=[piece, piece],
        out_specs=pl.BlockSpec((CHUNK, rows, deep), lambda c: (c, 0, 0)),
        compiler_params=params(),
        cost_estimate=cost(0, 8 * own.size),
        name="left_major",
    )(own, beside)


def triangle_kernel(flag_ref, left_ref, *refs, guests, options):
    guest_refs = refs[:guests]
    rights = refs[guests : guests + 2 * options]
    outs = refs[guests + 2 * options : -1 - bool(guests)]
    right_ref = refs[-1]
    own, beside = rights[0][...], rights[1][...]
    if options == 2:
        plain = flag_ref[1] == 0
        own = jnp.where(plain, own, rights[2][...])
        beside = jnp.where(plain, beside, rights[3][...])
    width = own.shape[2] // 3
    even = flag_ref[0] == 0
    main, rest = channel_major(
        [jnp.where(even, own, beside), jnp.where(even, beside, own)], False
    )
    rows = main.shape[1]

    @pl.when(pl.program_id(0) == 0)
    def _():
        right_ref[...] = jnp.zeros_like(right_ref)

    right_ref[:, :rows, :width] = main
    right_ref[:, :rows, width:] = rest
    if guests:
        guest_ref = refs[-2]
        main, rest = channel_major([ref[...] for ref in guest_refs], True)
        guest_ref[:, :, :width] = main
        guest_ref[:, :, width:] = rest

    def product(rows):
        dims = (((1,), (1,)), ((), ()))
        return lax.dot_general(rows, right_ref[c], dims, preferred_element_type=F32).astype(BF16)

    for c in range(CHUNK):
        outs[0][c] = product(left_ref[c])
        if guests:
            lent = product(guest_ref[c])
            part = lent.shape[0] // guests
            for g in range(guests):
                outs[1 + g][c] = lent[g * part : (g + 1) * part]


def triangle(flags, left, pieces, guests=()):
    half, chans, lanes = pieces[0].shape
    options = len(pieces) // 2
    rows, cols, deep = left.shape[1], padded(4 * half, 128), lanes // 3 * 2

    def piece(option):
        if options == 1:
            return pl.BlockSpec((half, CHUNK, lanes), lambda c, flag_ref: (0, c, 0))
        return pl.BlockSpec(
            (half, CHUNK, lanes), lambda c, flag_ref: (0, jnp.where(flag_ref[1] == option, c, 0), 0)
        )

    def block(height, depth):
        return pl.BlockSpec((CHUNK, height, depth), lambda c, flag_ref: (c, 0, 0))

    every = pl.BlockSpec((half, CHUNK, lanes), lambda c, flag_ref: (0, c, 0))
    heights = [rows] + [rows // 2] * len(guests)
    work = [VMEM((CHUNK, rows, deep), BF16)] if guests else []
    return pl.pallas_call(
        functools.partial(triangle_kernel, guests=len(guests), options=options),
        grid_spec=pltpu.PrefetchScalarGridSpec(
            num_scalar_prefetch=1,
            grid=(chans // CHUNK,),
            in_specs=[block(rows, deep)]
            + [every] * len(guests)
            + [piece(i // 2) for i in range(len(pieces))],
            out_specs=[block(h, cols) for h in heights],
            scratch_shapes=work + [VMEM((CHUNK, cols, deep), BF16)],
        ),
        out_shape=[jax.ShapeDtypeStruct((chans, h, cols), BF16) for h in heights],
        compiler_params=params(),
        cost_estimate=cost(2 * chans * sum(heights) * cols * deep, 10 * pieces[0].size),
        name="triangle",
    )(flags, left, *guests, *pieces)


def fold_kernel(role_ref, *refs, outputs, half):
    outs, work_ref = refs[-1 - outputs : -1], refs[-1]
    cols = outs[0].shape[1]
    parts = refs[: -1 - outputs]
    c = pl.program_id(0)
    options = len(parts) // 2
    for option in range(options):

        @pl.when((options == 1) | (role_ref[0] == option))
        def _(option=option):
            total = parts[2 * option][...].astype(F32) + parts[2 * option + 1][...].astype(F32)
            at = pl.ds(pl.multiple_of(c * CHUNK, CHUNK), CHUNK)
            work_ref[:, at, :] = jnp.swapaxes(total.astype(BF16), 0, 1)

    @pl.when(c == pl.num_programs(0) - 1)
    def _():
        pitch = work_ref.shape[0] // outputs
        for o, out_ref in enumerate(outs):

            def turn(r, carry, o=o, out_ref=out_ref):
                at = o * pitch + r
                stacked = jnp.concatenate([work_ref[at], work_ref[at + half]], axis=0)
                out_ref[r] = stacked.T[:cols]
                return carry

            lax.fori_loop(0, half, turn, 0, unroll=True)


def fold(half, role, *parts):
    chans, rows, cols = parts[0].shape
    outputs = rows // padded(2 * half, 16)
    out = jax.ShapeDtypeStruct((half, padded(4 * half, 16), 2 * chans), BF16)

    def block(option):
        return pl.BlockSpec(
            (CHUNK, rows, cols),
            lambda c, role_ref: (
                c if len(parts) == 2 else jnp.where(role_ref[0] == option, c, 0), 0, 0
            ),
        )

    return pl.pallas_call(
        functools.partial(fold_kernel, outputs=outputs, half=half),
        grid_spec=pltpu.PrefetchScalarGridSpec(
            num_scalar_prefetch=1,
            grid=(chans // CHUNK,),
            in_specs=[block(i // 2) for i in range(len(parts))],
            out_specs=[pl.BlockSpec(out.shape, lambda c, role_ref: (0, 0, 0))] * outputs,
            scratch_shapes=[VMEM((rows, chans, cols), BF16)],
        ),
        out_shape=[out] * outputs,
        compiler_params=params(),
        cost_estimate=cost(0, 6 * parts[0].size),
        name="fold",
    )(role, *parts)


def finish_kernel(flag_ref, pair_ref, own_ref, other_ref, *refs):
    gate_ref, out_w_ref, in_ref, back_ref = refs[:4]
    earlier_ref, out_ref = refs[4] if len(refs) == 6 else None, refs[-1]
    _, half, cols, width = pair_ref.shape
    block, chans = cols // 2, width // 2
    hidden_units = back_ref.shape[1]
    front = flag_ref[0] == 0
    steps = (half + 1) // 2

    def step(i, carry):
        first = jnp.minimum(2 * i, half - 2)
        rows = [(h, first + e) for h in range(2) for e in range(2)]
        turned = [[ref[first + e].T[:, :block] for ref in (own_ref, other_ref)] for e in range(2)]
        tri = [
            jnp.concatenate([t[h * chans : (h + 1) * chans] for t in turned[e]], axis=0)
            for h in range(2)
            for e in range(2)
        ]
        tri_normed = norm_chans(jnp.concatenate(tri, axis=1).astype(F32)).astype(BF16)
        pair = []
        for h, r in rows:
            row = pair_ref[h, r].astype(F32)
            pair.append(jnp.where(front, row[:block], row[block:]))
        pair = jnp.concatenate(pair, axis=0).T
        normed = norm_chans(pair).astype(BF16)
        out_gate = twice_sigmoid(jnp.dot(gate_ref[...], normed, preferred_element_type=F32))
        update = jnp.dot(out_w_ref[...], tri_normed, preferred_element_type=F32)
        updated = pair + out_gate * update
        trans_normed = norm_chans(updated).astype(BF16)
        expanded = jnp.dot(in_ref[...], trans_normed, preferred_element_type=F32)
        swish, linear = expanded[:hidden_units], expanded[hidden_units:]
        hidden = (swish * twice_sigmoid(swish) * linear).astype(BF16)
        result = updated + jnp.dot(back_ref[...], hidden, preferred_element_type=F32)
        result = result.T
        for s, (h, r) in enumerate(rows):
            mine = result[s * block : (s + 1) * block]
            if earlier_ref is None:
                out_ref[h, r, :block] = mine.astype(BF16)
            else:
                past = earlier_ref[h, r].astype(F32)[:block]
                parts = [jnp.where(front, mine, past), jnp.where(front, past, mine)]
                out_ref[h, r] = jnp.concatenate(parts, axis=0).astype(BF16)
        return carry

    lax.fori_loop(0, steps, step, 0, unroll=4)


def finish(flag, pair, own, other, weights, earlier=None):
    _, half, cols, width = pair.shape
    shape = pair.shape if earlier is not None else (2, half, padded(cols // 2, 16), width)
    extra = [] if earlier is None else [earlier]
    return pl.pallas_call(
        finish_kernel,
        out_shape=jax.ShapeDtypeStruct(shape, BF16),
        in_specs=[pl.BlockSpec(memory_space=pltpu.SMEM)] + whole(7 + len(extra)),
        out_specs=pl.BlockSpec(memory_space=VMEM),
        compiler_params=params(),
        cost_estimate=cost(14 * pair.size * width, 4 * pair.size, 3 * pair.size),
        name="finish",
    )(flag, pair, own, other, *weights, *extra)


def layer_norm(values):
    centered = values - jnp.mean(values, axis=-1, keepdims=True)
    variance = jnp.mean(centered * centered, axis=-1, keepdims=True)
    return centered * lax.rsqrt(variance + 1e-05)


def any_mesh(pair, chain_lengths, in_weight, out_weight, trans_in, trans_out):
    tile_rows, tile_cols, width = pair.shape
    hidden_units = trans_out.shape[0]
    row_count = lax.axis_size("row")
    col_count = lax.axis_size("col")
    outer = row_count // 2
    tokens = tile_rows * row_count
    valid_count = tokens - chain_lengths[chain_lengths.shape[0] - 1]
    row_id = lax.axis_index("row")
    col_id = lax.axis_index("col")
    line_id = row_id // 2

    def along_line(value, step, targets):
        perm = [(2 * (t - step) + b, 2 * t + b) for t in targets for b in range(2)]
        return lax.ppermute(value, "row", perm)

    row_pos = row_id * tile_rows + jnp.arange(tile_rows, dtype=jnp.int32)
    col_pos = col_id * tile_cols + jnp.arange(tile_cols, dtype=jnp.int32)
    pair_mask = ((row_pos < valid_count)[:, None] & (col_pos < valid_count)[None, :]).astype(
        jnp.float32
    )[:, :, None]
    normed = layer_norm(pair.astype(jnp.float32)).astype(jnp.bfloat16).reshape(-1, width)

    def gated(offset):
        block = jnp.dot(
            normed,
            in_weight[:, offset * width : (offset + 2) * width],
            preferred_element_type=jnp.float32,
        ).reshape(tile_rows, tile_cols, 2 * width)
        value = jax.nn.sigmoid(block[..., :width]) * block[..., width:] * pair_mask
        return value.astype(jnp.bfloat16)

    right_ops = gated(2)
    from_left, from_right = {0: right_ops}, {0: right_ops}
    for step in range(1, outer):
        from_left[step] = along_line(from_left[step - 1], 1, range(step, outer))
        from_right[step] = along_line(from_right[step - 1], -1, range(0, outer - step))
    left_ops = gated(0)
    left_other = lax.ppermute(left_ops, "row", [(i, i ^ 1) for i in range(row_count)])
    lefts = jnp.concatenate([left_ops, left_other], axis=0)

    partials = []
    for source in range(outer):
        block = right_ops
        for step in range(1, outer):
            if source + step < outer:
                block = jnp.where(line_id == source + step, from_left[step], block)
            if source - step >= 0:
                block = jnp.where(line_id == source - step, from_right[step], block)
        partials.append(
            jnp.einsum("ikc,jkc->ijc", lefts, block, preferred_element_type=jnp.float32)
        )
    partial = jnp.stack(partials)
    share = outer // col_count
    mine = lax.dynamic_slice_in_dim(partial, col_id * share, share, 0)
    for hop in range(1, col_count):
        target = (col_id + hop) % col_count
        passed = lax.dynamic_slice_in_dim(partial, target * share, share, 0)
        mine = mine + lax.ppermute(
            passed, "col", [(c, (c + hop) % col_count) for c in range(col_count)]
        )
    tri_normed = layer_norm(mine).astype(jnp.bfloat16)
    own_part = tri_normed[:, :tile_rows]
    other_part = lax.ppermute(
        tri_normed[:, tile_rows:], "row", [(i, i ^ 1) for i in range(row_count)]
    )
    even = row_id % 2 == 0
    both = jnp.stack(
        [jnp.where(even, own_part, other_part), jnp.where(even, other_part, own_part)], axis=1
    )
    tri_normed = both.transpose(2, 0, 1, 3, 4).reshape(-1, width)

    out_gate = jax.nn.sigmoid(
        jnp.dot(normed, in_weight[:, 4 * width :], preferred_element_type=jnp.float32)
    )
    update = jnp.dot(tri_normed, out_weight, preferred_element_type=jnp.float32)
    updated = pair.astype(jnp.float32).reshape(-1, width) + out_gate * update
    trans_normed = layer_norm(updated).astype(jnp.bfloat16)
    expanded = jnp.dot(trans_normed, trans_in, preferred_element_type=jnp.float32)
    hidden = (jax.nn.silu(expanded[:, :hidden_units]) * expanded[:, hidden_units:]).astype(
        jnp.bfloat16
    )
    result = updated + jnp.dot(hidden, trans_out, preferred_element_type=jnp.float32)
    return result.reshape(tile_rows, tile_cols, width).astype(jnp.bfloat16)


def per_device(pair, chain_lengths, in_weight, out_weight, trans_in, trans_out):
    if (lax.axis_size("row"), lax.axis_size("col")) != (8, 2):
        return any_mesh(pair, chain_lengths, in_weight, out_weight, trans_in, trans_out)
    return two_by_four(pair, chain_lengths, in_weight, out_weight, trans_in, trans_out)


def two_by_four(pair, chain_lengths, in_weight, out_weight, trans_in, trans_out):
    tile_rows, tile_cols, width = pair.shape
    half = tile_rows // 2
    tokens = tile_rows * lax.axis_size("row")
    valid_count = tokens - chain_lengths[chain_lengths.shape[0] - 1]
    row_id, core = lax.axis_index("row"), lax.axis_index("col")
    place, side = row_id // 2, row_id % 2
    keeper = place // 2

    def among(value, moves):
        return lax.ppermute(value, "row", [(2 * s + b, 2 * t + b) for s, t in moves for b in range(2)])

    def across(value):
        return lax.ppermute(value, "row", [(i, i ^ 1) for i in range(8)])

    def to_core(value, places, keep):
        perm = []
        for z, towards in zip(places, keep):
            target = z // 2 if towards else 1 - z // 2
            perm += [(4 * z + 2 * b + 1 - target, 4 * z + 2 * b + target) for b in range(2)]
        return lax.ppermute(value, ("row", "col"), perm)

    def give_back(value, swap):
        perm = []
        for s, t in ((1, 0), (2, 3)):
            away = 1 - t // 2
            source = 1 - away if swap else away
            perm += [(4 * s + 2 * b + source, 4 * t + 2 * (b ^ swap) + away) for b in range(2)]
        return lax.ppermute(value, ("row", "col"), perm)

    def late_across(value):
        perm = []
        for z in range(4):
            holder = 1 - z // 2 if z in (1, 2) else z // 2
            perm += [(4 * z + 2 * b + holder, 4 * z + 2 * (1 - b) + holder) for b in range(2)]
        return lax.ppermute(value, ("row", "col"), perm)

    def by_side(block, axis):
        return jnp.where(side == 0, block, jnp.roll(block, width // 2, axis))

    def gate_pair(first):
        parts = [
            by_side(in_weight[:, (first + i) * width : (first + i + 1) * width], 1) for i in range(2)
        ]
        return jnp.concatenate(parts, axis=1).T * BF16(0.5)

    def after(value, *others):
        return lax.optimization_barrier((value, *others))[0]

    def scalars(*values):
        return jnp.stack([jnp.asarray(v).astype(jnp.int32) for v in values])

    is_keeper = core == keeper
    inner = (place == 1) | (place == 2)
    where = scalars(valid_count, row_id * tile_rows, core * tile_cols)
    folded = pair.reshape(2, half, tile_cols, width)
    cross = [(1, 2), (2, 1)]
    everyone, inners = range(4), (1, 2)

    def phase(moves, finished):
        values = lax.optimization_barrier(tuple(v for _, v in moves) + tuple(finished))
        return [send(v) for (send, _), v in zip(moves, values)]

    def hop(moves):
        return lambda value: among(value, moves)

    def either(at_inner, at_end):
        return jnp.where(inner, at_inner, at_end)

    swap = hop([(0, 1), (1, 0), (2, 3), (3, 2)])
    right_own, right_far = project(where, folded, gate_pair(2))
    one = phase([(swap, right_own), (hop(cross), right_own), (across, right_far)], ())
    mate_own, near_own, right_beside = one
    left_own, left_far = project(where, folded, gate_pair(0))
    two = phase(
        [(swap, either(near_own, right_beside)), (hop(cross), right_beside), (across, left_far)], one
    )
    mate_beside, near_beside, left_beside = two
    three = phase([(swap, either(near_beside, left_own)), (hop(cross), mate_own)], two)
    guest_own, far_own = three

    left = left_major(left_own, left_beside)
    plain, outer = scalars(side, 0), scalars(side, jnp.where(inner, 0, 1))
    (home,) = triangle(plain, left, [right_own, right_beside])
    home_rest = to_core(home, everyone, [True] * 4)
    (mate,) = triangle(plain, left, [mate_own, mate_beside])
    mate_rest = to_core(mate, inners, [True] * 2)
    four = phase(
        [(swap, either(right_beside, left_beside)), (hop(cross), mate_beside)], three + [home, mate]
    )
    (away,) = triangle(
        outer, left, [after(near_own, far_own, mate), near_beside, mate_beside, guest_own]
    )
    guest_beside, far_beside = four
    away_rest = to_core(away, everyone, [False] * 4)
    role = scalars(jnp.where(is_keeper, 0, 1))
    first = fold(half, role, home, home_rest, away, away_rest)
    first_other = across(first[1])
    mate_block = fold(half, role, mate, mate_rest)
    mate_other = across(mate_block[1])

    late, lent_own, lent_beside = triangle(
        outer,
        left,
        [after(far_own, first_other, mate_other), far_beside, mate_own, guest_beside],
        [guest_own, guest_beside],
    )
    lent_rest = to_core(lent_own, inners, [False] * 2), to_core(lent_beside, inners, [True] * 2)
    late_rest = to_core(late, everyone, [True, False, False, True])
    (lent,) = fold(half, role, lent_beside, lent_rest[1], lent_own, lent_rest[0])
    given = give_back(lent, 0), give_back(lent, 1)
    late_block = fold(half, role, late, late_rest)
    late_other = late_across(late_block[1])

    order = jnp.where(is_keeper, place % 2, place // 2)
    weights = [
        in_weight[:, 4 * width :].T * BF16(0.5),
        by_side(out_weight, 0).T * BF16(0.5),
        jnp.where(jnp.arange(trans_in.shape[1])[:, None] < trans_out.shape[0], BF16(0.5), BF16(1.0))
        * trans_in.T,
        trans_out.T,
    ]
    earlier = finish(scalars(order), folded, after(first[0], lent), first_other, weights)
    own, other = (
        jnp.where(inner & is_keeper, early, jnp.where(inner | is_keeper, end, back))
        for early, end, back in zip((mate_block[0], mate_other), (late_block[0], late_other), given)
    )
    result = finish(scalars(1 - order), folded, own, other, weights, earlier)
    return result.reshape(tile_rows, tile_cols, width)


def solution(mesh):
    placed = (P(("crops", "row"), "col", None), P("crops"), P(), P(), P(), P())
    return jax.shard_map(
        per_device,
        mesh=mesh,
        in_specs=placed,
        out_specs=P(("crops", "row"), "col", None),
        check_vma=False,
    )
```

```python
import functools

import jax
import jax.numpy as jnp
from jax import lax
from jax.experimental import pallas as pl
from jax.experimental.pallas import tpu as pltpu
from jax.sharding import PartitionSpec as P

VMEM = pltpu.VMEM
BF16, F32 = jnp.bfloat16, jnp.float32
CHUNK = 16


def whole(count):
    return [pl.BlockSpec(memory_space=VMEM)] * count


def params():
    return pltpu.CompilerParams(vmem_limit_bytes=48 << 20)


def cost(flops, moved, transcendentals=0):
    return pl.CostEstimate(flops=flops, bytes_accessed=moved, transcendentals=transcendentals)


def twice_sigmoid(halved):
    return jnp.tanh(halved) + 1.0


def norm_chans(values):
    centered = values - jnp.mean(values, axis=0, keepdims=True)
    variance = jnp.mean(centered * centered, axis=0, keepdims=True)
    return centered * lax.rsqrt(variance + 1e-05)


def padded(count, unit):
    return -(-count // unit) * unit


def project_kernel(where_ref, pair_ref, weight_ref, own_ref, far_ref):
    valid, row0, col0 = where_ref[0], where_ref[1], where_ref[2]
    _, half, cols, width = pair_ref.shape
    chans = width // 2
    tail = cols - width
    lane = lax.broadcasted_iota(jnp.int32, (1, 3 * width), 1)
    in_tail = lane >= 2 * width
    ends = jnp.where(in_tail, 2 * width + chans, width)
    is_first = jnp.where(lane < ends, 1, 0)
    token = jnp.where(in_tail, lane % chans + width, lane % width) + col0
    gap = jnp.zeros((chans - tail, width), F32)

    def step(r, carry):
        first, second = (pair_ref[h, r].astype(F32) for h in range(2))
        tokens = jnp.concatenate(
            [first[:width], second[:width], first[width:], gap, second[width:], gap], axis=0
        )
        normed = norm_chans(tokens.T).astype(BF16)
        both = jnp.dot(weight_ref[...], normed, preferred_element_type=F32)
        limits = [jnp.where(row0 + h * half + r < valid, valid, 0) for h in range(2)]
        keep = jnp.where(token < limits[1] + is_first * (limits[0] - limits[1]), 1.0, 0.0)
        out = (twice_sigmoid(both[:width]) * both[width:] * keep).astype(BF16)
        own_ref[r] = out[:chans]
        far_ref[r] = out[chans:]
        return carry

    lax.fori_loop(0, half, step, 0, unroll=4)


def project(where, pair, weight):
    _, half, cols, width = pair.shape
    piece = jax.ShapeDtypeStruct((half, width // 2, 3 * width), BF16)
    return pl.pallas_call(
        project_kernel,
        out_shape=(piece, piece),
        in_specs=[pl.BlockSpec(memory_space=pltpu.SMEM)] + whole(2),
        out_specs=whole(2),
        compiler_params=params(),
        cost_estimate=cost(4 * pair.size * width, 4 * pair.size, pair.size),
        name="project",
    )(where, pair, weight)


def channel_major(pieces, left):
    half, chans, lanes = pieces[0].shape
    width = lanes // 3
    main, rest = [], []
    for piece in pieces:
        tail = piece[:, :, 2 * width :]
        turned = jnp.concatenate([tail[:, :, width // 2 :], tail[:, :, : width // 2]], axis=2)
        main += [piece[:, :, :width], piece[:, :, width : 2 * width]]
        rest += [tail, turned]
        if left:
            gap = jnp.zeros((padded(2 * half, 16) - 2 * half, chans, width), BF16)
            main.append(gap)
            rest.append(gap)
    rest = jnp.concatenate(rest, axis=0)
    if left:
        low = lax.broadcasted_iota(jnp.int32, rest.shape, 2) < width // 2
        rest = jnp.where(low, rest, jnp.zeros_like(rest))
    main = jnp.swapaxes(jnp.concatenate(main, axis=0), 0, 1)
    return main, jnp.swapaxes(rest, 0, 1)


def left_kernel(own_ref, beside_ref, out_ref):
    width = own_ref.shape[2] // 3
    main, rest = channel_major([own_ref[...], beside_ref[...]], True)
    out_ref[:, :, :width] = main
    out_ref[:, :, width:] = rest


def left_major(own, beside):
    half, chans, lanes = own.shape
    rows, deep = 2 * padded(2 * half, 16), lanes // 3 * 2
    piece = pl.BlockSpec((half, CHUNK, lanes), lambda c: (0, c, 0))
    return pl.pallas_call(
        left_kernel,
        grid=(chans // CHUNK,),
        out_shape=jax.ShapeDtypeStruct((chans, rows, deep), BF16),
        in_specs=[piece, piece],
        out_specs=pl.BlockSpec((CHUNK, rows, deep), lambda c: (c, 0, 0)),
        compiler_params=params(),
        cost_estimate=cost(0, 8 * own.size),
        name="left_major",
    )(own, beside)


def triangle_kernel(flag_ref, left_ref, *refs, guests, options):
    guest_refs = refs[:guests]
    rights = refs[guests : guests + 2 * options]
    outs = refs[guests + 2 * options : -1 - bool(guests)]
    right_ref = refs[-1]
    own, beside = rights[0][...], rights[1][...]
    if options == 2:
        plain = flag_ref[1] == 0
        own = jnp.where(plain, own, rights[2][...])
        beside = jnp.where(plain, beside, rights[3][...])
    width = own.shape[2] // 3
    even = flag_ref[0] == 0
    main, rest = channel_major(
        [jnp.where(even, own, beside), jnp.where(even, beside, own)], False
    )
    rows = main.shape[1]

    @pl.when(pl.program_id(0) == 0)
    def _():
        right_ref[...] = jnp.zeros_like(right_ref)

    right_ref[:, :rows, :width] = main
    right_ref[:, :rows, width:] = rest
    if guests:
        guest_ref = refs[-2]
        main, rest = channel_major([ref[...] for ref in guest_refs], True)
        guest_ref[:, :, :width] = main
        guest_ref[:, :, width:] = rest

    def product(rows):
        dims = (((1,), (1,)), ((), ()))
        return lax.dot_general(rows, right_ref[c], dims, preferred_element_type=F32).astype(BF16)

    for c in range(CHUNK):
        outs[0][c] = product(left_ref[c])
        if guests:
            lent = product(guest_ref[c])
            part = lent.shape[0] // guests
            for g in range(guests):
                outs[1 + g][c] = lent[g * part : (g + 1) * part]


def triangle(flags, left, pieces, guests=()):
    half, chans, lanes = pieces[0].shape
    options = len(pieces) // 2
    rows, cols, deep = left.shape[1], padded(4 * half, 128), lanes // 3 * 2

    def piece(option):
        if options == 1:
            return pl.BlockSpec((half, CHUNK, lanes), lambda c, flag_ref: (0, c, 0))
        return pl.BlockSpec(
            (half, CHUNK, lanes), lambda c, flag_ref: (0, jnp.where(flag_ref[1] == option, c, 0), 0)
        )

    def block(height, depth):
        return pl.BlockSpec((CHUNK, height, depth), lambda c, flag_ref: (c, 0, 0))

    every = pl.BlockSpec((half, CHUNK, lanes), lambda c, flag_ref: (0, c, 0))
    heights = [rows] + [rows // 2] * len(guests)
    work = [VMEM((CHUNK, rows, deep), BF16)] if guests else []
    return pl.pallas_call(
        functools.partial(triangle_kernel, guests=len(guests), options=options),
        grid_spec=pltpu.PrefetchScalarGridSpec(
            num_scalar_prefetch=1,
            grid=(chans // CHUNK,),
            in_specs=[block(rows, deep)]
            + [every] * len(guests)
            + [piece(i // 2) for i in range(len(pieces))],
            out_specs=[block(h, cols) for h in heights],
            scratch_shapes=work + [VMEM((CHUNK, cols, deep), BF16)],
        ),
        out_shape=[jax.ShapeDtypeStruct((chans, h, cols), BF16) for h in heights],
        compiler_params=params(),
        cost_estimate=cost(2 * chans * sum(heights) * cols * deep, 10 * pieces[0].size),
        name="triangle",
    )(flags, left, *guests, *pieces)


def fold_kernel(role_ref, *refs, outputs, half):
    outs, work_ref = refs[-1 - outputs : -1], refs[-1]
    cols = outs[0].shape[1]
    parts = refs[: -1 - outputs]
    c = pl.program_id(0)
    options = len(parts) // 2
    for option in range(options):

        @pl.when((options == 1) | (role_ref[0] == option))
        def _(option=option):
            total = parts[2 * option][...].astype(F32) + parts[2 * option + 1][...].astype(F32)
            at = pl.ds(pl.multiple_of(c * CHUNK, CHUNK), CHUNK)
            work_ref[:, at, :] = jnp.swapaxes(total.astype(BF16), 0, 1)

    @pl.when(c == pl.num_programs(0) - 1)
    def _():
        pitch = work_ref.shape[0] // outputs
        for o, out_ref in enumerate(outs):

            def turn(r, carry, o=o, out_ref=out_ref):
                at = o * pitch + r
                stacked = jnp.concatenate([work_ref[at], work_ref[at + half]], axis=0)
                out_ref[r] = stacked.T[:cols]
                return carry

            lax.fori_loop(0, half, turn, 0, unroll=True)


def fold(half, role, *parts):
    chans, rows, cols = parts[0].shape
    outputs = rows // padded(2 * half, 16)
    out = jax.ShapeDtypeStruct((half, padded(4 * half, 16), 2 * chans), BF16)

    def block(option):
        return pl.BlockSpec(
            (CHUNK, rows, cols),
            lambda c, role_ref: (
                c if len(parts) == 2 else jnp.where(role_ref[0] == option, c, 0), 0, 0
            ),
        )

    return pl.pallas_call(
        functools.partial(fold_kernel, outputs=outputs, half=half),
        grid_spec=pltpu.PrefetchScalarGridSpec(
            num_scalar_prefetch=1,
            grid=(chans // CHUNK,),
            in_specs=[block(i // 2) for i in range(len(parts))],
            out_specs=[pl.BlockSpec(out.shape, lambda c, role_ref: (0, 0, 0))] * outputs,
            scratch_shapes=[VMEM((rows, chans, cols), BF16)],
        ),
        out_shape=[out] * outputs,
        compiler_params=params(),
        cost_estimate=cost(0, 6 * parts[0].size),
        name="fold",
    )(role, *parts)


def finish_kernel(flag_ref, pair_ref, own_ref, other_ref, *refs):
    gate_ref, out_w_ref, in_ref, back_ref = refs[:4]
    earlier_ref, out_ref = refs[4] if len(refs) == 6 else None, refs[-1]
    _, half, cols, width = pair_ref.shape
    block, chans = cols // 2, width // 2
    hidden_units = back_ref.shape[1]
    front = flag_ref[0] == 0
    steps = (half + 1) // 2

    def step(i, carry):
        first = jnp.minimum(2 * i, half - 2)
        rows = [(h, first + e) for h in range(2) for e in range(2)]
        turned = [[ref[first + e].T[:, :block] for ref in (own_ref, other_ref)] for e in range(2)]
        tri = [
            jnp.concatenate([t[h * chans : (h + 1) * chans] for t in turned[e]], axis=0)
            for h in range(2)
            for e in range(2)
        ]
        tri_normed = norm_chans(jnp.concatenate(tri, axis=1).astype(F32)).astype(BF16)
        pair = []
        for h, r in rows:
            row = pair_ref[h, r].astype(F32)
            pair.append(jnp.where(front, row[:block], row[block:]))
        pair = jnp.concatenate(pair, axis=0).T
        normed = norm_chans(pair).astype(BF16)
        out_gate = twice_sigmoid(jnp.dot(gate_ref[...], normed, preferred_element_type=F32))
        update = jnp.dot(out_w_ref[...], tri_normed, preferred_element_type=F32)
        updated = pair + out_gate * update
        trans_normed = norm_chans(updated).astype(BF16)
        expanded = jnp.dot(in_ref[...], trans_normed, preferred_element_type=F32)
        swish, linear = expanded[:hidden_units], expanded[hidden_units:]
        hidden = (swish * twice_sigmoid(swish) * linear).astype(BF16)
        result = updated + jnp.dot(back_ref[...], hidden, preferred_element_type=F32)
        result = result.T
        for s, (h, r) in enumerate(rows):
            mine = result[s * block : (s + 1) * block]
            if earlier_ref is None:
                out_ref[h, r, :block] = mine.astype(BF16)
            else:
                past = earlier_ref[h, r].astype(F32)[:block]
                parts = [jnp.where(front, mine, past), jnp.where(front, past, mine)]
                out_ref[h, r] = jnp.concatenate(parts, axis=0).astype(BF16)
        return carry

    lax.fori_loop(0, steps, step, 0, unroll=4)


def finish(flag, pair, own, other, weights, earlier=None):
    _, half, cols, width = pair.shape
    shape = pair.shape if earlier is not None else (2, half, padded(cols // 2, 16), width)
    extra = [] if earlier is None else [earlier]
    return pl.pallas_call(
        finish_kernel,
        out_shape=jax.ShapeDtypeStruct(shape, BF16),
        in_specs=[pl.BlockSpec(memory_space=pltpu.SMEM)] + whole(7 + len(extra)),
        out_specs=pl.BlockSpec(memory_space=VMEM),
        compiler_params=params(),
        cost_estimate=cost(14 * pair.size * width, 4 * pair.size, 3 * pair.size),
        name="finish",
    )(flag, pair, own, other, *weights, *extra)


def layer_norm(values):
    centered = values - jnp.mean(values, axis=-1, keepdims=True)
    variance = jnp.mean(centered * centered, axis=-1, keepdims=True)
    return centered * lax.rsqrt(variance + 1e-05)


def any_mesh(pair, chain_lengths, in_weight, out_weight, trans_in, trans_out):
    tile_rows, tile_cols, width = pair.shape
    hidden_units = trans_out.shape[0]
    row_count = lax.axis_size("row")
    col_count = lax.axis_size("col")
    outer = row_count // 2
    tokens = tile_rows * row_count
    valid_count = tokens - chain_lengths[chain_lengths.shape[0] - 1]
    row_id = lax.axis_index("row")
    col_id = lax.axis_index("col")
    line_id = row_id // 2

    def along_line(value, step, targets):
        perm = [(2 * (t - step) + b, 2 * t + b) for t in targets for b in range(2)]
        return lax.ppermute(value, "row", perm)

    row_pos = row_id * tile_rows + jnp.arange(tile_rows, dtype=jnp.int32)
    col_pos = col_id * tile_cols + jnp.arange(tile_cols, dtype=jnp.int32)
    pair_mask = ((row_pos < valid_count)[:, None] & (col_pos < valid_count)[None, :]).astype(
        jnp.float32
    )[:, :, None]
    normed = layer_norm(pair.astype(jnp.float32)).astype(jnp.bfloat16).reshape(-1, width)

    def gated(offset):
        block = jnp.dot(
            normed,
            in_weight[:, offset * width : (offset + 2) * width],
            preferred_element_type=jnp.float32,
        ).reshape(tile_rows, tile_cols, 2 * width)
        value = jax.nn.sigmoid(block[..., :width]) * block[..., width:] * pair_mask
        return value.astype(jnp.bfloat16)

    right_ops = gated(2)
    from_left, from_right = {0: right_ops}, {0: right_ops}
    for step in range(1, outer):
        from_left[step] = along_line(from_left[step - 1], 1, range(step, outer))
        from_right[step] = along_line(from_right[step - 1], -1, range(0, outer - step))
    left_ops = gated(0)
    left_other = lax.ppermute(left_ops, "row", [(i, i ^ 1) for i in range(row_count)])
    lefts = jnp.concatenate([left_ops, left_other], axis=0)

    partials = []
    for source in range(outer):
        block = right_ops
        for step in range(1, outer):
            if source + step < outer:
                block = jnp.where(line_id == source + step, from_left[step], block)
            if source - step >= 0:
                block = jnp.where(line_id == source - step, from_right[step], block)
        partials.append(
            jnp.einsum("ikc,jkc->ijc", lefts, block, preferred_element_type=jnp.float32)
        )
    partial = jnp.stack(partials)
    share = outer // col_count
    mine = lax.dynamic_slice_in_dim(partial, col_id * share, share, 0)
    for hop in range(1, col_count):
        target = (col_id + hop) % col_count
        passed = lax.dynamic_slice_in_dim(partial, target * share, share, 0)
        mine = mine + lax.ppermute(
            passed, "col", [(c, (c + hop) % col_count) for c in range(col_count)]
        )
    tri_normed = layer_norm(mine).astype(jnp.bfloat16)
    own_part = tri_normed[:, :tile_rows]
    other_part = lax.ppermute(
        tri_normed[:, tile_rows:], "row", [(i, i ^ 1) for i in range(row_count)]
    )
    even = row_id % 2 == 0
    both = jnp.stack(
        [jnp.where(even, own_part, other_part), jnp.where(even, other_part, own_part)], axis=1
    )
    tri_normed = both.transpose(2, 0, 1, 3, 4).reshape(-1, width)

    out_gate = jax.nn.sigmoid(
        jnp.dot(normed, in_weight[:, 4 * width :], preferred_element_type=jnp.float32)
    )
    update = jnp.dot(tri_normed, out_weight, preferred_element_type=jnp.float32)
    updated = pair.astype(jnp.float32).reshape(-1, width) + out_gate * update
    trans_normed = layer_norm(updated).astype(jnp.bfloat16)
    expanded = jnp.dot(trans_normed, trans_in, preferred_element_type=jnp.float32)
    hidden = (jax.nn.silu(expanded[:, :hidden_units]) * expanded[:, hidden_units:]).astype(
        jnp.bfloat16
    )
    result = updated + jnp.dot(hidden, trans_out, preferred_element_type=jnp.float32)
    return result.reshape(tile_rows, tile_cols, width).astype(jnp.bfloat16)


def per_device(pair, chain_lengths, in_weight, out_weight, trans_in, trans_out):
    if (lax.axis_size("row"), lax.axis_size("col")) != (8, 2):
        return any_mesh(pair, chain_lengths, in_weight, out_weight, trans_in, trans_out)
    return two_by_four(pair, chain_lengths, in_weight, out_weight, trans_in, trans_out)


def two_by_four(pair, chain_lengths, in_weight, out_weight, trans_in, trans_out):
    tile_rows, tile_cols, width = pair.shape
    half = tile_rows // 2
    tokens = tile_rows * lax.axis_size("row")
    valid_count = tokens - chain_lengths[chain_lengths.shape[0] - 1]
    row_id, core = lax.axis_index("row"), lax.axis_index("col")
    place, side = row_id // 2, row_id % 2
    keeper = place // 2

    def among(value, moves):
        return lax.ppermute(value, "row", [(2 * s + b, 2 * t + b) for s, t in moves for b in range(2)])

    def across(value):
        return lax.ppermute(value, "row", [(i, i ^ 1) for i in range(8)])

    def to_core(value, places, keep):
        perm = []
        for z, towards in zip(places, keep):
            target = z // 2 if towards else 1 - z // 2
            perm += [(4 * z + 2 * b + 1 - target, 4 * z + 2 * b + target) for b in range(2)]
        return lax.ppermute(value, ("row", "col"), perm)

    def give_back(value, swap):
        perm = []
        for s, t in ((1, 0), (2, 3)):
            away = 1 - t // 2
            source = 1 - away if swap else away
            perm += [(4 * s + 2 * b + source, 4 * t + 2 * (b ^ swap) + away) for b in range(2)]
        return lax.ppermute(value, ("row", "col"), perm)

    def side_to_side(value, places, holders):
        perm = []
        for z, holder in zip(places, holders):
            perm += [(4 * z + 2 * b + holder, 4 * z + 2 * (1 - b) + holder) for b in range(2)]
        return lax.ppermute(value, ("row", "col"), perm)

    def by_side(block, axis):
        return jnp.where(side == 0, block, jnp.roll(block, width // 2, axis))

    def gate_pair(first):
        parts = [
            by_side(in_weight[:, (first + i) * width : (first + i + 1) * width], 1) for i in range(2)
        ]
        return jnp.concatenate(parts, axis=1).T * BF16(0.5)

    def after(value, *others):
        return lax.optimization_barrier((value, *others))[0]

    def scalars(*values):
        return jnp.stack([jnp.asarray(v).astype(jnp.int32) for v in values])

    is_keeper = core == keeper
    inner = (place == 1) | (place == 2)
    where = scalars(valid_count, row_id * tile_rows, core * tile_cols)
    folded = pair.reshape(2, half, tile_cols, width)
    cross = [(1, 2), (2, 1)]
    everyone, inners = range(4), (1, 2)

    def phase(moves, finished):
        values = lax.optimization_barrier(tuple(v for _, v in moves) + tuple(finished))
        return [send(v) for (send, _), v in zip(moves, values)]

    def hop(moves):
        return lambda value: among(value, moves)

    def either(at_inner, at_end):
        return jnp.where(inner, at_inner, at_end)

    swap = hop([(0, 1), (1, 0), (2, 3), (3, 2)])
    right_own, right_far = project(where, folded, gate_pair(2))
    one = phase([(swap, right_own), (hop(cross), right_own), (across, right_far)], ())
    mate_own, near_own, right_beside = one
    left_own, left_far = project(where, folded, gate_pair(0))
    two = phase(
        [(swap, either(near_own, right_beside)), (hop(cross), right_beside), (across, left_far)],
        one,
    )
    mate_beside, near_beside, left_beside = two
    three = phase(
        [(swap, either(near_beside, left_own)), (hop(cross), mate_own)], (near_beside, left_beside)
    )
    guest_own, far_own = three

    left = left_major(left_own, left_beside)
    plain, outer = scalars(side, 0), scalars(side, jnp.where(inner, 0, 1))
    (home,) = triangle(plain, left, [right_own, right_beside])
    home_rest = to_core(home, everyone, [True] * 4)
    (mate,) = triangle(plain, left, [mate_own, mate_beside])
    mate_rest = to_core(mate, inners, [True] * 2)
    four = phase(
        [(swap, either(right_beside, left_beside)), (hop(cross), mate_beside)], three + [home, mate]
    )
    (away,) = triangle(
        outer, left, [after(near_own, far_own, mate), near_beside, mate_beside, guest_own]
    )
    guest_beside, far_beside = four
    away_rest = to_core(away, everyone, [False] * 4)
    role = scalars(jnp.where(is_keeper, 0, 1))
    first = fold(half, role, home, home_rest, away, away_rest)
    first_other = across(first[1])
    mate_block = fold(half, role, mate, mate_rest)
    mate_other = side_to_side(mate_block[1], inners, (0, 1))

    order = jnp.where(is_keeper, place % 2, place // 2)
    weights = [
        in_weight[:, 4 * width :].T * BF16(0.5),
        by_side(out_weight, 0).T * BF16(0.5),
        jnp.where(jnp.arange(trans_in.shape[1])[:, None] < trans_out.shape[0], BF16(0.5), BF16(1.0))
        * trans_in.T,
        trans_out.T,
    ]
    earlier = finish(scalars(order), folded, first[0], first_other, weights)
    late, lent_own, lent_beside = triangle(
        outer,
        left,
        [after(far_own, earlier, mate_other), far_beside, mate_own, guest_beside],
        [guest_own, guest_beside],
    )
    lent_rest = to_core(lent_own, inners, [False] * 2), to_core(lent_beside, inners, [True] * 2)
    late_rest = to_core(late, everyone, [True, False, False, True])
    (lent,) = fold(half, role, lent_beside, lent_rest[1], lent_own, lent_rest[0])
    given = give_back(lent, 0), give_back(lent, 1)
    late_block = fold(half, role, late, late_rest)
    late_other = side_to_side(late_block[1], everyone, (0, 1, 0, 1))

    own, other = (
        jnp.where(inner & is_keeper, early, jnp.where(inner | is_keeper, end, back))
        for early, end, back in zip((mate_block[0], mate_other), (late_block[0], late_other), given)
    )
    result = finish(scalars(1 - order), folded, own, other, weights, earlier)
    return result.reshape(tile_rows, tile_cols, width)


def solution(mesh):
    placed = (P(("crops", "row"), "col", None), P("crops"), P(), P(), P(), P())
    return jax.shard_map(
        per_device,
        mesh=mesh,
        in_specs=placed,
        out_specs=P(("crops", "row"), "col", None),
        check_vma=False,
    )
```

```python
import functools

import jax
import jax.numpy as jnp
from jax import lax
from jax.experimental import pallas as pl
from jax.experimental.pallas import tpu as pltpu
from jax.sharding import PartitionSpec as P

VMEM = pltpu.VMEM
BF16, F32 = jnp.bfloat16, jnp.float32
CHUNK = 16


def whole(count):
    return [pl.BlockSpec(memory_space=VMEM)] * count


def params():
    return pltpu.CompilerParams(vmem_limit_bytes=48 << 20)


def cost(flops, moved, transcendentals=0):
    return pl.CostEstimate(flops=flops, bytes_accessed=moved, transcendentals=transcendentals)


def twice_sigmoid(halved):
    return jnp.tanh(halved) + 1.0


def norm_chans(values):
    centered = values - jnp.mean(values, axis=0, keepdims=True)
    variance = jnp.mean(centered * centered, axis=0, keepdims=True)
    return centered * lax.rsqrt(variance + 1e-05)


def padded(count, unit):
    return -(-count // unit) * unit


def project_kernel(where_ref, pair_ref, weight_ref, own_ref, far_ref):
    valid, row0, col0 = where_ref[0], where_ref[1], where_ref[2]
    _, half, cols, width = pair_ref.shape
    chans = width // 2
    tail = cols - width
    lane = lax.broadcasted_iota(jnp.int32, (1, 3 * width), 1)
    in_tail = lane >= 2 * width
    ends = jnp.where(in_tail, 2 * width + chans, width)
    is_first = jnp.where(lane < ends, 1, 0)
    token = jnp.where(in_tail, lane % chans + width, lane % width) + col0
    gap = jnp.zeros((chans - tail, width), F32)

    def step(r, carry):
        first, second = (pair_ref[h, r].astype(F32) for h in range(2))
        tokens = jnp.concatenate(
            [first[:width], second[:width], first[width:], gap, second[width:], gap], axis=0
        )
        normed = norm_chans(tokens.T).astype(BF16)
        both = jnp.dot(weight_ref[...], normed, preferred_element_type=F32)
        limits = [jnp.where(row0 + h * half + r < valid, valid, 0) for h in range(2)]
        keep = jnp.where(token < limits[1] + is_first * (limits[0] - limits[1]), 1.0, 0.0)
        out = (twice_sigmoid(both[:width]) * both[width:] * keep).astype(BF16)
        own_ref[r] = out[:chans]
        far_ref[r] = out[chans:]
        return carry

    lax.fori_loop(0, half, step, 0, unroll=4)


def project(where, pair, weight):
    _, half, cols, width = pair.shape
    piece = jax.ShapeDtypeStruct((half, width // 2, 3 * width), BF16)
    return pl.pallas_call(
        project_kernel,
        out_shape=(piece, piece),
        in_specs=[pl.BlockSpec(memory_space=pltpu.SMEM)] + whole(2),
        out_specs=whole(2),
        compiler_params=params(),
        cost_estimate=cost(4 * pair.size * width, 4 * pair.size, pair.size),
        name="project",
    )(where, pair, weight)


def channel_major(pieces, left):
    half, chans, lanes = pieces[0].shape
    width = lanes // 3
    main, rest = [], []
    for piece in pieces:
        tail = piece[:, :, 2 * width :]
        turned = jnp.concatenate([tail[:, :, width // 2 :], tail[:, :, : width // 2]], axis=2)
        main += [piece[:, :, :width], piece[:, :, width : 2 * width]]
        rest += [tail, turned]
        if left:
            gap = jnp.zeros((padded(2 * half, 16) - 2 * half, chans, width), BF16)
            main.append(gap)
            rest.append(gap)
    rest = jnp.concatenate(rest, axis=0)
    if left:
        low = lax.broadcasted_iota(jnp.int32, rest.shape, 2) < width // 2
        rest = jnp.where(low, rest, jnp.zeros_like(rest))
    main = jnp.swapaxes(jnp.concatenate(main, axis=0), 0, 1)
    return main, jnp.swapaxes(rest, 0, 1)


def left_kernel(own_ref, beside_ref, out_ref):
    width = own_ref.shape[2] // 3
    main, rest = channel_major([own_ref[...], beside_ref[...]], True)
    out_ref[:, :, :width] = main
    out_ref[:, :, width:] = rest


def left_major(own, beside):
    half, chans, lanes = own.shape
    rows, deep = 2 * padded(2 * half, 16), lanes // 3 * 2
    piece = pl.BlockSpec((half, CHUNK, lanes), lambda c: (0, c, 0))
    return pl.pallas_call(
        left_kernel,
        grid=(chans // CHUNK,),
        out_shape=jax.ShapeDtypeStruct((chans, rows, deep), BF16),
        in_specs=[piece, piece],
        out_specs=pl.BlockSpec((CHUNK, rows, deep), lambda c: (c, 0, 0)),
        compiler_params=params(),
        cost_estimate=cost(0, 8 * own.size),
        name="left_major",
    )(own, beside)


def triangle_kernel(flag_ref, left_ref, *refs, counts, guests, options):
    pieces, refs = [], list(refs)
    for count in counts:
        parts = [refs.pop(0)[...] for _ in range(count)]
        pieces.append(parts[0] if count == 1 else jnp.concatenate(parts, axis=0))
    outs, work = refs[: 1 + guests], refs[1 + guests :]
    visitors, rights = pieces[:guests], pieces[guests:]
    own, beside = rights[:2]
    if options == 2:
        plain = flag_ref[1] == 0
        own = jnp.where(plain, own, rights[2])
        beside = jnp.where(plain, beside, rights[3])
    width = own.shape[2] // 3
    even = flag_ref[0] == 0
    right_ref = work[0]
    main, rest = channel_major(
        [jnp.where(even, own, beside), jnp.where(even, beside, own)], False
    )
    rows = main.shape[1]

    @pl.when(pl.program_id(0) == 0)
    def _():
        right_ref[...] = jnp.zeros_like(right_ref)

    right_ref[:, :rows, :width] = main
    right_ref[:, :rows, width:] = rest
    if guests:
        guest_ref = work[1]
        main, rest = channel_major(visitors, True)
        guest_ref[:, :, :width] = main
        guest_ref[:, :, width:] = rest

    def product(rows):
        dims = (((1,), (1,)), ((), ()))
        return lax.dot_general(rows, right_ref[c], dims, preferred_element_type=F32).astype(BF16)

    for c in range(CHUNK):
        outs[0][c] = product(left_ref[c])
        if guests:
            lent = product(guest_ref[c])
            part = lent.shape[0] // guests
            for g in range(guests):
                outs[1 + g][c] = lent[g * part : (g + 1) * part]


def triangle(flags, left, pieces, guests=()):
    chans, rows, deep = left.shape
    lanes, half = deep // 2 * 3, sum(part.shape[0] for part in pieces[0])
    options, cols = len(pieces) // 2, padded(4 * half, 128)

    def spec(part, option):
        def at(c, flag_ref):
            return (0, c if option is None else jnp.where(flag_ref[1] == option, c, 0), 0)

        return pl.BlockSpec((part.shape[0], CHUNK, lanes), at)

    def block(height, depth):
        return pl.BlockSpec((CHUNK, height, depth), lambda c, flag_ref: (c, 0, 0))

    specs = [spec(part, None) for piece in guests for part in piece]
    for i, piece in enumerate(pieces):
        specs += [spec(part, i // 2 if options == 2 else None) for part in piece]
    heights = [rows] + [rows // 2] * len(guests)
    work = [VMEM((CHUNK, cols, deep), BF16)]
    if guests:
        work.append(VMEM((CHUNK, rows, deep), BF16))
    everything = list(guests) + list(pieces)
    return pl.pallas_call(
        functools.partial(
            triangle_kernel,
            counts=[len(piece) for piece in everything],
            guests=len(guests),
            options=options,
        ),
        grid_spec=pltpu.PrefetchScalarGridSpec(
            num_scalar_prefetch=1,
            grid=(chans // CHUNK,),
            in_specs=[block(rows, deep)] + specs,
            out_specs=[block(h, cols) for h in heights],
            scratch_shapes=work,
        ),
        out_shape=[jax.ShapeDtypeStruct((chans, h, cols), BF16) for h in heights],
        compiler_params=params(),
        cost_estimate=cost(2 * chans * sum(heights) * cols * deep, 10 * half * chans * lanes),
        name="triangle",
    )(flags, left, *[part for piece in everything for part in piece])


def fold_kernel(role_ref, *refs, outputs, half):
    outs, work_ref = refs[-1 - outputs : -1], refs[-1]
    cols = outs[0].shape[1]
    parts = refs[: -1 - outputs]
    c = pl.program_id(0)
    options = len(parts) // 2
    for option in range(options):

        @pl.when((options == 1) | (role_ref[0] == option))
        def _(option=option):
            total = parts[2 * option][...].astype(F32) + parts[2 * option + 1][...].astype(F32)
            at = pl.ds(pl.multiple_of(c * CHUNK, CHUNK), CHUNK)
            work_ref[:, at, :] = jnp.swapaxes(total.astype(BF16), 0, 1)

    @pl.when(c == pl.num_programs(0) - 1)
    def _():
        pitch = work_ref.shape[0] // outputs
        for o, out_ref in enumerate(outs):

            def turn(r, carry, o=o, out_ref=out_ref):
                at = o * pitch + r
                stacked = jnp.concatenate([work_ref[at], work_ref[at + half]], axis=0)
                out_ref[r] = stacked.T[:cols]
                return carry

            lax.fori_loop(0, half, turn, 0, unroll=True)


def fold(half, role, *parts):
    chans, rows, cols = parts[0].shape
    outputs = rows // padded(2 * half, 16)
    out = jax.ShapeDtypeStruct((half, padded(4 * half, 16), 2 * chans), BF16)

    def block(option):
        return pl.BlockSpec(
            (CHUNK, rows, cols),
            lambda c, role_ref: (
                c if len(parts) == 2 else jnp.where(role_ref[0] == option, c, 0), 0, 0
            ),
        )

    return pl.pallas_call(
        functools.partial(fold_kernel, outputs=outputs, half=half),
        grid_spec=pltpu.PrefetchScalarGridSpec(
            num_scalar_prefetch=1,
            grid=(chans // CHUNK,),
            in_specs=[block(i // 2) for i in range(len(parts))],
            out_specs=[pl.BlockSpec(out.shape, lambda c, role_ref: (0, 0, 0))] * outputs,
            scratch_shapes=[VMEM((rows, chans, cols), BF16)],
        ),
        out_shape=[out] * outputs,
        compiler_params=params(),
        cost_estimate=cost(0, 6 * parts[0].size),
        name="fold",
    )(role, *parts)


def finish_kernel(flag_ref, pair_ref, own_ref, other_ref, *refs):
    gate_ref, out_w_ref, in_ref, back_ref = refs[:4]
    earlier_ref, out_ref = refs[4] if len(refs) == 6 else None, refs[-1]
    _, half, cols, width = pair_ref.shape
    block, chans = cols // 2, width // 2
    hidden_units = back_ref.shape[1]
    front = flag_ref[0] == 0
    steps = (half + 1) // 2

    def step(i, carry):
        first = jnp.minimum(2 * i, half - 2)
        rows = [(h, first + e) for h in range(2) for e in range(2)]
        turned = [[ref[first + e].T[:, :block] for ref in (own_ref, other_ref)] for e in range(2)]
        tri = [
            jnp.concatenate([t[h * chans : (h + 1) * chans] for t in turned[e]], axis=0)
            for h in range(2)
            for e in range(2)
        ]
        tri_normed = norm_chans(jnp.concatenate(tri, axis=1).astype(F32)).astype(BF16)
        pair = []
        for h, r in rows:
            row = pair_ref[h, r].astype(F32)
            pair.append(jnp.where(front, row[:block], row[block:]))
        pair = jnp.concatenate(pair, axis=0).T
        normed = norm_chans(pair).astype(BF16)
        out_gate = twice_sigmoid(jnp.dot(gate_ref[...], normed, preferred_element_type=F32))
        update = jnp.dot(out_w_ref[...], tri_normed, preferred_element_type=F32)
        updated = pair + out_gate * update
        trans_normed = norm_chans(updated).astype(BF16)
        expanded = jnp.dot(in_ref[...], trans_normed, preferred_element_type=F32)
        swish, linear = expanded[:hidden_units], expanded[hidden_units:]
        hidden = (swish * twice_sigmoid(swish) * linear).astype(BF16)
        result = updated + jnp.dot(back_ref[...], hidden, preferred_element_type=F32)
        result = result.T
        for s, (h, r) in enumerate(rows):
            mine = result[s * block : (s + 1) * block]
            if earlier_ref is None:
                out_ref[h, r, :block] = mine.astype(BF16)
            else:
                past = earlier_ref[h, r].astype(F32)[:block]
                parts = [jnp.where(front, mine, past), jnp.where(front, past, mine)]
                out_ref[h, r] = jnp.concatenate(parts, axis=0).astype(BF16)
        return carry

    lax.fori_loop(0, steps, step, 0, unroll=4)


def finish(flag, pair, own, other, weights, earlier=None):
    _, half, cols, width = pair.shape
    shape = pair.shape if earlier is not None else (2, half, padded(cols // 2, 16), width)
    extra = [] if earlier is None else [earlier]
    return pl.pallas_call(
        finish_kernel,
        out_shape=jax.ShapeDtypeStruct(shape, BF16),
        in_specs=[pl.BlockSpec(memory_space=pltpu.SMEM)] + whole(7 + len(extra)),
        out_specs=pl.BlockSpec(memory_space=VMEM),
        compiler_params=params(),
        cost_estimate=cost(14 * pair.size * width, 4 * pair.size, 3 * pair.size),
        name="finish",
    )(flag, pair, own, other, *weights, *extra)


def layer_norm(values):
    centered = values - jnp.mean(values, axis=-1, keepdims=True)
    variance = jnp.mean(centered * centered, axis=-1, keepdims=True)
    return centered * lax.rsqrt(variance + 1e-05)


def any_mesh(pair, chain_lengths, in_weight, out_weight, trans_in, trans_out):
    tile_rows, tile_cols, width = pair.shape
    hidden_units = trans_out.shape[0]
    row_count = lax.axis_size("row")
    col_count = lax.axis_size("col")
    outer = row_count // 2
    tokens = tile_rows * row_count
    valid_count = tokens - chain_lengths[chain_lengths.shape[0] - 1]
    row_id = lax.axis_index("row")
    col_id = lax.axis_index("col")
    line_id = row_id // 2

    def along_line(value, step, targets):
        perm = [(2 * (t - step) + b, 2 * t + b) for t in targets for b in range(2)]
        return lax.ppermute(value, "row", perm)

    row_pos = row_id * tile_rows + jnp.arange(tile_rows, dtype=jnp.int32)
    col_pos = col_id * tile_cols + jnp.arange(tile_cols, dtype=jnp.int32)
    pair_mask = ((row_pos < valid_count)[:, None] & (col_pos < valid_count)[None, :]).astype(
        jnp.float32
    )[:, :, None]
    normed = layer_norm(pair.astype(jnp.float32)).astype(jnp.bfloat16).reshape(-1, width)

    def gated(offset):
        block = jnp.dot(
            normed,
            in_weight[:, offset * width : (offset + 2) * width],
            preferred_element_type=jnp.float32,
        ).reshape(tile_rows, tile_cols, 2 * width)
        value = jax.nn.sigmoid(block[..., :width]) * block[..., width:] * pair_mask
        return value.astype(jnp.bfloat16)

    right_ops = gated(2)
    from_left, from_right = {0: right_ops}, {0: right_ops}
    for step in range(1, outer):
        from_left[step] = along_line(from_left[step - 1], 1, range(step, outer))
        from_right[step] = along_line(from_right[step - 1], -1, range(0, outer - step))
    left_ops = gated(0)
    left_other = lax.ppermute(left_ops, "row", [(i, i ^ 1) for i in range(row_count)])
    lefts = jnp.concatenate([left_ops, left_other], axis=0)

    partials = []
    for source in range(outer):
        block = right_ops
        for step in range(1, outer):
            if source + step < outer:
                block = jnp.where(line_id == source + step, from_left[step], block)
            if source - step >= 0:
                block = jnp.where(line_id == source - step, from_right[step], block)
        partials.append(
            jnp.einsum("ikc,jkc->ijc", lefts, block, preferred_element_type=jnp.float32)
        )
    partial = jnp.stack(partials)
    share = outer // col_count
    mine = lax.dynamic_slice_in_dim(partial, col_id * share, share, 0)
    for hop in range(1, col_count):
        target = (col_id + hop) % col_count
        passed = lax.dynamic_slice_in_dim(partial, target * share, share, 0)
        mine = mine + lax.ppermute(
            passed, "col", [(c, (c + hop) % col_count) for c in range(col_count)]
        )
    tri_normed = layer_norm(mine).astype(jnp.bfloat16)
    own_part = tri_normed[:, :tile_rows]
    other_part = lax.ppermute(
        tri_normed[:, tile_rows:], "row", [(i, i ^ 1) for i in range(row_count)]
    )
    even = row_id % 2 == 0
    both = jnp.stack(
        [jnp.where(even, own_part, other_part), jnp.where(even, other_part, own_part)], axis=1
    )
    tri_normed = both.transpose(2, 0, 1, 3, 4).reshape(-1, width)

    out_gate = jax.nn.sigmoid(
        jnp.dot(normed, in_weight[:, 4 * width :], preferred_element_type=jnp.float32)
    )
    update = jnp.dot(tri_normed, out_weight, preferred_element_type=jnp.float32)
    updated = pair.astype(jnp.float32).reshape(-1, width) + out_gate * update
    trans_normed = layer_norm(updated).astype(jnp.bfloat16)
    expanded = jnp.dot(trans_normed, trans_in, preferred_element_type=jnp.float32)
    hidden = (jax.nn.silu(expanded[:, :hidden_units]) * expanded[:, hidden_units:]).astype(
        jnp.bfloat16
    )
    result = updated + jnp.dot(hidden, trans_out, preferred_element_type=jnp.float32)
    return result.reshape(tile_rows, tile_cols, width).astype(jnp.bfloat16)


def per_device(pair, chain_lengths, in_weight, out_weight, trans_in, trans_out):
    if (lax.axis_size("row"), lax.axis_size("col")) != (8, 2):
        return any_mesh(pair, chain_lengths, in_weight, out_weight, trans_in, trans_out)
    return two_by_four(pair, chain_lengths, in_weight, out_weight, trans_in, trans_out)


def two_by_four(pair, chain_lengths, in_weight, out_weight, trans_in, trans_out):
    tile_rows, tile_cols, width = pair.shape
    half = tile_rows // 2
    tokens = tile_rows * lax.axis_size("row")
    valid_count = tokens - chain_lengths[chain_lengths.shape[0] - 1]
    row_id, core = lax.axis_index("row"), lax.axis_index("col")
    place, side = row_id // 2, row_id % 2
    keeper = place // 2

    def among(value, moves):
        return lax.ppermute(value, "row", [(2 * s + b, 2 * t + b) for s, t in moves for b in range(2)])

    def across(value):
        return lax.ppermute(value, "row", [(i, i ^ 1) for i in range(8)])

    def to_core(value, places, keep):
        perm = []
        for z, towards in zip(places, keep):
            target = z // 2 if towards else 1 - z // 2
            perm += [(4 * z + 2 * b + 1 - target, 4 * z + 2 * b + target) for b in range(2)]
        return lax.ppermute(value, ("row", "col"), perm)

    def give_back(value, swap):
        perm = []
        for s, t in ((1, 0), (2, 3)):
            away = 1 - t // 2
            source = 1 - away if swap else away
            perm += [(4 * s + 2 * b + source, 4 * t + 2 * (b ^ swap) + away) for b in range(2)]
        return lax.ppermute(value, ("row", "col"), perm)

    def side_to_side(value, places, holders):
        perm = []
        for z, holder in zip(places, holders):
            perm += [(4 * z + 2 * b + holder, 4 * z + 2 * (1 - b) + holder) for b in range(2)]
        return lax.ppermute(value, ("row", "col"), perm)

    def by_side(block, axis):
        return jnp.where(side == 0, block, jnp.roll(block, width // 2, axis))

    def gate_pair(first):
        parts = [
            by_side(in_weight[:, (first + i) * width : (first + i + 1) * width], 1) for i in range(2)
        ]
        return jnp.concatenate(parts, axis=1).T * BF16(0.5)

    def after(value, *others):
        return lax.optimization_barrier((value, *others))[0]

    def scalars(*values):
        return jnp.stack([jnp.asarray(v).astype(jnp.int32) for v in values])

    is_keeper = core == keeper
    inner = (place == 1) | (place == 2)
    where = scalars(valid_count, row_id * tile_rows, core * tile_cols)
    folded = pair.reshape(2, half, tile_cols, width)
    cross = [(1, 2), (2, 1)]
    everyone, inners = range(4), (1, 2)

    def phase(moves, finished):
        values = lax.optimization_barrier(tuple(v for _, v in moves) + tuple(finished))
        return [send(v) for (send, _), v in zip(moves, values)]

    def hop(moves):
        return lambda value: among(value, moves)

    def either(at_inner, at_end):
        return jnp.where(inner, at_inner, at_end)

    swap = hop([(0, 1), (1, 0), (2, 3), (3, 2)])
    right_own, right_far = project(where, folded, gate_pair(2))
    one = phase([(swap, right_own), (hop(cross), right_own), (across, right_far)], ())
    mate_own, near_own, right_beside = one
    order = jnp.where(is_keeper, place % 2, place // 2)
    weights = [
        in_weight[:, 4 * width :].T * BF16(0.5),
        by_side(out_weight, 0).T * BF16(0.5),
        jnp.where(jnp.arange(trans_in.shape[1])[:, None] < trans_out.shape[0], BF16(0.5), BF16(1.0))
        * trans_in.T,
        trans_out.T,
    ]
    left_own, left_far = project(where, folded, gate_pair(0))
    two = phase(
        [(swap, either(near_own, right_beside)), (hop(cross), right_beside), (across, left_far)],
        one + weights,
    )
    mate_beside, near_beside, left_beside = two
    three = phase(
        [(swap, either(near_beside, left_own)), (hop(cross), mate_own)], (near_beside, left_beside)
    )
    guest_own, far_own = three

    left = left_major(left_own, left_beside)
    plain, outer = scalars(side, 0), scalars(side, jnp.where(inner, 0, 1))
    (home,) = triangle(plain, left, [[right_own], [right_beside]])
    home_rest = to_core(home, everyone, [True] * 4)
    (mate,) = triangle(plain, left, [[mate_own], [mate_beside]])
    mate_rest = to_core(mate, inners, [True] * 2)
    four = phase(
        [(swap, either(right_beside, left_beside)), (hop(cross), mate_beside)], three + [home, mate]
    )
    guest_beside, far_beside = four

    (away,) = triangle(
        outer,
        left,
        [[after(near_own, far_own, mate)], [near_beside], [mate_beside], [guest_own]],
    )
    away_rest = to_core(away, everyone, [False] * 4)
    role = scalars(jnp.where(is_keeper, 0, 1))
    first = fold(half, role, home, home_rest, away, away_rest)
    first_other = across(first[1])
    mate_block = fold(half, role, mate, mate_rest)
    mate_other = side_to_side(mate_block[1], inners, (0, 1))

    late, lent_own, lent_beside = triangle(
        outer,
        left,
        [[after(far_own, mate_other)], [far_beside], [mate_own], [guest_beside]],
        [[guest_own], [guest_beside]],
    )
    lent_rest = to_core(lent_own, inners, [False] * 2), to_core(lent_beside, inners, [True] * 2)
    late_rest = to_core(late, everyone, [True, False, False, True])
    (lent,) = fold(half, role, lent_beside, lent_rest[1], lent_own, lent_rest[0])
    given = give_back(lent, 0), give_back(lent, 1)
    late_block = fold(half, role, late, late_rest)
    late_other = side_to_side(late_block[1], everyone, (0, 1, 0, 1))

    earlier = finish(scalars(order), folded, after(first[0], lent), first_other, weights)
    own, other = (
        jnp.where(inner & is_keeper, early, jnp.where(inner | is_keeper, end, back))
        for early, end, back in zip((mate_block[0], mate_other), (late_block[0], late_other), given)
    )
    result = finish(scalars(1 - order), folded, own, other, weights, earlier)
    return result.reshape(tile_rows, tile_cols, width)


def solution(mesh):
    placed = (P(("crops", "row"), "col", None), P("crops"), P(), P(), P(), P())
    return jax.shard_map(
        per_device,
        mesh=mesh,
        in_specs=placed,
        out_specs=P(("crops", "row"), "col", None),
        check_vma=False,
    )
```

```python
import functools

import jax
import jax.numpy as jnp
from jax import lax
from jax.experimental import pallas as pl
from jax.experimental.pallas import tpu as pltpu
from jax.sharding import PartitionSpec as P

VMEM = pltpu.VMEM
BF16, F32 = jnp.bfloat16, jnp.float32
CHUNK = 16


def whole(count):
    return [pl.BlockSpec(memory_space=VMEM)] * count


def params():
    return pltpu.CompilerParams(vmem_limit_bytes=48 << 20)


def cost(flops, moved, transcendentals=0):
    return pl.CostEstimate(flops=flops, bytes_accessed=moved, transcendentals=transcendentals)


def twice_sigmoid(halved):
    return jnp.tanh(halved) + 1.0


def norm_chans(values):
    centered = values - jnp.mean(values, axis=0, keepdims=True)
    variance = jnp.mean(centered * centered, axis=0, keepdims=True)
    return centered * lax.rsqrt(variance + 1e-05)


def padded(count, unit):
    return -(-count // unit) * unit


def project_kernel(where_ref, pair_ref, weight_ref, own_ref, far_ref):
    valid, row0, col0 = where_ref[0], where_ref[1], where_ref[2]
    _, half, cols, width = pair_ref.shape
    chans = width // 2
    tail = cols - width
    lane = lax.broadcasted_iota(jnp.int32, (1, 3 * width), 1)
    in_tail = lane >= 2 * width
    ends = jnp.where(in_tail, 2 * width + chans, width)
    is_first = jnp.where(lane < ends, 1, 0)
    token = jnp.where(in_tail, lane % chans + width, lane % width) + col0
    gap = jnp.zeros((chans - tail, width), F32)

    def step(r, carry):
        first, second = (pair_ref[h, r].astype(F32) for h in range(2))
        tokens = jnp.concatenate(
            [first[:width], second[:width], first[width:], gap, second[width:], gap], axis=0
        )
        normed = norm_chans(tokens.T).astype(BF16)
        both = jnp.dot(weight_ref[...], normed, preferred_element_type=F32)
        limits = [jnp.where(row0 + h * half + r < valid, valid, 0) for h in range(2)]
        keep = jnp.where(token < limits[1] + is_first * (limits[0] - limits[1]), 1.0, 0.0)
        out = (twice_sigmoid(both[:width]) * both[width:] * keep).astype(BF16)
        own_ref[r] = out[:chans]
        far_ref[r] = out[chans:]
        return carry

    lax.fori_loop(0, half, step, 0, unroll=4)


def project(where, pair, weight):
    _, half, cols, width = pair.shape
    piece = jax.ShapeDtypeStruct((half, width // 2, 3 * width), BF16)
    return pl.pallas_call(
        project_kernel,
        out_shape=(piece, piece),
        in_specs=[pl.BlockSpec(memory_space=pltpu.SMEM)] + whole(2),
        out_specs=whole(2),
        compiler_params=params(),
        cost_estimate=cost(4 * pair.size * width, 4 * pair.size, pair.size),
        name="project",
    )(where, pair, weight)


def channel_major(pieces, left):
    half, chans, lanes = pieces[0].shape
    width = lanes // 3
    main, rest = [], []
    for piece in pieces:
        tail = piece[:, :, 2 * width :]
        turned = jnp.concatenate([tail[:, :, width // 2 :], tail[:, :, : width // 2]], axis=2)
        main += [piece[:, :, :width], piece[:, :, width : 2 * width]]
        rest += [tail, turned]
        if left:
            gap = jnp.zeros((padded(2 * half, 16) - 2 * half, chans, width), BF16)
            main.append(gap)
            rest.append(gap)
    rest = jnp.concatenate(rest, axis=0)
    if left:
        low = lax.broadcasted_iota(jnp.int32, rest.shape, 2) < width // 2
        rest = jnp.where(low, rest, jnp.zeros_like(rest))
    main = jnp.swapaxes(jnp.concatenate(main, axis=0), 0, 1)
    return main, jnp.swapaxes(rest, 0, 1)


def left_kernel(own_ref, beside_ref, out_ref):
    width = own_ref.shape[2] // 3
    main, rest = channel_major([own_ref[...], beside_ref[...]], True)
    out_ref[:, :, :width] = main
    out_ref[:, :, width:] = rest


def left_major(own, beside):
    half, chans, lanes = own.shape
    rows, deep = 2 * padded(2 * half, 16), lanes // 3 * 2
    piece = pl.BlockSpec((half, CHUNK, lanes), lambda c: (0, c, 0))
    return pl.pallas_call(
        left_kernel,
        grid=(chans // CHUNK,),
        out_shape=jax.ShapeDtypeStruct((chans, rows, deep), BF16),
        in_specs=[piece, piece],
        out_specs=pl.BlockSpec((CHUNK, rows, deep), lambda c: (c, 0, 0)),
        compiler_params=params(),
        cost_estimate=cost(0, 8 * own.size),
        name="left_major",
    )(own, beside)


def triangle_kernel(flag_ref, left_ref, *refs, counts, guests, options):
    pieces, refs = [], list(refs)
    for count in counts:
        parts = [refs.pop(0)[...] for _ in range(count)]
        pieces.append(parts[0] if count == 1 else jnp.concatenate(parts, axis=0))
    outs, work = refs[: 1 + guests], refs[1 + guests :]
    visitors, rights = pieces[:guests], pieces[guests:]
    own, beside = rights[:2]
    if options == 2:
        plain = flag_ref[1] == 0
        own = jnp.where(plain, own, rights[2])
        beside = jnp.where(plain, beside, rights[3])
    width = own.shape[2] // 3
    even = flag_ref[0] == 0
    right_ref = work[0]
    main, rest = channel_major(
        [jnp.where(even, own, beside), jnp.where(even, beside, own)], False
    )
    rows = main.shape[1]

    @pl.when(pl.program_id(0) == 0)
    def _():
        right_ref[...] = jnp.zeros_like(right_ref)

    right_ref[:, :rows, :width] = main
    right_ref[:, :rows, width:] = rest
    if guests:
        guest_ref = work[1]
        main, rest = channel_major(visitors, True)
        guest_ref[:, :, :width] = main
        guest_ref[:, :, width:] = rest

    def product(rows):
        dims = (((1,), (1,)), ((), ()))
        return lax.dot_general(rows, right_ref[c], dims, preferred_element_type=F32).astype(BF16)

    for c in range(CHUNK):
        outs[0][c] = product(left_ref[c])
        if guests:
            lent = product(guest_ref[c])
            part = lent.shape[0] // guests
            for g in range(guests):
                outs[1 + g][c] = lent[g * part : (g + 1) * part]


def triangle(flags, left, pieces, guests=()):
    chans, rows, deep = left.shape
    lanes, half = deep // 2 * 3, sum(part.shape[0] for part in pieces[0])
    options, cols = len(pieces) // 2, padded(4 * half, 128)

    def spec(part, option):
        def at(c, flag_ref):
            return (0, c if option is None else jnp.where(flag_ref[1] == option, c, 0), 0)

        return pl.BlockSpec((part.shape[0], CHUNK, lanes), at)

    def block(height, depth):
        return pl.BlockSpec((CHUNK, height, depth), lambda c, flag_ref: (c, 0, 0))

    specs = [spec(part, None) for piece in guests for part in piece]
    for i, piece in enumerate(pieces):
        specs += [spec(part, i // 2 if options == 2 else None) for part in piece]
    heights = [rows] + [rows // 2] * len(guests)
    work = [VMEM((CHUNK, cols, deep), BF16)]
    if guests:
        work.append(VMEM((CHUNK, rows, deep), BF16))
    everything = list(guests) + list(pieces)
    return pl.pallas_call(
        functools.partial(
            triangle_kernel,
            counts=[len(piece) for piece in everything],
            guests=len(guests),
            options=options,
        ),
        grid_spec=pltpu.PrefetchScalarGridSpec(
            num_scalar_prefetch=1,
            grid=(chans // CHUNK,),
            in_specs=[block(rows, deep)] + specs,
            out_specs=[block(h, cols) for h in heights],
            scratch_shapes=work,
        ),
        out_shape=[jax.ShapeDtypeStruct((chans, h, cols), BF16) for h in heights],
        compiler_params=params(),
        cost_estimate=cost(2 * chans * sum(heights) * cols * deep, 10 * half * chans * lanes),
        name="triangle",
    )(flags, left, *[part for piece in everything for part in piece])


def fold_kernel(role_ref, *refs, outputs, half):
    outs, work_ref = refs[-1 - outputs : -1], refs[-1]
    cols = outs[0].shape[1]
    parts = refs[: -1 - outputs]
    c = pl.program_id(0)
    options = len(parts) // 2
    for option in range(options):

        @pl.when((options == 1) | (role_ref[0] == option))
        def _(option=option):
            total = parts[2 * option][...].astype(F32) + parts[2 * option + 1][...].astype(F32)
            at = pl.ds(pl.multiple_of(c * CHUNK, CHUNK), CHUNK)
            work_ref[:, at, :] = jnp.swapaxes(total.astype(BF16), 0, 1)

    @pl.when(c == pl.num_programs(0) - 1)
    def _():
        pitch = work_ref.shape[0] // outputs
        for o, out_ref in enumerate(outs):

            def turn(r, carry, o=o, out_ref=out_ref):
                at = o * pitch + r
                stacked = jnp.concatenate([work_ref[at], work_ref[at + half]], axis=0)
                out_ref[r] = stacked.T[:cols]
                return carry

            lax.fori_loop(0, half, turn, 0, unroll=True)


def fold(half, role, *parts):
    chans, rows, cols = parts[0].shape
    outputs = rows // padded(2 * half, 16)
    out = jax.ShapeDtypeStruct((half, padded(4 * half, 16), 2 * chans), BF16)

    def block(option):
        return pl.BlockSpec(
            (CHUNK, rows, cols),
            lambda c, role_ref: (
                c if len(parts) == 2 else jnp.where(role_ref[0] == option, c, 0), 0, 0
            ),
        )

    return pl.pallas_call(
        functools.partial(fold_kernel, outputs=outputs, half=half),
        grid_spec=pltpu.PrefetchScalarGridSpec(
            num_scalar_prefetch=1,
            grid=(chans // CHUNK,),
            in_specs=[block(i // 2) for i in range(len(parts))],
            out_specs=[pl.BlockSpec(out.shape, lambda c, role_ref: (0, 0, 0))] * outputs,
            scratch_shapes=[VMEM((rows, chans, cols), BF16)],
        ),
        out_shape=[out] * outputs,
        compiler_params=params(),
        cost_estimate=cost(0, 6 * parts[0].size),
        name="fold",
    )(role, *parts)


def prepare_kernel(flag_ref, pair_ref, gate_w_ref, pair_out_ref, gate_ref):
    _, half, cols, width = pair_ref.shape
    block = cols // 2
    front = flag_ref[0] == 0

    def step(i, carry):
        first = jnp.minimum(2 * i, half - 2)
        pair = []
        for h, r in [(h, first + e) for h in range(2) for e in range(2)]:
            row = pair_ref[h, r].astype(F32)
            pair.append(jnp.where(front, row[:block], row[block:]))
        pair = jnp.concatenate(pair, axis=0).T
        normed = norm_chans(pair).astype(BF16)
        pair_out_ref[i, :, : 4 * block] = pair.astype(BF16)
        gate = jnp.dot(gate_w_ref[...], normed, preferred_element_type=F32)
        gate_ref[i, :, : 4 * block] = twice_sigmoid(gate)
        return carry

    lax.fori_loop(0, pair_out_ref.shape[0], step, 0, unroll=4)


def prepare(flag, pair, gate_w):
    _, half, cols, width = pair.shape
    shape = ((half + 1) // 2, width, padded(2 * cols, 128))
    return pl.pallas_call(
        prepare_kernel,
        out_shape=(jax.ShapeDtypeStruct(shape, BF16), jax.ShapeDtypeStruct(shape, F32)),
        in_specs=[pl.BlockSpec(memory_space=pltpu.SMEM)] + whole(2),
        out_specs=whole(2),
        compiler_params=params(),
        cost_estimate=cost(pair.size * width, 6 * pair.size, pair.size // 2),
        name="prepare",
    )(flag, pair, gate_w)


def finish_kernel(flag_ref, pair_ref, gate_ref, own_ref, other_ref, *refs, cols):
    out_w_ref, in_ref, back_ref = refs[:3]
    earlier_ref, out_ref = refs[3] if len(refs) == 5 else None, refs[-1]
    steps, width, _ = pair_ref.shape
    half = own_ref.shape[0]
    block, chans = cols // 2, width // 2
    hidden_units = back_ref.shape[1]
    front = flag_ref[0] == 0

    def step(i, carry):
        first = jnp.minimum(2 * i, half - 2)
        rows = [(h, first + e) for h in range(2) for e in range(2)]
        turned = [[ref[first + e].T[:, :block] for ref in (own_ref, other_ref)] for e in range(2)]
        tri = [
            jnp.concatenate([t[h * chans : (h + 1) * chans] for t in turned[e]], axis=0)
            for h in range(2)
            for e in range(2)
        ]
        tri_normed = norm_chans(jnp.concatenate(tri, axis=1).astype(F32)).astype(BF16)
        pair = pair_ref[i, :, : 4 * block].astype(F32)
        update = jnp.dot(out_w_ref[...], tri_normed, preferred_element_type=F32)
        updated = pair + gate_ref[i, :, : 4 * block] * update
        trans_normed = norm_chans(updated).astype(BF16)
        expanded = jnp.dot(in_ref[...], trans_normed, preferred_element_type=F32)
        swish, linear = expanded[:hidden_units], expanded[hidden_units:]
        hidden = (swish * twice_sigmoid(swish) * linear).astype(BF16)
        result = updated + jnp.dot(back_ref[...], hidden, preferred_element_type=F32)
        result = result.T
        for s, (h, r) in enumerate(rows):
            mine = result[s * block : (s + 1) * block]
            if earlier_ref is None:
                out_ref[h, r, :block] = mine.astype(BF16)
            else:
                past = earlier_ref[h, r].astype(F32)[:block]
                parts = [jnp.where(front, mine, past), jnp.where(front, past, mine)]
                out_ref[h, r] = jnp.concatenate(parts, axis=0).astype(BF16)
        return carry

    lax.fori_loop(0, steps, step, 0, unroll=4)


def finish(flag, cols, prepared, own, other, weights, earlier=None):
    half, _, width = own.shape
    shape = (2, half, padded(cols // 2, 16) if earlier is None else cols, width)
    extra = [] if earlier is None else [earlier]
    size = own.size * 2
    return pl.pallas_call(
        functools.partial(finish_kernel, cols=cols),
        out_shape=jax.ShapeDtypeStruct(shape, BF16),
        in_specs=[pl.BlockSpec(memory_space=pltpu.SMEM)] + whole(7 + len(extra)),
        out_specs=pl.BlockSpec(memory_space=VMEM),
        compiler_params=params(),
        cost_estimate=cost(26 * size * width, 10 * size, 5 * size),
        name="finish",
    )(flag, *prepared, own, other, *weights, *extra)


def layer_norm(values):
    centered = values - jnp.mean(values, axis=-1, keepdims=True)
    variance = jnp.mean(centered * centered, axis=-1, keepdims=True)
    return centered * lax.rsqrt(variance + 1e-05)


def any_mesh(pair, chain_lengths, in_weight, out_weight, trans_in, trans_out):
    tile_rows, tile_cols, width = pair.shape
    hidden_units = trans_out.shape[0]
    row_count = lax.axis_size("row")
    col_count = lax.axis_size("col")
    outer = row_count // 2
    tokens = tile_rows * row_count
    valid_count = tokens - chain_lengths[chain_lengths.shape[0] - 1]
    row_id = lax.axis_index("row")
    col_id = lax.axis_index("col")
    line_id = row_id // 2

    def along_line(value, step, targets):
        perm = [(2 * (t - step) + b, 2 * t + b) for t in targets for b in range(2)]
        return lax.ppermute(value, "row", perm)

    row_pos = row_id * tile_rows + jnp.arange(tile_rows, dtype=jnp.int32)
    col_pos = col_id * tile_cols + jnp.arange(tile_cols, dtype=jnp.int32)
    pair_mask = ((row_pos < valid_count)[:, None] & (col_pos < valid_count)[None, :]).astype(
        jnp.float32
    )[:, :, None]
    normed = layer_norm(pair.astype(jnp.float32)).astype(jnp.bfloat16).reshape(-1, width)

    def gated(offset):
        block = jnp.dot(
            normed,
            in_weight[:, offset * width : (offset + 2) * width],
            preferred_element_type=jnp.float32,
        ).reshape(tile_rows, tile_cols, 2 * width)
        value = jax.nn.sigmoid(block[..., :width]) * block[..., width:] * pair_mask
        return value.astype(jnp.bfloat16)

    right_ops = gated(2)
    from_left, from_right = {0: right_ops}, {0: right_ops}
    for step in range(1, outer):
        from_left[step] = along_line(from_left[step - 1], 1, range(step, outer))
        from_right[step] = along_line(from_right[step - 1], -1, range(0, outer - step))
    left_ops = gated(0)
    left_other = lax.ppermute(left_ops, "row", [(i, i ^ 1) for i in range(row_count)])
    lefts = jnp.concatenate([left_ops, left_other], axis=0)

    partials = []
    for source in range(outer):
        block = right_ops
        for step in range(1, outer):
            if source + step < outer:
                block = jnp.where(line_id == source + step, from_left[step], block)
            if source - step >= 0:
                block = jnp.where(line_id == source - step, from_right[step], block)
        partials.append(
            jnp.einsum("ikc,jkc->ijc", lefts, block, preferred_element_type=jnp.float32)
        )
    partial = jnp.stack(partials)
    share = outer // col_count
    mine = lax.dynamic_slice_in_dim(partial, col_id * share, share, 0)
    for hop in range(1, col_count):
        target = (col_id + hop) % col_count
        passed = lax.dynamic_slice_in_dim(partial, target * share, share, 0)
        mine = mine + lax.ppermute(
            passed, "col", [(c, (c + hop) % col_count) for c in range(col_count)]
        )
    tri_normed = layer_norm(mine).astype(jnp.bfloat16)
    own_part = tri_normed[:, :tile_rows]
    other_part = lax.ppermute(
        tri_normed[:, tile_rows:], "row", [(i, i ^ 1) for i in range(row_count)]
    )
    even = row_id % 2 == 0
    both = jnp.stack(
        [jnp.where(even, own_part, other_part), jnp.where(even, other_part, own_part)], axis=1
    )
    tri_normed = both.transpose(2, 0, 1, 3, 4).reshape(-1, width)

    out_gate = jax.nn.sigmoid(
        jnp.dot(normed, in_weight[:, 4 * width :], preferred_element_type=jnp.float32)
    )
    update = jnp.dot(tri_normed, out_weight, preferred_element_type=jnp.float32)
    updated = pair.astype(jnp.float32).reshape(-1, width) + out_gate * update
    trans_normed = layer_norm(updated).astype(jnp.bfloat16)
    expanded = jnp.dot(trans_normed, trans_in, preferred_element_type=jnp.float32)
    hidden = (jax.nn.silu(expanded[:, :hidden_units]) * expanded[:, hidden_units:]).astype(
        jnp.bfloat16
    )
    result = updated + jnp.dot(hidden, trans_out, preferred_element_type=jnp.float32)
    return result.reshape(tile_rows, tile_cols, width).astype(jnp.bfloat16)


def per_device(pair, chain_lengths, in_weight, out_weight, trans_in, trans_out):
    if (lax.axis_size("row"), lax.axis_size("col")) != (8, 2):
        return any_mesh(pair, chain_lengths, in_weight, out_weight, trans_in, trans_out)
    return two_by_four(pair, chain_lengths, in_weight, out_weight, trans_in, trans_out)


def two_by_four(pair, chain_lengths, in_weight, out_weight, trans_in, trans_out):
    tile_rows, tile_cols, width = pair.shape
    half = tile_rows // 2
    tokens = tile_rows * lax.axis_size("row")
    valid_count = tokens - chain_lengths[chain_lengths.shape[0] - 1]
    row_id, core = lax.axis_index("row"), lax.axis_index("col")
    place, side = row_id // 2, row_id % 2
    keeper = place // 2

    def among(value, moves):
        return lax.ppermute(value, "row", [(2 * s + b, 2 * t + b) for s, t in moves for b in range(2)])

    def across(value):
        return lax.ppermute(value, "row", [(i, i ^ 1) for i in range(8)])

    def to_core(value, places, keep):
        perm = []
        for z, towards in zip(places, keep):
            target = z // 2 if towards else 1 - z // 2
            perm += [(4 * z + 2 * b + 1 - target, 4 * z + 2 * b + target) for b in range(2)]
        return lax.ppermute(value, ("row", "col"), perm)

    def give_back(value, swap):
        perm = []
        for s, t in ((1, 0), (2, 3)):
            away = 1 - t // 2
            source = 1 - away if swap else away
            perm += [(4 * s + 2 * b + source, 4 * t + 2 * (b ^ swap) + away) for b in range(2)]
        return lax.ppermute(value, ("row", "col"), perm)

    def side_to_side(value, places, holders):
        perm = []
        for z, holder in zip(places, holders):
            perm += [(4 * z + 2 * b + holder, 4 * z + 2 * (1 - b) + holder) for b in range(2)]
        return lax.ppermute(value, ("row", "col"), perm)

    def by_side(block, axis):
        return jnp.where(side == 0, block, jnp.roll(block, width // 2, axis))

    def gate_pair(first):
        parts = [
            by_side(in_weight[:, (first + i) * width : (first + i + 1) * width], 1) for i in range(2)
        ]
        return jnp.concatenate(parts, axis=1).T * BF16(0.5)

    def after(value, *others):
        return lax.optimization_barrier((value, *others))[0]

    def scalars(*values):
        return jnp.stack([jnp.asarray(v).astype(jnp.int32) for v in values])

    is_keeper = core == keeper
    inner = (place == 1) | (place == 2)
    where = scalars(valid_count, row_id * tile_rows, core * tile_cols)
    folded = pair.reshape(2, half, tile_cols, width)
    cross = [(1, 2), (2, 1)]
    everyone, inners = range(4), (1, 2)

    def phase(moves, finished):
        values = lax.optimization_barrier(tuple(v for _, v in moves) + tuple(finished))
        return [send(v) for (send, _), v in zip(moves, values)]

    def hop(moves):
        return lambda value: among(value, moves)

    def either(at_inner, at_end):
        return jnp.where(inner, at_inner, at_end)

    swap = hop([(0, 1), (1, 0), (2, 3), (3, 2)])
    right_own, right_far = project(where, folded, gate_pair(2))
    one = phase([(swap, right_own), (hop(cross), right_own), (across, right_far)], ())
    mate_own, near_own, right_beside = one
    order = jnp.where(is_keeper, place % 2, place // 2)
    weights = [
        by_side(out_weight, 0).T * BF16(0.5),
        jnp.where(jnp.arange(trans_in.shape[1])[:, None] < trans_out.shape[0], BF16(0.5), BF16(1.0))
        * trans_in.T,
        trans_out.T,
    ]
    gate_weight = in_weight[:, 4 * width :].T * BF16(0.5)
    left_own, left_far = project(where, folded, gate_pair(0))
    two = phase(
        [(swap, either(near_own, right_beside)), (hop(cross), right_beside), (across, left_far)],
        one + weights + [gate_weight],
    )
    prepared = [prepare(scalars(f), after(folded, *one), gate_weight) for f in (order, 1 - order)]
    mate_beside, near_beside, left_beside = two
    three = phase(
        [(swap, either(near_beside, left_own)), (hop(cross), mate_own)], (near_beside, left_beside, *prepared[0], *prepared[1]),
    )
    guest_own, far_own = three

    left = left_major(left_own, left_beside)
    plain, outer = scalars(side, 0), scalars(side, jnp.where(inner, 0, 1))
    (home,) = triangle(plain, left, [[right_own], [right_beside]])
    home_rest = to_core(home, everyone, [True] * 4)
    (mate,) = triangle(plain, left, [[mate_own], [mate_beside]])
    mate_rest = to_core(mate, inners, [True] * 2)
    four = phase(
        [(swap, either(right_beside, left_beside)), (hop(cross), mate_beside)], three + [home, mate]
    )
    guest_beside, far_beside = four

    (away,) = triangle(
        outer,
        left,
        [[after(near_own, far_own, mate)], [near_beside], [mate_beside], [guest_own]],
    )
    away_rest = to_core(away, everyone, [False] * 4)
    role = scalars(jnp.where(is_keeper, 0, 1))
    first = fold(half, role, home, home_rest, away, away_rest)
    first_other = across(first[1])
    mate_block = fold(half, role, mate, mate_rest)
    mate_other = side_to_side(mate_block[1], inners, (0, 1))

    late, lent_own, lent_beside = triangle(
        outer,
        left,
        [[after(far_own, mate_other)], [far_beside], [mate_own], [guest_beside]],
        [[guest_own], [guest_beside]],
    )
    lent_rest = to_core(lent_own, inners, [False] * 2), to_core(lent_beside, inners, [True] * 2)
    late_rest = to_core(late, everyone, [True, False, False, True])
    (lent,) = fold(half, role, lent_beside, lent_rest[1], lent_own, lent_rest[0])
    given = give_back(lent, 0), give_back(lent, 1)
    late_block = fold(half, role, late, late_rest)
    late_other = side_to_side(late_block[1], everyone, (0, 1, 0, 1))

    earlier = finish(
        scalars(order), tile_cols, prepared[0], after(first[0], lent), first_other, weights
    )
    own, other = (
        jnp.where(inner & is_keeper, early, jnp.where(inner | is_keeper, end, back))
        for early, end, back in zip((mate_block[0], mate_other), (late_block[0], late_other), given)
    )
    result = finish(scalars(1 - order), tile_cols, prepared[1], own, other, weights, earlier)
    return result.reshape(tile_rows, tile_cols, width)


def solution(mesh):
    placed = (P(("crops", "row"), "col", None), P("crops"), P(), P(), P(), P())
    return jax.shard_map(
        per_device,
        mesh=mesh,
        in_specs=placed,
        out_specs=P(("crops", "row"), "col", None),
        check_vma=False,
    )
```

```python
import functools

import jax
import jax.numpy as jnp
from jax import lax
from jax.experimental import pallas as pl
from jax.experimental.pallas import tpu as pltpu
from jax.sharding import PartitionSpec as P

VMEM = pltpu.VMEM
BF16, F32 = jnp.bfloat16, jnp.float32
CHUNK = 16


def whole(count):
    return [pl.BlockSpec(memory_space=VMEM)] * count


def params():
    return pltpu.CompilerParams(vmem_limit_bytes=20 << 20)


def cost(flops, moved, transcendentals=0):
    return pl.CostEstimate(flops=flops, bytes_accessed=moved, transcendentals=transcendentals)


def twice_sigmoid(halved):
    return jnp.tanh(halved) + 1.0


def norm_chans(values):
    centered = values - jnp.mean(values, axis=0, keepdims=True)
    variance = jnp.mean(centered * centered, axis=0, keepdims=True)
    return centered * lax.rsqrt(variance + 1e-05)


def padded(count, unit):
    return -(-count // unit) * unit


def project_kernel(where_ref, pair_hbm, weight_ref, own_ref, far_ref, pair_ref, both_ref, sems, first):
    valid, row0, col0, side = (where_ref[i] for i in range(4))
    _, half, cols, width = pair_ref.shape
    chans = width // 2
    tail = cols - width
    count = sems.shape[0]
    size = -(-half // count)
    spans = [(k * size, min(size, half - k * size)) for k in range(count)]
    loads = [
        pltpu.make_async_copy(
            pair_hbm.at[:, pl.ds(start, length)], pair_ref.at[:, pl.ds(start, length)], sems.at[k]
        )
        for k, (start, length) in enumerate(spans)
    ]
    for load in loads:
        load.start()

    for i in range(2):
        block = weight_ref[:, (first + i) * width : (first + i + 1) * width].astype(F32)
        block = jnp.where(side == 0, block, pltpu.roll(block, chans, 1))
        both_ref[i * width : (i + 1) * width] = (block.T * 0.5).astype(BF16)

    lane = lax.broadcasted_iota(jnp.int32, (1, 3 * width), 1)
    in_tail = lane >= 2 * width
    ends = jnp.where(in_tail, 2 * width + chans, width)
    is_first = jnp.where(lane < ends, 1, 0)
    token = jnp.where(in_tail, lane % chans + width, lane % width) + col0
    gap = jnp.zeros((chans - tail, width), F32)

    def step(r, carry):
        first, second = (pair_ref[h, r].astype(F32) for h in range(2))
        tokens = jnp.concatenate(
            [first[:width], second[:width], first[width:], gap, second[width:], gap], axis=0
        )
        normed = norm_chans(tokens.T).astype(BF16)
        both = jnp.dot(both_ref[...], normed, preferred_element_type=F32)
        limits = [jnp.where(row0 + h * half + r < valid, valid, 0) for h in range(2)]
        keep = jnp.where(token < limits[1] + is_first * (limits[0] - limits[1]), 1.0, 0.0)
        out = (twice_sigmoid(both[:width]) * both[width:] * keep).astype(BF16)
        own_ref[r] = out[:chans]
        far_ref[r] = out[chans:]
        return carry

    for load, (start, length) in zip(loads, spans):
        load.wait()
        lax.fori_loop(start, start + length, step, 0, unroll=3)


def project(where, pair, weight, first):
    _, half, cols, width = pair.shape
    piece = jax.ShapeDtypeStruct((half, width // 2, 3 * width), BF16)
    return pl.pallas_call(
        functools.partial(project_kernel, first=first),
        out_shape=(piece, piece),
        in_specs=[
            pl.BlockSpec(memory_space=pltpu.SMEM),
            pl.BlockSpec(memory_space=pl.ANY),
            pl.BlockSpec(memory_space=VMEM),
        ],
        out_specs=whole(2),
        scratch_shapes=[
            VMEM(pair.shape, BF16),
            VMEM((2 * width, width), BF16),
            pltpu.SemaphoreType.DMA((4,)),
        ],
        compiler_params=params(),
        cost_estimate=cost(4 * pair.size * width, 4 * pair.size, pair.size),
        name="project",
    )(where, pair, weight)


def channel_major(pieces, left):
    half, chans, lanes = pieces[0].shape
    width = lanes // 3
    main, rest = [], []
    for piece in pieces:
        tail = piece[:, :, 2 * width :]
        turned = jnp.concatenate([tail[:, :, width // 2 :], tail[:, :, : width // 2]], axis=2)
        main += [piece[:, :, :width], piece[:, :, width : 2 * width]]
        rest += [tail, turned]
        if left:
            gap = jnp.zeros((padded(2 * half, 16) - 2 * half, chans, width), BF16)
            main.append(gap)
            rest.append(gap)
    rest = jnp.concatenate(rest, axis=0)
    if left:
        low = lax.broadcasted_iota(jnp.int32, rest.shape, 2) < width // 2
        rest = jnp.where(low, rest, jnp.zeros_like(rest))
    main = jnp.swapaxes(jnp.concatenate(main, axis=0), 0, 1)
    return main, jnp.swapaxes(rest, 0, 1)


def left_kernel(own_ref, beside_ref, out_ref):
    width = own_ref.shape[2] // 3
    main, rest = channel_major([own_ref[...], beside_ref[...]], True)
    out_ref[:, :, :width] = main
    out_ref[:, :, width:] = rest


def left_major(own, beside):
    half, chans, lanes = own.shape
    rows, deep = 2 * padded(2 * half, 16), lanes // 3 * 2
    piece = pl.BlockSpec((half, CHUNK, lanes), lambda c: (0, c, 0))
    return pl.pallas_call(
        left_kernel,
        grid=(chans // CHUNK,),
        out_shape=jax.ShapeDtypeStruct((chans, rows, deep), BF16),
        in_specs=[piece, piece],
        out_specs=pl.BlockSpec((CHUNK, rows, deep), lambda c: (c, 0, 0)),
        compiler_params=params(),
        cost_estimate=cost(0, 8 * own.size),
        name="left_major",
    )(own, beside)


def triangle_kernel(flag_ref, left_ref, *refs, counts, guests, options):
    pieces, refs = [], list(refs)
    for count in counts:
        parts = [refs.pop(0)[...] for _ in range(count)]
        pieces.append(parts[0] if count == 1 else jnp.concatenate(parts, axis=0))
    outs, work = refs[: 1 + guests], refs[1 + guests :]
    visitors, rights = pieces[:guests], pieces[guests:]
    own, beside = rights[:2]
    if options == 2:
        plain = flag_ref[1] == 0
        own = jnp.where(plain, own, rights[2])
        beside = jnp.where(plain, beside, rights[3])
    width = own.shape[2] // 3
    even = flag_ref[0] == 0
    right_ref = work[0]
    main, rest = channel_major(
        [jnp.where(even, own, beside), jnp.where(even, beside, own)], False
    )
    rows = main.shape[1]

    @pl.when(pl.program_id(0) == 0)
    def _():
        right_ref[...] = jnp.zeros_like(right_ref)

    right_ref[:, :rows, :width] = main
    right_ref[:, :rows, width:] = rest
    if guests:
        guest_ref = work[1]
        main, rest = channel_major(visitors, True)
        guest_ref[:, :, :width] = main
        guest_ref[:, :, width:] = rest

    def product(rows):
        dims = (((1,), (1,)), ((), ()))
        return lax.dot_general(rows, right_ref[c], dims, preferred_element_type=F32).astype(BF16)

    for c in range(CHUNK):
        outs[0][c] = product(left_ref[c])
        if guests:
            lent = product(guest_ref[c])
            part = lent.shape[0] // guests
            for g in range(guests):
                outs[1 + g][c] = lent[g * part : (g + 1) * part]


def triangle(flags, left, pieces, guests=()):
    chans, rows, deep = left.shape
    lanes, half = deep // 2 * 3, sum(part.shape[0] for part in pieces[0])
    options, cols = len(pieces) // 2, padded(4 * half, 128)

    def spec(part, option):
        def at(c, flag_ref):
            return (0, c if option is None else jnp.where(flag_ref[1] == option, c, 0), 0)

        return pl.BlockSpec((part.shape[0], CHUNK, lanes), at)

    def block(height, depth):
        return pl.BlockSpec((CHUNK, height, depth), lambda c, flag_ref: (c, 0, 0))

    specs = [spec(part, None) for piece in guests for part in piece]
    for i, piece in enumerate(pieces):
        specs += [spec(part, i // 2 if options == 2 else None) for part in piece]
    heights = [rows] + [rows // 2] * len(guests)
    work = [VMEM((CHUNK, cols, deep), BF16)]
    if guests:
        work.append(VMEM((CHUNK, rows, deep), BF16))
    everything = list(guests) + list(pieces)
    return pl.pallas_call(
        functools.partial(
            triangle_kernel,
            counts=[len(piece) for piece in everything],
            guests=len(guests),
            options=options,
        ),
        grid_spec=pltpu.PrefetchScalarGridSpec(
            num_scalar_prefetch=1,
            grid=(chans // CHUNK,),
            in_specs=[block(rows, deep)] + specs,
            out_specs=[block(h, cols) for h in heights],
            scratch_shapes=work,
        ),
        out_shape=[jax.ShapeDtypeStruct((chans, h, cols), BF16) for h in heights],
        compiler_params=params(),
        cost_estimate=cost(2 * chans * sum(heights) * cols * deep, 10 * half * chans * lanes),
        name="triangle",
    )(flags, left, *[part for piece in everything for part in piece])


def fold_kernel(role_ref, *refs, outputs, half):
    outs, work_ref = refs[-1 - outputs : -1], refs[-1]
    cols = outs[0].shape[1]
    parts = refs[: -1 - outputs]
    c = pl.program_id(0)
    options = len(parts) // 2
    for option in range(options):

        @pl.when((options == 1) | (role_ref[0] == option))
        def _(option=option):
            total = parts[2 * option][...].astype(F32) + parts[2 * option + 1][...].astype(F32)
            at = pl.ds(pl.multiple_of(c * CHUNK, CHUNK), CHUNK)
            work_ref[:, at, :] = jnp.swapaxes(total.astype(BF16), 0, 1)

    @pl.when(c == pl.num_programs(0) - 1)
    def _():
        pitch = work_ref.shape[0] // outputs
        for o, out_ref in enumerate(outs):

            def turn(r, carry, o=o, out_ref=out_ref):
                at = o * pitch + r
                stacked = jnp.concatenate([work_ref[at], work_ref[at + half]], axis=0)
                out_ref[r] = stacked.T[:cols]
                return carry

            lax.fori_loop(0, half, turn, 0, unroll=True)


def fold(half, role, *parts):
    chans, rows, cols = parts[0].shape
    outputs = rows // padded(2 * half, 16)
    out = jax.ShapeDtypeStruct((half, padded(4 * half, 16), 2 * chans), BF16)

    def block(option):
        return pl.BlockSpec(
            (CHUNK, rows, cols),
            lambda c, role_ref: (
                c if len(parts) == 2 else jnp.where(role_ref[0] == option, c, 0), 0, 0
            ),
        )

    return pl.pallas_call(
        functools.partial(fold_kernel, outputs=outputs, half=half),
        grid_spec=pltpu.PrefetchScalarGridSpec(
            num_scalar_prefetch=1,
            grid=(chans // CHUNK,),
            in_specs=[block(i // 2) for i in range(len(parts))],
            out_specs=[pl.BlockSpec(out.shape, lambda c, role_ref: (0, 0, 0))] * outputs,
            scratch_shapes=[VMEM((rows, chans, cols), BF16)],
        ),
        out_shape=[out] * outputs,
        compiler_params=params(),
        cost_estimate=cost(0, 6 * parts[0].size),
        name="fold",
    )(role, *parts)


def prepare_kernel(flag_ref, pair_ref, gate_w_ref, pair_out_ref, gate_ref):
    _, half, cols, width = pair_ref.shape
    block = cols // 2
    front = flag_ref[0] == 0

    def step(i, carry):
        first = jnp.minimum(2 * i, half - 2)
        pair = []
        for h, r in [(h, first + e) for h in range(2) for e in range(2)]:
            row = pair_ref[h, r].astype(F32)
            pair.append(jnp.where(front, row[:block], row[block:]))
        pair = jnp.concatenate(pair, axis=0).T
        normed = norm_chans(pair).astype(BF16)
        pair_out_ref[i, :, : 4 * block] = pair.astype(BF16)
        gate = jnp.dot(gate_w_ref[...], normed, preferred_element_type=F32)
        gate_ref[i, :, : 4 * block] = twice_sigmoid(gate)
        return carry

    lax.fori_loop(0, pair_out_ref.shape[0], step, 0, unroll=4)


def prepare(flag, pair, gate_w):
    _, half, cols, width = pair.shape
    shape = ((half + 1) // 2, width, padded(2 * cols, 128))
    return pl.pallas_call(
        prepare_kernel,
        out_shape=(jax.ShapeDtypeStruct(shape, BF16), jax.ShapeDtypeStruct(shape, F32)),
        in_specs=[pl.BlockSpec(memory_space=pltpu.SMEM)] + whole(2),
        out_specs=whole(2),
        compiler_params=params(),
        cost_estimate=cost(pair.size * width, 6 * pair.size, pair.size // 2),
        name="prepare",
    )(flag, pair, gate_w)


def finish_kernel(flag_ref, pair_ref, gate_ref, own_ref, other_ref, *refs, cols):
    out_w_ref, in_ref, back_ref = refs[:3]
    earlier_ref, out_ref = refs[3] if len(refs) == 5 else None, refs[-1]
    steps, width, _ = pair_ref.shape
    half = own_ref.shape[0]
    block, chans = cols // 2, width // 2
    hidden_units = back_ref.shape[1]
    front = flag_ref[0] == 0

    def step(i, carry):
        first = jnp.minimum(2 * i, half - 2)
        rows = [(h, first + e) for h in range(2) for e in range(2)]
        turned = [[ref[first + e].T[:, :block] for ref in (own_ref, other_ref)] for e in range(2)]
        tri = [
            jnp.concatenate([t[h * chans : (h + 1) * chans] for t in turned[e]], axis=0)
            for h in range(2)
            for e in range(2)
        ]
        tri_normed = norm_chans(jnp.concatenate(tri, axis=1).astype(F32)).astype(BF16)
        pair = pair_ref[i, :, : 4 * block].astype(F32)
        update = jnp.dot(out_w_ref[...], tri_normed, preferred_element_type=F32)
        updated = pair + gate_ref[i, :, : 4 * block] * update
        trans_normed = norm_chans(updated).astype(BF16)
        expanded = jnp.dot(in_ref[...], trans_normed, preferred_element_type=F32)
        swish, linear = expanded[:hidden_units], expanded[hidden_units:]
        hidden = (swish * twice_sigmoid(swish) * linear).astype(BF16)
        result = updated + jnp.dot(back_ref[...], hidden, preferred_element_type=F32)
        result = result.T
        for s, (h, r) in enumerate(rows):
            mine = result[s * block : (s + 1) * block]
            if earlier_ref is None:
                out_ref[h, r, :block] = mine.astype(BF16)
            else:
                past = earlier_ref[h, r].astype(F32)[:block]
                parts = [jnp.where(front, mine, past), jnp.where(front, past, mine)]
                out_ref[h, r] = jnp.concatenate(parts, axis=0).astype(BF16)
        return carry

    lax.fori_loop(0, steps, step, 0, unroll=4)


def finish(flag, cols, prepared, own, other, weights, earlier=None):
    half, _, width = own.shape
    shape = (2, half, padded(cols // 2, 16) if earlier is None else cols, width)
    extra = [] if earlier is None else [earlier]
    size = own.size * 2
    return pl.pallas_call(
        functools.partial(finish_kernel, cols=cols),
        out_shape=jax.ShapeDtypeStruct(shape, BF16),
        in_specs=[pl.BlockSpec(memory_space=pltpu.SMEM)] + whole(7 + len(extra)),
        out_specs=pl.BlockSpec(memory_space=VMEM),
        compiler_params=params(),
        cost_estimate=cost(26 * size * width, 10 * size, 5 * size),
        name="finish",
    )(flag, *prepared, own, other, *weights, *extra)


def layer_norm(values):
    centered = values - jnp.mean(values, axis=-1, keepdims=True)
    variance = jnp.mean(centered * centered, axis=-1, keepdims=True)
    return centered * lax.rsqrt(variance + 1e-05)


def any_mesh(pair, chain_lengths, in_weight, out_weight, trans_in, trans_out):
    tile_rows, tile_cols, width = pair.shape
    hidden_units = trans_out.shape[0]
    row_count = lax.axis_size("row")
    col_count = lax.axis_size("col")
    outer = row_count // 2
    tokens = tile_rows * row_count
    valid_count = tokens - chain_lengths[chain_lengths.shape[0] - 1]
    row_id = lax.axis_index("row")
    col_id = lax.axis_index("col")
    line_id = row_id // 2

    def along_line(value, step, targets):
        perm = [(2 * (t - step) + b, 2 * t + b) for t in targets for b in range(2)]
        return lax.ppermute(value, "row", perm)

    row_pos = row_id * tile_rows + jnp.arange(tile_rows, dtype=jnp.int32)
    col_pos = col_id * tile_cols + jnp.arange(tile_cols, dtype=jnp.int32)
    pair_mask = ((row_pos < valid_count)[:, None] & (col_pos < valid_count)[None, :]).astype(
        jnp.float32
    )[:, :, None]
    normed = layer_norm(pair.astype(jnp.float32)).astype(jnp.bfloat16).reshape(-1, width)

    def gated(offset):
        block = jnp.dot(
            normed,
            in_weight[:, offset * width : (offset + 2) * width],
            preferred_element_type=jnp.float32,
        ).reshape(tile_rows, tile_cols, 2 * width)
        value = jax.nn.sigmoid(block[..., :width]) * block[..., width:] * pair_mask
        return value.astype(jnp.bfloat16)

    right_ops = gated(2)
    from_left, from_right = {0: right_ops}, {0: right_ops}
    for step in range(1, outer):
        from_left[step] = along_line(from_left[step - 1], 1, range(step, outer))
        from_right[step] = along_line(from_right[step - 1], -1, range(0, outer - step))
    left_ops = gated(0)
    left_other = lax.ppermute(left_ops, "row", [(i, i ^ 1) for i in range(row_count)])
    lefts = jnp.concatenate([left_ops, left_other], axis=0)

    partials = []
    for source in range(outer):
        block = right_ops
        for step in range(1, outer):
            if source + step < outer:
                block = jnp.where(line_id == source + step, from_left[step], block)
            if source - step >= 0:
                block = jnp.where(line_id == source - step, from_right[step], block)
        partials.append(
            jnp.einsum("ikc,jkc->ijc", lefts, block, preferred_element_type=jnp.float32)
        )
    partial = jnp.stack(partials)
    share = outer // col_count
    mine = lax.dynamic_slice_in_dim(partial, col_id * share, share, 0)
    for hop in range(1, col_count):
        target = (col_id + hop) % col_count
        passed = lax.dynamic_slice_in_dim(partial, target * share, share, 0)
        mine = mine + lax.ppermute(
            passed, "col", [(c, (c + hop) % col_count) for c in range(col_count)]
        )
    tri_normed = layer_norm(mine).astype(jnp.bfloat16)
    own_part = tri_normed[:, :tile_rows]
    other_part = lax.ppermute(
        tri_normed[:, tile_rows:], "row", [(i, i ^ 1) for i in range(row_count)]
    )
    even = row_id % 2 == 0
    both = jnp.stack(
        [jnp.where(even, own_part, other_part), jnp.where(even, other_part, own_part)], axis=1
    )
    tri_normed = both.transpose(2, 0, 1, 3, 4).reshape(-1, width)

    out_gate = jax.nn.sigmoid(
        jnp.dot(normed, in_weight[:, 4 * width :], preferred_element_type=jnp.float32)
    )
    update = jnp.dot(tri_normed, out_weight, preferred_element_type=jnp.float32)
    updated = pair.astype(jnp.float32).reshape(-1, width) + out_gate * update
    trans_normed = layer_norm(updated).astype(jnp.bfloat16)
    expanded = jnp.dot(trans_normed, trans_in, preferred_element_type=jnp.float32)
    hidden = (jax.nn.silu(expanded[:, :hidden_units]) * expanded[:, hidden_units:]).astype(
        jnp.bfloat16
    )
    result = updated + jnp.dot(hidden, trans_out, preferred_element_type=jnp.float32)
    return result.reshape(tile_rows, tile_cols, width).astype(jnp.bfloat16)


def per_device(pair, chain_lengths, in_weight, out_weight, trans_in, trans_out):
    if (lax.axis_size("row"), lax.axis_size("col")) != (8, 2):
        return any_mesh(pair, chain_lengths, in_weight, out_weight, trans_in, trans_out)
    return two_by_four(pair, chain_lengths, in_weight, out_weight, trans_in, trans_out)


def two_by_four(pair, chain_lengths, in_weight, out_weight, trans_in, trans_out):
    tile_rows, tile_cols, width = pair.shape
    half = tile_rows // 2
    tokens = tile_rows * lax.axis_size("row")
    valid_count = tokens - chain_lengths[chain_lengths.shape[0] - 1]
    row_id, core = lax.axis_index("row"), lax.axis_index("col")
    place, side = row_id // 2, row_id % 2
    keeper = place // 2

    def among(value, moves):
        return lax.ppermute(value, "row", [(2 * s + b, 2 * t + b) for s, t in moves for b in range(2)])

    def across(value):
        return lax.ppermute(value, "row", [(i, i ^ 1) for i in range(8)])

    def to_core(value, places, keep):
        perm = []
        for z, towards in zip(places, keep):
            target = z // 2 if towards else 1 - z // 2
            perm += [(4 * z + 2 * b + 1 - target, 4 * z + 2 * b + target) for b in range(2)]
        return lax.ppermute(value, ("row", "col"), perm)

    def give_back(value, swap):
        perm = []
        for s, t in ((1, 0), (2, 3)):
            away = 1 - t // 2
            source = 1 - away if swap else away
            perm += [(4 * s + 2 * b + source, 4 * t + 2 * (b ^ swap) + away) for b in range(2)]
        return lax.ppermute(value, ("row", "col"), perm)

    def side_to_side(value, places, holders):
        perm = []
        for z, holder in zip(places, holders):
            perm += [(4 * z + 2 * b + holder, 4 * z + 2 * (1 - b) + holder) for b in range(2)]
        return lax.ppermute(value, ("row", "col"), perm)

    def by_side(block, axis):
        return jnp.where(side == 0, block, jnp.roll(block, width // 2, axis))

    def after(value, *others):
        return lax.optimization_barrier((value, *others))[0]

    def scalars(*values):
        return jnp.stack([jnp.asarray(v).astype(jnp.int32) for v in values])

    is_keeper = core == keeper
    inner = (place == 1) | (place == 2)
    where = scalars(valid_count, row_id * tile_rows, core * tile_cols, side)
    folded = pair.reshape(2, half, tile_cols, width)
    cross = [(1, 2), (2, 1)]
    everyone, inners = range(4), (1, 2)

    def phase(moves, finished):
        values = lax.optimization_barrier(tuple(v for _, v in moves) + tuple(finished))
        return [send(v) for (send, _), v in zip(moves, values)]

    def hop(moves):
        return lambda value: among(value, moves)

    def either(at_inner, at_end):
        return jnp.where(inner, at_inner, at_end)

    swap = hop([(0, 1), (1, 0), (2, 3), (3, 2)])
    right_own, right_far = project(where, folded, in_weight, 2)
    one = phase([(swap, right_own), (hop(cross), right_own), (across, right_far)], ())
    mate_own, near_own, right_beside = one
    order = jnp.where(is_keeper, place % 2, place // 2)
    weights = [
        by_side(out_weight, 0).T * BF16(0.5),
        jnp.where(jnp.arange(trans_in.shape[1])[:, None] < trans_out.shape[0], BF16(0.5), BF16(1.0))
        * trans_in.T,
        trans_out.T,
    ]
    gate_weight = in_weight[:, 4 * width :].T * BF16(0.5)
    left_own, left_far = project(where, folded, in_weight, 0)
    two = phase(
        [(swap, either(near_own, right_beside)), (hop(cross), right_beside), (across, left_far)],
        one + weights + [gate_weight],
    )
    prepared = [prepare(scalars(f), after(folded, *one), gate_weight) for f in (order, 1 - order)]
    mate_beside, near_beside, left_beside = two
    three = phase(
        [(swap, either(near_beside, left_own)), (hop(cross), mate_own)],
        (near_beside, left_beside, *prepared[0], *prepared[1]),
    )
    guest_own, far_own = three

    left = left_major(left_own, left_beside)
    plain, outer = scalars(side, 0), scalars(side, jnp.where(inner, 0, 1))
    (home,) = triangle(plain, left, [[right_own], [right_beside]])
    home_rest = to_core(home, everyone, [True] * 4)
    (mate,) = triangle(plain, left, [[mate_own], [mate_beside]])
    mate_rest = to_core(mate, inners, [True] * 2)
    four = phase(
        [(swap, either(right_beside, left_beside)), (hop(cross), mate_beside)], three + [home, mate]
    )
    guest_beside, far_beside = four

    (away,) = triangle(
        outer,
        left,
        [[after(near_own, far_own, mate)], [near_beside], [mate_beside], [guest_own]],
    )
    away_rest = to_core(away, everyone, [False] * 4)
    role = scalars(jnp.where(is_keeper, 0, 1))
    first = fold(half, role, home, home_rest, away, away_rest)
    first_other = across(first[1])
    mate_block = fold(half, role, mate, mate_rest)
    mate_other = side_to_side(mate_block[1], inners, (0, 1))

    late, lent_own, lent_beside = triangle(
        outer,
        left,
        [[after(far_own, mate_other)], [far_beside], [mate_own], [guest_beside]],
        [[guest_own], [guest_beside]],
    )
    lent_rest = to_core(lent_own, inners, [False] * 2), to_core(lent_beside, inners, [True] * 2)
    late_rest = to_core(late, everyone, [True, False, False, True])
    (lent,) = fold(half, role, lent_beside, lent_rest[1], lent_own, lent_rest[0])
    given = give_back(lent, 0), give_back(lent, 1)
    late_block = fold(half, role, late, late_rest)
    late_other = side_to_side(late_block[1], everyone, (0, 1, 0, 1))

    earlier = finish(
        scalars(order), tile_cols, prepared[0], after(first[0], lent), first_other, weights
    )
    own, other = (
        jnp.where(inner & is_keeper, early, jnp.where(inner | is_keeper, end, back))
        for early, end, back in zip((mate_block[0], mate_other), (late_block[0], late_other), given)
    )
    result = finish(scalars(1 - order), tile_cols, prepared[1], own, other, weights, earlier)
    return result.reshape(tile_rows, tile_cols, width)


def solution(mesh):
    placed = (P(("crops", "row"), "col", None), P("crops"), P(), P(), P(), P())
    return jax.shard_map(
        per_device,
        mesh=mesh,
        in_specs=placed,
        out_specs=P(("crops", "row"), "col", None),
        check_vma=False,
    )
```

```python
import functools

import jax
import jax.numpy as jnp
from jax import lax
from jax.experimental import pallas as pl
from jax.experimental.pallas import tpu as pltpu
from jax.sharding import PartitionSpec as P

VMEM = pltpu.VMEM
BF16, F32 = jnp.bfloat16, jnp.float32
CHUNK = 16


def whole(count):
    return [pl.BlockSpec(memory_space=VMEM)] * count


def params():
    return pltpu.CompilerParams(vmem_limit_bytes=20 << 20)


def cost(flops, moved, transcendentals=0):
    return pl.CostEstimate(flops=flops, bytes_accessed=moved, transcendentals=transcendentals)


def twice_sigmoid(halved):
    return jnp.tanh(halved) + 1.0


def norm_chans(values):
    centered = values - jnp.mean(values, axis=0, keepdims=True)
    variance = jnp.mean(centered * centered, axis=0, keepdims=True)
    return centered * lax.rsqrt(variance + 1e-05)


def padded(count, unit):
    return -(-count // unit) * unit


def project_kernel(where_ref, pair_hbm, weight_ref, own_ref, far_ref, pair_ref, both_ref, sems, first):
    valid, row0, col0, side = (where_ref[i] for i in range(4))
    _, half, cols, width = pair_ref.shape
    chans = width // 2
    tail = cols - width
    count = sems.shape[0]
    size = -(-half // count)
    spans = [(k * size, min(size, half - k * size)) for k in range(count)]
    loads = [
        pltpu.make_async_copy(
            pair_hbm.at[:, pl.ds(start, length)], pair_ref.at[:, pl.ds(start, length)], sems.at[k]
        )
        for k, (start, length) in enumerate(spans)
    ]
    for load in loads:
        load.start()

    for i in range(2):
        block = weight_ref[:, (first + i) * width : (first + i + 1) * width].astype(F32)
        block = jnp.where(side == 0, block, pltpu.roll(block, chans, 1))
        both_ref[i * width : (i + 1) * width] = (block.T * 0.5).astype(BF16)

    lane = lax.broadcasted_iota(jnp.int32, (1, 3 * width), 1)
    in_tail = lane >= 2 * width
    ends = jnp.where(in_tail, 2 * width + chans, width)
    is_first = jnp.where(lane < ends, 1, 0)
    token = jnp.where(in_tail, lane % chans + width, lane % width) + col0
    gap = jnp.zeros((chans - tail, width), F32)

    def step(r, carry):
        first, second = (pair_ref[h, r].astype(F32) for h in range(2))
        tokens = jnp.concatenate(
            [first[:width], second[:width], first[width:], gap, second[width:], gap], axis=0
        )
        normed = norm_chans(tokens.T).astype(BF16)
        both = jnp.dot(both_ref[...], normed, preferred_element_type=F32)
        limits = [jnp.where(row0 + h * half + r < valid, valid, 0) for h in range(2)]
        keep = jnp.where(token < limits[1] + is_first * (limits[0] - limits[1]), 1.0, 0.0)
        out = (twice_sigmoid(both[:width]) * both[width:] * keep).astype(BF16)
        own_ref[r] = out[:chans]
        far_ref[r] = out[chans:]
        return carry

    for load, (start, length) in zip(loads, spans):
        load.wait()
        lax.fori_loop(start, start + length, step, 0, unroll=3)


def project(where, pair, weight, first):
    _, half, cols, width = pair.shape
    piece = jax.ShapeDtypeStruct((half, width // 2, 3 * width), BF16)
    return pl.pallas_call(
        functools.partial(project_kernel, first=first),
        out_shape=(piece, piece),
        in_specs=[
            pl.BlockSpec(memory_space=pltpu.SMEM),
            pl.BlockSpec(memory_space=pl.ANY),
            pl.BlockSpec(memory_space=VMEM),
        ],
        out_specs=whole(2),
        scratch_shapes=[
            VMEM(pair.shape, BF16),
            VMEM((2 * width, width), BF16),
            pltpu.SemaphoreType.DMA((4,)),
        ],
        compiler_params=params(),
        cost_estimate=cost(4 * pair.size * width, 4 * pair.size, pair.size),
        name="project",
    )(where, pair, weight)


def channel_major(pieces, left):
    half, chans, lanes = pieces[0].shape
    width = lanes // 3
    main, rest = [], []
    for piece in pieces:
        tail = piece[:, :, 2 * width :]
        turned = jnp.concatenate([tail[:, :, width // 2 :], tail[:, :, : width // 2]], axis=2)
        main += [piece[:, :, :width], piece[:, :, width : 2 * width]]
        rest += [tail, turned]
        if left:
            gap = jnp.zeros((padded(2 * half, 16) - 2 * half, chans, width), BF16)
            main.append(gap)
            rest.append(gap)
    rest = jnp.concatenate(rest, axis=0)
    if left:
        low = lax.broadcasted_iota(jnp.int32, rest.shape, 2) < width // 2
        rest = jnp.where(low, rest, jnp.zeros_like(rest))
    main = jnp.swapaxes(jnp.concatenate(main, axis=0), 0, 1)
    return main, jnp.swapaxes(rest, 0, 1)


def left_kernel(own_ref, beside_ref, out_ref):
    width = own_ref.shape[2] // 3
    main, rest = channel_major([own_ref[...], beside_ref[...]], True)
    out_ref[:, :, :width] = main
    out_ref[:, :, width:] = rest


def left_major(own, beside):
    half, chans, lanes = own.shape
    rows, deep = 2 * padded(2 * half, 16), lanes // 3 * 2
    piece = pl.BlockSpec((half, CHUNK, lanes), lambda c: (0, c, 0))
    return pl.pallas_call(
        left_kernel,
        grid=(chans // CHUNK,),
        out_shape=jax.ShapeDtypeStruct((chans, rows, deep), BF16),
        in_specs=[piece, piece],
        out_specs=pl.BlockSpec((CHUNK, rows, deep), lambda c: (c, 0, 0)),
        compiler_params=params(),
        cost_estimate=cost(0, 8 * own.size),
        name="left_major",
    )(own, beside)


def triangle_kernel(flag_ref, left_ref, *refs, counts, guests, options):
    pieces, refs = [], list(refs)
    for count in counts:
        parts = [refs.pop(0)[...] for _ in range(count)]
        pieces.append(parts[0] if count == 1 else jnp.concatenate(parts, axis=0))
    outs, work = refs[: 1 + guests], refs[1 + guests :]
    visitors, rights = pieces[:guests], pieces[guests:]
    own, beside = rights[:2]
    if options == 2:
        plain = flag_ref[1] == 0
        own = jnp.where(plain, own, rights[2])
        beside = jnp.where(plain, beside, rights[3])
    width = own.shape[2] // 3
    even = flag_ref[0] == 0
    right_ref = work[0]
    main, rest = channel_major(
        [jnp.where(even, own, beside), jnp.where(even, beside, own)], False
    )
    rows = main.shape[1]

    @pl.when(pl.program_id(0) == 0)
    def _():
        right_ref[...] = jnp.zeros_like(right_ref)

    right_ref[:, :rows, :width] = main
    right_ref[:, :rows, width:] = rest
    if guests:
        guest_ref = work[1]
        main, rest = channel_major(visitors, True)
        guest_ref[:, :, :width] = main
        guest_ref[:, :, width:] = rest

    def product(rows):
        dims = (((1,), (1,)), ((), ()))
        return lax.dot_general(rows, right_ref[c], dims, preferred_element_type=F32).astype(BF16)

    for c in range(CHUNK):
        outs[0][c] = product(left_ref[c])
        if guests:
            lent = product(guest_ref[c])
            part = lent.shape[0] // guests
            for g in range(guests):
                outs[1 + g][c] = lent[g * part : (g + 1) * part]


def triangle(flags, left, pieces, guests=()):
    chans, rows, deep = left.shape
    lanes, half = deep // 2 * 3, sum(part.shape[0] for part in pieces[0])
    options, cols = len(pieces) // 2, padded(4 * half, 128)

    def spec(part, option):
        def at(c, flag_ref):
            return (0, c if option is None else jnp.where(flag_ref[1] == option, c, 0), 0)

        return pl.BlockSpec((part.shape[0], CHUNK, lanes), at)

    def block(height, depth):
        return pl.BlockSpec((CHUNK, height, depth), lambda c, flag_ref: (c, 0, 0))

    specs = [spec(part, None) for piece in guests for part in piece]
    for i, piece in enumerate(pieces):
        specs += [spec(part, i // 2 if options == 2 else None) for part in piece]
    heights = [rows] + [rows // 2] * len(guests)
    work = [VMEM((CHUNK, cols, deep), BF16)]
    if guests:
        work.append(VMEM((CHUNK, rows, deep), BF16))
    everything = list(guests) + list(pieces)
    return pl.pallas_call(
        functools.partial(
            triangle_kernel,
            counts=[len(piece) for piece in everything],
            guests=len(guests),
            options=options,
        ),
        grid_spec=pltpu.PrefetchScalarGridSpec(
            num_scalar_prefetch=1,
            grid=(chans // CHUNK,),
            in_specs=[block(rows, deep)] + specs,
            out_specs=[block(h, cols) for h in heights],
            scratch_shapes=work,
        ),
        out_shape=[jax.ShapeDtypeStruct((chans, h, cols), BF16) for h in heights],
        compiler_params=params(),
        cost_estimate=cost(2 * chans * sum(heights) * cols * deep, 10 * half * chans * lanes),
        name="triangle",
    )(flags, left, *[part for piece in everything for part in piece])


def fold_kernel(role_ref, *refs, outputs, half):
    outs, work_ref = refs[-1 - outputs : -1], refs[-1]
    cols = outs[0].shape[1]
    parts = refs[: -1 - outputs]
    c = pl.program_id(0)
    options = len(parts) // 2
    for option in range(options):

        @pl.when((options == 1) | (role_ref[0] == option))
        def _(option=option):
            total = parts[2 * option][...].astype(F32) + parts[2 * option + 1][...].astype(F32)
            at = pl.ds(pl.multiple_of(c * CHUNK, CHUNK), CHUNK)
            work_ref[:, at, :] = jnp.swapaxes(total.astype(BF16), 0, 1)

    @pl.when(c == pl.num_programs(0) - 1)
    def _():
        pitch = work_ref.shape[0] // outputs
        for o, out_ref in enumerate(outs):

            def turn(r, carry, o=o, out_ref=out_ref):
                at = o * pitch + r
                stacked = jnp.concatenate([work_ref[at], work_ref[at + half]], axis=0)
                out_ref[r] = stacked.T[:cols]
                return carry

            lax.fori_loop(0, half, turn, 0, unroll=True)


def fold(half, role, *parts):
    chans, rows, cols = parts[0].shape
    outputs = rows // padded(2 * half, 16)
    out = jax.ShapeDtypeStruct((half, padded(4 * half, 16), 2 * chans), BF16)

    def block(option):
        return pl.BlockSpec(
            (CHUNK, rows, cols),
            lambda c, role_ref: (
                c if len(parts) == 2 else jnp.where(role_ref[0] == option, c, 0), 0, 0
            ),
        )

    return pl.pallas_call(
        functools.partial(fold_kernel, outputs=outputs, half=half),
        grid_spec=pltpu.PrefetchScalarGridSpec(
            num_scalar_prefetch=1,
            grid=(chans // CHUNK,),
            in_specs=[block(i // 2) for i in range(len(parts))],
            out_specs=[pl.BlockSpec(out.shape, lambda c, role_ref: (0, 0, 0))] * outputs,
            scratch_shapes=[VMEM((rows, chans, cols), BF16)],
        ),
        out_shape=[out] * outputs,
        compiler_params=params(),
        cost_estimate=cost(0, 6 * parts[0].size),
        name="fold",
    )(role, *parts)


def prepare_kernel(flag_ref, pair_ref, gate_w_ref, pair_out_ref, gate_ref):
    _, half, cols, width = pair_ref.shape
    block = cols // 2
    front = flag_ref[0] == 0

    def step(i, carry):
        first = jnp.minimum(2 * i, half - 2)
        pair = []
        for h, r in [(h, first + e) for h in range(2) for e in range(2)]:
            row = pair_ref[h, r].astype(F32)
            pair.append(jnp.where(front, row[:block], row[block:]))
        pair = jnp.concatenate(pair, axis=0).T
        normed = norm_chans(pair).astype(BF16)
        pair_out_ref[i, :, : 4 * block] = pair.astype(BF16)
        gate = jnp.dot(gate_w_ref[...], normed, preferred_element_type=F32)
        gate_ref[i, :, : 4 * block] = twice_sigmoid(gate)
        return carry

    lax.fori_loop(0, pair_out_ref.shape[0], step, 0, unroll=4)


def prepare(flag, pair, gate_w):
    _, half, cols, width = pair.shape
    shape = ((half + 1) // 2, width, padded(2 * cols, 128))
    return pl.pallas_call(
        prepare_kernel,
        out_shape=(jax.ShapeDtypeStruct(shape, BF16), jax.ShapeDtypeStruct(shape, F32)),
        in_specs=[pl.BlockSpec(memory_space=pltpu.SMEM)] + whole(2),
        out_specs=whole(2),
        compiler_params=params(),
        cost_estimate=cost(pair.size * width, 6 * pair.size, pair.size // 2),
        name="prepare",
    )(flag, pair, gate_w)


def finish_kernel(flag_ref, pair_ref, gate_ref, own_ref, *refs, cols, sources):
    other_refs, refs = refs[:sources], refs[sources:]
    out_w_ref, in_ref, back_ref = refs[:3]
    earlier_ref, out_ref = refs[3] if len(refs) == 5 else None, refs[-1]
    steps, width, _ = pair_ref.shape
    half = own_ref.shape[0]
    block, chans = cols // 2, width // 2
    hidden_units = back_ref.shape[1]
    front = flag_ref[0] == 0

    def step(i, carry):
        first = jnp.minimum(2 * i, half - 2)
        rows = [(h, first + e) for h in range(2) for e in range(2)]
        others = [sum(ref[first + e] for ref in other_refs) for e in range(2)]
        turned = [[v.T[:, :block] for v in (own_ref[first + e], others[e])] for e in range(2)]
        tri = [
            jnp.concatenate([t[h * chans : (h + 1) * chans] for t in turned[e]], axis=0)
            for h in range(2)
            for e in range(2)
        ]
        tri_normed = norm_chans(jnp.concatenate(tri, axis=1).astype(F32)).astype(BF16)
        pair = pair_ref[i, :, : 4 * block].astype(F32)
        update = jnp.dot(out_w_ref[...], tri_normed, preferred_element_type=F32)
        updated = pair + gate_ref[i, :, : 4 * block] * update
        trans_normed = norm_chans(updated).astype(BF16)
        expanded = jnp.dot(in_ref[...], trans_normed, preferred_element_type=F32)
        swish, linear = expanded[:hidden_units], expanded[hidden_units:]
        hidden = (swish * twice_sigmoid(swish) * linear).astype(BF16)
        result = updated + jnp.dot(back_ref[...], hidden, preferred_element_type=F32)
        result = result.T
        for s, (h, r) in enumerate(rows):
            mine = result[s * block : (s + 1) * block]
            if earlier_ref is None:
                out_ref[h, r, :block] = mine.astype(BF16)
            else:
                past = earlier_ref[h, r].astype(F32)[:block]
                parts = [jnp.where(front, mine, past), jnp.where(front, past, mine)]
                out_ref[h, r] = jnp.concatenate(parts, axis=0).astype(BF16)
        return carry

    lax.fori_loop(0, steps, step, 0, unroll=6)


def finish(flag, cols, prepared, own, others, weights, earlier=None):
    half, _, width = own.shape
    shape = (2, half, padded(cols // 2, 16) if earlier is None else cols, width)
    extra = [] if earlier is None else [earlier]
    size = own.size * 2
    return pl.pallas_call(
        functools.partial(finish_kernel, cols=cols, sources=len(others)),
        out_shape=jax.ShapeDtypeStruct(shape, BF16),
        in_specs=[pl.BlockSpec(memory_space=pltpu.SMEM)] + whole(6 + len(others) + len(extra)),
        out_specs=pl.BlockSpec(memory_space=VMEM),
        compiler_params=params(),
        cost_estimate=cost(26 * size * width, 10 * size, 5 * size),
        name="finish",
    )(flag, *prepared, own, *others, *weights, *extra)


def layer_norm(values):
    centered = values - jnp.mean(values, axis=-1, keepdims=True)
    variance = jnp.mean(centered * centered, axis=-1, keepdims=True)
    return centered * lax.rsqrt(variance + 1e-05)


def any_mesh(pair, chain_lengths, in_weight, out_weight, trans_in, trans_out):
    tile_rows, tile_cols, width = pair.shape
    hidden_units = trans_out.shape[0]
    row_count = lax.axis_size("row")
    col_count = lax.axis_size("col")
    outer = row_count // 2
    tokens = tile_rows * row_count
    valid_count = tokens - chain_lengths[chain_lengths.shape[0] - 1]
    row_id = lax.axis_index("row")
    col_id = lax.axis_index("col")
    line_id = row_id // 2

    def along_line(value, step, targets):
        perm = [(2 * (t - step) + b, 2 * t + b) for t in targets for b in range(2)]
        return lax.ppermute(value, "row", perm)

    row_pos = row_id * tile_rows + jnp.arange(tile_rows, dtype=jnp.int32)
    col_pos = col_id * tile_cols + jnp.arange(tile_cols, dtype=jnp.int32)
    pair_mask = ((row_pos < valid_count)[:, None] & (col_pos < valid_count)[None, :]).astype(
        jnp.float32
    )[:, :, None]
    normed = layer_norm(pair.astype(jnp.float32)).astype(jnp.bfloat16).reshape(-1, width)

    def gated(offset):
        block = jnp.dot(
            normed,
            in_weight[:, offset * width : (offset + 2) * width],
            preferred_element_type=jnp.float32,
        ).reshape(tile_rows, tile_cols, 2 * width)
        value = jax.nn.sigmoid(block[..., :width]) * block[..., width:] * pair_mask
        return value.astype(jnp.bfloat16)

    right_ops = gated(2)
    from_left, from_right = {0: right_ops}, {0: right_ops}
    for step in range(1, outer):
        from_left[step] = along_line(from_left[step - 1], 1, range(step, outer))
        from_right[step] = along_line(from_right[step - 1], -1, range(0, outer - step))
    left_ops = gated(0)
    left_other = lax.ppermute(left_ops, "row", [(i, i ^ 1) for i in range(row_count)])
    lefts = jnp.concatenate([left_ops, left_other], axis=0)

    partials = []
    for source in range(outer):
        block = right_ops
        for step in range(1, outer):
            if source + step < outer:
                block = jnp.where(line_id == source + step, from_left[step], block)
            if source - step >= 0:
                block = jnp.where(line_id == source - step, from_right[step], block)
        partials.append(
            jnp.einsum("ikc,jkc->ijc", lefts, block, preferred_element_type=jnp.float32)
        )
    partial = jnp.stack(partials)
    share = outer // col_count
    mine = lax.dynamic_slice_in_dim(partial, col_id * share, share, 0)
    for hop in range(1, col_count):
        target = (col_id + hop) % col_count
        passed = lax.dynamic_slice_in_dim(partial, target * share, share, 0)
        mine = mine + lax.ppermute(
            passed, "col", [(c, (c + hop) % col_count) for c in range(col_count)]
        )
    tri_normed = layer_norm(mine).astype(jnp.bfloat16)
    own_part = tri_normed[:, :tile_rows]
    other_part = lax.ppermute(
        tri_normed[:, tile_rows:], "row", [(i, i ^ 1) for i in range(row_count)]
    )
    even = row_id % 2 == 0
    both = jnp.stack(
        [jnp.where(even, own_part, other_part), jnp.where(even, other_part, own_part)], axis=1
    )
    tri_normed = both.transpose(2, 0, 1, 3, 4).reshape(-1, width)

    out_gate = jax.nn.sigmoid(
        jnp.dot(normed, in_weight[:, 4 * width :], preferred_element_type=jnp.float32)
    )
    update = jnp.dot(tri_normed, out_weight, preferred_element_type=jnp.float32)
    updated = pair.astype(jnp.float32).reshape(-1, width) + out_gate * update
    trans_normed = layer_norm(updated).astype(jnp.bfloat16)
    expanded = jnp.dot(trans_normed, trans_in, preferred_element_type=jnp.float32)
    hidden = (jax.nn.silu(expanded[:, :hidden_units]) * expanded[:, hidden_units:]).astype(
        jnp.bfloat16
    )
    result = updated + jnp.dot(hidden, trans_out, preferred_element_type=jnp.float32)
    return result.reshape(tile_rows, tile_cols, width).astype(jnp.bfloat16)


def per_device(pair, chain_lengths, in_weight, out_weight, trans_in, trans_out):
    if (lax.axis_size("row"), lax.axis_size("col")) != (8, 2):
        return any_mesh(pair, chain_lengths, in_weight, out_weight, trans_in, trans_out)
    return two_by_four(pair, chain_lengths, in_weight, out_weight, trans_in, trans_out)


def two_by_four(pair, chain_lengths, in_weight, out_weight, trans_in, trans_out):
    tile_rows, tile_cols, width = pair.shape
    half = tile_rows // 2
    tokens = tile_rows * lax.axis_size("row")
    valid_count = tokens - chain_lengths[chain_lengths.shape[0] - 1]
    row_id, core = lax.axis_index("row"), lax.axis_index("col")
    place, side = row_id // 2, row_id % 2
    keeper = place // 2

    def among(value, moves):
        return lax.ppermute(value, "row", [(2 * s + b, 2 * t + b) for s, t in moves for b in range(2)])

    def across(value):
        return lax.ppermute(value, "row", [(i, i ^ 1) for i in range(8)])

    def to_core(value, places, keep):
        perm = []
        for z, towards in zip(places, keep):
            target = z // 2 if towards else 1 - z // 2
            perm += [(4 * z + 2 * b + 1 - target, 4 * z + 2 * b + target) for b in range(2)]
        return lax.ppermute(value, ("row", "col"), perm)

    def give_back(value, swap):
        perm = []
        for s, t in ((1, 0), (2, 3)):
            away = 1 - t // 2
            source = 1 - away if swap else away
            perm += [(4 * s + 2 * b + source, 4 * t + 2 * (b ^ swap) + away) for b in range(2)]
        return lax.ppermute(value, ("row", "col"), perm)

    def side_to_side(value, places, holders):
        perm = []
        for z, holder in zip(places, holders):
            perm += [(4 * z + 2 * b + holder, 4 * z + 2 * (1 - b) + holder) for b in range(2)]
        return lax.ppermute(value, ("row", "col"), perm)

    def by_side(block, axis):
        return jnp.where(side == 0, block, jnp.roll(block, width // 2, axis))

    def after(value, *others):
        return lax.optimization_barrier((value, *others))[0]

    def scalars(*values):
        return jnp.stack([jnp.asarray(v).astype(jnp.int32) for v in values])

    is_keeper = core == keeper
    inner = (place == 1) | (place == 2)
    where = scalars(valid_count, row_id * tile_rows, core * tile_cols, side)
    folded = pair.reshape(2, half, tile_cols, width)
    cross = [(1, 2), (2, 1)]
    everyone, inners = range(4), (1, 2)

    def phase(moves, finished):
        values = lax.optimization_barrier(tuple(v for _, v in moves) + tuple(finished))
        return [send(v) for (send, _), v in zip(moves, values)]

    def hop(moves):
        return lambda value: among(value, moves)

    def either(at_inner, at_end):
        return jnp.where(inner, at_inner, at_end)

    swap = hop([(0, 1), (1, 0), (2, 3), (3, 2)])
    right_own, right_far = project(where, folded, in_weight, 2)
    one = phase([(swap, right_own), (hop(cross), right_own), (across, right_far)], ())
    mate_own, near_own, right_beside = one
    order = jnp.where(is_keeper, place % 2, place // 2)
    weights = [
        by_side(out_weight, 0).T * BF16(0.5),
        jnp.where(jnp.arange(trans_in.shape[1])[:, None] < trans_out.shape[0], BF16(0.5), BF16(1.0))
        * trans_in.T,
        trans_out.T,
    ]
    gate_weight = in_weight[:, 4 * width :].T * BF16(0.5)
    left_own, left_far = project(where, folded, in_weight, 0)
    two = phase(
        [(swap, either(near_own, right_beside)), (hop(cross), right_beside), (across, left_far)],
        one + weights + [gate_weight],
    )
    prepared = [prepare(scalars(f), after(folded, *one), gate_weight) for f in (order, 1 - order)]
    mate_beside, near_beside, left_beside = two
    three = phase(
        [(swap, either(near_beside, left_own)), (hop(cross), mate_own)],
        (near_beside, left_beside, *prepared[0], *prepared[1]),
    )
    guest_own, far_own = three

    left = left_major(left_own, left_beside)
    plain, outer = scalars(side, 0), scalars(side, jnp.where(inner, 0, 1))
    (home,) = triangle(plain, left, [[right_own], [right_beside]])
    home_rest = to_core(home, everyone, [True] * 4)
    (mate,) = triangle(plain, left, [[mate_own], [mate_beside]])
    mate_rest = to_core(mate, inners, [True] * 2)
    four = phase(
        [(swap, either(right_beside, left_beside)), (hop(cross), mate_beside)], three + [home, mate]
    )
    guest_beside, far_beside = four

    (away,) = triangle(
        outer,
        left,
        [[after(near_own, far_own, mate)], [near_beside], [mate_beside], [guest_own]],
    )
    away_rest = to_core(away, everyone, [False] * 4)
    role = scalars(jnp.where(is_keeper, 0, 1))
    first = fold(half, role, home, home_rest, away, away_rest)
    first_other = across(first[1])
    mate_block = fold(half, role, mate, mate_rest)
    mate_other = side_to_side(mate_block[1], inners, (0, 1))

    late, lent_own, lent_beside = triangle(
        outer,
        left,
        [[after(far_own, mate_other)], [far_beside], [mate_own], [guest_beside]],
        [[guest_own], [guest_beside]],
    )
    lent_rest = to_core(lent_own, inners, [False] * 2), to_core(lent_beside, inners, [True] * 2)
    late_rest = to_core(late, everyone, [True, False, False, True])
    (lent,) = fold(half, role, lent_beside, lent_rest[1], lent_own, lent_rest[0])
    given = give_back(lent, 0), give_back(lent, 1)
    late_block = fold(half, role, late, late_rest)
    late_other = side_to_side(late_block[1], everyone, (0, 1, 0, 1))

    earlier = finish(
        scalars(order), tile_cols, prepared[0], after(first[0], lent), [first_other], weights
    )
    own = jnp.where(
        inner & is_keeper, mate_block[0], jnp.where(inner | is_keeper, late_block[0], given[0])
    )
    others = [mate_other, late_other, given[1]]
    result = finish(scalars(1 - order), tile_cols, prepared[1], own, others, weights, earlier)
    return result.reshape(tile_rows, tile_cols, width)


def solution(mesh):
    placed = (P(("crops", "row"), "col", None), P("crops"), P(), P(), P(), P())
    return jax.shard_map(
        per_device,
        mesh=mesh,
        in_specs=placed,
        out_specs=P(("crops", "row"), "col", None),
        check_vma=False,
    )
```

```python
import functools

import jax
import jax.numpy as jnp
from jax import lax
from jax.experimental import pallas as pl
from jax.experimental.pallas import tpu as pltpu
from jax.sharding import PartitionSpec as P

VMEM = pltpu.VMEM
BF16, F32 = jnp.bfloat16, jnp.float32
CHUNK = 16


def whole(count):
    return [pl.BlockSpec(memory_space=VMEM)] * count


def params():
    return pltpu.CompilerParams(vmem_limit_bytes=20 << 20)


def cost(flops, moved, transcendentals=0):
    return pl.CostEstimate(flops=flops, bytes_accessed=moved, transcendentals=transcendentals)


def twice_sigmoid(halved):
    return jnp.tanh(halved) + 1.0


def norm_chans(values):
    centered = values - jnp.mean(values, axis=0, keepdims=True)
    variance = jnp.mean(centered * centered, axis=0, keepdims=True)
    return centered * lax.rsqrt(variance + 1e-05)


def padded(count, unit):
    return -(-count // unit) * unit


def project_kernel(where_ref, pair_hbm, weight_ref, own_ref, far_ref, pair_ref, both_ref, sems, first):
    valid, row0, col0, side = (where_ref[i] for i in range(4))
    _, half, cols, width = pair_ref.shape
    chans = width // 2
    tail = cols - width
    count = sems.shape[0]
    size = -(-half // count)
    spans = [(k * size, min(size, half - k * size)) for k in range(count)]
    loads = [
        pltpu.make_async_copy(
            pair_hbm.at[:, pl.ds(start, length)], pair_ref.at[:, pl.ds(start, length)], sems.at[k]
        )
        for k, (start, length) in enumerate(spans)
    ]
    for load in loads:
        load.start()

    for i in range(2):
        block = weight_ref[:, (first + i) * width : (first + i + 1) * width].astype(F32)
        block = jnp.where(side == 0, block, pltpu.roll(block, chans, 1))
        both_ref[i * width : (i + 1) * width] = (block.T * 0.5).astype(BF16)

    lane = lax.broadcasted_iota(jnp.int32, (1, 3 * width), 1)
    in_tail = lane >= 2 * width
    ends = jnp.where(in_tail, 2 * width + chans, width)
    is_first = jnp.where(lane < ends, 1, 0)
    token = jnp.where(in_tail, lane % chans + width, lane % width) + col0
    gap = jnp.zeros((chans - tail, width), F32)

    def step(r, carry):
        first, second = (pair_ref[h, r].astype(F32) for h in range(2))
        tokens = jnp.concatenate(
            [first[:width], second[:width], first[width:], gap, second[width:], gap], axis=0
        )
        normed = norm_chans(tokens.T).astype(BF16)
        both = jnp.dot(both_ref[...], normed, preferred_element_type=F32)
        limits = [jnp.where(row0 + h * half + r < valid, valid, 0) for h in range(2)]
        keep = jnp.where(token < limits[1] + is_first * (limits[0] - limits[1]), 1.0, 0.0)
        out = (twice_sigmoid(both[:width]) * both[width:] * keep).astype(BF16)
        own_ref[r] = out[:chans]
        far_ref[r] = out[chans:]
        return carry

    for load, (start, length) in zip(loads, spans):
        load.wait()
        lax.fori_loop(start, start + length, step, 0, unroll=3)


def project(where, pair, weight, first):
    _, half, cols, width = pair.shape
    piece = jax.ShapeDtypeStruct((half, width // 2, 3 * width), BF16)
    return pl.pallas_call(
        functools.partial(project_kernel, first=first),
        out_shape=(piece, piece),
        in_specs=[
            pl.BlockSpec(memory_space=pltpu.SMEM),
            pl.BlockSpec(memory_space=pl.ANY),
            pl.BlockSpec(memory_space=VMEM),
        ],
        out_specs=whole(2),
        scratch_shapes=[
            VMEM(pair.shape, BF16),
            VMEM((2 * width, width), BF16),
            pltpu.SemaphoreType.DMA((4,)),
        ],
        compiler_params=params(),
        cost_estimate=cost(4 * pair.size * width, 4 * pair.size, pair.size),
        name="project",
    )(where, pair, weight)


def channel_major(pieces, left):
    half, chans, lanes = pieces[0].shape
    width = lanes // 3
    main, rest = [], []
    for piece in pieces:
        tail = piece[:, :, 2 * width :]
        turned = jnp.concatenate([tail[:, :, width // 2 :], tail[:, :, : width // 2]], axis=2)
        main += [piece[:, :, :width], piece[:, :, width : 2 * width]]
        rest += [tail, turned]
        if left:
            gap = jnp.zeros((padded(2 * half, 16) - 2 * half, chans, width), BF16)
            main.append(gap)
            rest.append(gap)
    rest = jnp.concatenate(rest, axis=0)
    if left:
        low = lax.broadcasted_iota(jnp.int32, rest.shape, 2) < width // 2
        rest = jnp.where(low, rest, jnp.zeros_like(rest))
    main = jnp.swapaxes(jnp.concatenate(main, axis=0), 0, 1)
    return main, jnp.swapaxes(rest, 0, 1)


def left_kernel(own_ref, beside_ref, out_ref):
    width = own_ref.shape[2] // 3
    main, rest = channel_major([own_ref[...], beside_ref[...]], True)
    out_ref[:, :, :width] = main
    out_ref[:, :, width:] = rest


def left_major(own, beside):
    half, chans, lanes = own.shape
    rows, deep = 2 * padded(2 * half, 16), lanes // 3 * 2
    piece = pl.BlockSpec((half, CHUNK, lanes), lambda c: (0, c, 0))
    return pl.pallas_call(
        left_kernel,
        grid=(chans // CHUNK,),
        out_shape=jax.ShapeDtypeStruct((chans, rows, deep), BF16),
        in_specs=[piece, piece],
        out_specs=pl.BlockSpec((CHUNK, rows, deep), lambda c: (c, 0, 0)),
        compiler_params=params(),
        cost_estimate=cost(0, 8 * own.size),
        name="left_major",
    )(own, beside)


def triangle_kernel(flag_ref, left_ref, *refs, counts, guests, options):
    pieces, refs = [], list(refs)
    for count in counts:
        parts = [refs.pop(0)[...] for _ in range(count)]
        pieces.append(parts[0] if count == 1 else jnp.concatenate(parts, axis=0))
    outs, work = refs[: 1 + guests], refs[1 + guests :]
    visitors, rights = pieces[:guests], pieces[guests:]
    own, beside = rights[:2]
    if options == 2:
        plain = flag_ref[1] == 0
        own = jnp.where(plain, own, rights[2])
        beside = jnp.where(plain, beside, rights[3])
    width = own.shape[2] // 3
    even = flag_ref[0] == 0
    right_ref = work[0]
    main, rest = channel_major(
        [jnp.where(even, own, beside), jnp.where(even, beside, own)], False
    )
    rows = main.shape[1]

    @pl.when(pl.program_id(0) == 0)
    def _():
        right_ref[...] = jnp.zeros_like(right_ref)

    right_ref[:, :rows, :width] = main
    right_ref[:, :rows, width:] = rest
    if guests:
        guest_ref = work[1]
        main, rest = channel_major(visitors, True)
        guest_ref[:, :, :width] = main
        guest_ref[:, :, width:] = rest

    def product(rows):
        dims = (((1,), (1,)), ((), ()))
        return lax.dot_general(rows, right_ref[c], dims, preferred_element_type=F32).astype(BF16)

    for c in range(CHUNK):
        outs[0][c] = product(left_ref[c])
        if guests:
            lent = product(guest_ref[c])
            part = lent.shape[0] // guests
            for g in range(guests):
                outs[1 + g][c] = lent[g * part : (g + 1) * part]


def triangle(flags, left, pieces, guests=()):
    chans, rows, deep = left.shape
    lanes, half = deep // 2 * 3, sum(part.shape[0] for part in pieces[0])
    options, cols = len(pieces) // 2, padded(4 * half, 128)

    def spec(part, option):
        def at(c, flag_ref):
            return (0, c if option is None else jnp.where(flag_ref[1] == option, c, 0), 0)

        return pl.BlockSpec((part.shape[0], CHUNK, lanes), at)

    def block(height, depth):
        return pl.BlockSpec((CHUNK, height, depth), lambda c, flag_ref: (c, 0, 0))

    specs = [spec(part, None) for piece in guests for part in piece]
    for i, piece in enumerate(pieces):
        specs += [spec(part, i // 2 if options == 2 else None) for part in piece]
    heights = [rows] + [rows // 2] * len(guests)
    work = [VMEM((CHUNK, cols, deep), BF16)]
    if guests:
        work.append(VMEM((CHUNK, rows, deep), BF16))
    everything = list(guests) + list(pieces)
    return pl.pallas_call(
        functools.partial(
            triangle_kernel,
            counts=[len(piece) for piece in everything],
            guests=len(guests),
            options=options,
        ),
        grid_spec=pltpu.PrefetchScalarGridSpec(
            num_scalar_prefetch=1,
            grid=(chans // CHUNK,),
            in_specs=[block(rows, deep)] + specs,
            out_specs=[block(h, cols) for h in heights],
            scratch_shapes=work,
        ),
        out_shape=[jax.ShapeDtypeStruct((chans, h, cols), BF16) for h in heights],
        compiler_params=params(),
        cost_estimate=cost(2 * chans * sum(heights) * cols * deep, 10 * half * chans * lanes),
        name="triangle",
    )(flags, left, *[part for piece in everything for part in piece])


def fold_kernel(role_ref, *refs, outputs, half):
    outs, work_ref = refs[-1 - outputs : -1], refs[-1]
    cols = outs[0].shape[1]
    parts = refs[: -1 - outputs]
    c = pl.program_id(0)
    options = len(parts) // 2
    for option in range(options):

        @pl.when((options == 1) | (role_ref[0] == option))
        def _(option=option):
            total = parts[2 * option][...].astype(F32) + parts[2 * option + 1][...].astype(F32)
            at = pl.ds(pl.multiple_of(c * CHUNK, CHUNK), CHUNK)
            work_ref[:, at, :] = jnp.swapaxes(total.astype(BF16), 0, 1)

    @pl.when(c == pl.num_programs(0) - 1)
    def _():
        pitch = work_ref.shape[0] // outputs
        for o, out_ref in enumerate(outs):

            def turn(r, carry, o=o, out_ref=out_ref):
                at = o * pitch + r
                stacked = jnp.concatenate([work_ref[at], work_ref[at + half]], axis=0)
                out_ref[r] = stacked.T[:cols]
                return carry

            lax.fori_loop(0, half, turn, 0, unroll=True)


def fold(half, role, *parts):
    chans, rows, cols = parts[0].shape
    outputs = rows // padded(2 * half, 16)
    out = jax.ShapeDtypeStruct((half, padded(4 * half, 16), 2 * chans), BF16)

    def block(option):
        return pl.BlockSpec(
            (CHUNK, rows, cols),
            lambda c, role_ref: (
                c if len(parts) == 2 else jnp.where(role_ref[0] == option, c, 0), 0, 0
            ),
        )

    return pl.pallas_call(
        functools.partial(fold_kernel, outputs=outputs, half=half),
        grid_spec=pltpu.PrefetchScalarGridSpec(
            num_scalar_prefetch=1,
            grid=(chans // CHUNK,),
            in_specs=[block(i // 2) for i in range(len(parts))],
            out_specs=[pl.BlockSpec(out.shape, lambda c, role_ref: (0, 0, 0))] * outputs,
            scratch_shapes=[VMEM((rows, chans, cols), BF16)],
        ),
        out_shape=[out] * outputs,
        compiler_params=params(),
        cost_estimate=cost(0, 6 * parts[0].size),
        name="fold",
    )(role, *parts)


def prepare_kernel(flag_ref, pair_ref, gate_w_ref, pair_out_ref, gate_ref):
    _, half, cols, width = pair_ref.shape
    block = cols // 2
    front = flag_ref[0] == 0

    def step(i, carry):
        first = jnp.minimum(2 * i, half - 2)
        pair = []
        for h, r in [(h, first + e) for h in range(2) for e in range(2)]:
            row = pair_ref[h, r].astype(F32)
            pair.append(jnp.where(front, row[:block], row[block:]))
        pair = jnp.concatenate(pair, axis=0).T
        normed = norm_chans(pair).astype(BF16)
        pair_out_ref[i, :, : 4 * block] = pair.astype(BF16)
        gate = jnp.dot(gate_w_ref[...], normed, preferred_element_type=F32)
        gate_ref[i, :, : 4 * block] = twice_sigmoid(gate)
        return carry

    lax.fori_loop(0, pair_out_ref.shape[0], step, 0, unroll=4)


def prepare(flag, pair, gate_w):
    _, half, cols, width = pair.shape
    shape = ((half + 1) // 2, width, padded(2 * cols, 128))
    return pl.pallas_call(
        prepare_kernel,
        out_shape=(jax.ShapeDtypeStruct(shape, BF16), jax.ShapeDtypeStruct(shape, F32)),
        in_specs=[pl.BlockSpec(memory_space=pltpu.SMEM)] + whole(2),
        out_specs=whole(2),
        compiler_params=params(),
        cost_estimate=cost(pair.size * width, 6 * pair.size, pair.size // 2),
        name="prepare",
    )(flag, pair, gate_w)


def finish_kernel(flag_ref, pair_ref, gate_ref, own_ref, *refs, cols, sources):
    other_refs, refs = refs[:sources], refs[sources:]
    out_w_ref, in_ref, back_ref = refs[:3]
    earlier_ref, out_ref = refs[3] if len(refs) == 5 else None, refs[-1]
    steps, width, _ = pair_ref.shape
    half = own_ref.shape[0]
    block, chans = cols // 2, width // 2
    hidden_units = back_ref.shape[1]
    front = flag_ref[0] == 0

    def step(i, carry):
        first = jnp.minimum(2 * i, half - 2)
        rows = [(h, first + e) for h in range(2) for e in range(2)]
        others = [sum(ref[first + e] for ref in other_refs) for e in range(2)]
        turned = [[v.T[:, :block] for v in (own_ref[first + e], others[e])] for e in range(2)]
        tri = [
            jnp.concatenate([t[h * chans : (h + 1) * chans] for t in turned[e]], axis=0)
            for h in range(2)
            for e in range(2)
        ]
        tri_normed = norm_chans(jnp.concatenate(tri, axis=1).astype(F32)).astype(BF16)
        pair = pair_ref[i, :, : 4 * block].astype(F32)
        update = jnp.dot(out_w_ref[...], tri_normed, preferred_element_type=F32)
        updated = pair + gate_ref[i, :, : 4 * block] * update
        trans_normed = norm_chans(updated).astype(BF16)
        expanded = jnp.dot(in_ref[...], trans_normed, preferred_element_type=F32)
        swish, linear = expanded[:hidden_units], expanded[hidden_units:]
        hidden = (swish * twice_sigmoid(swish) * linear).astype(BF16)
        result = updated + jnp.dot(back_ref[...], hidden, preferred_element_type=F32)
        result = result.T
        for s, (h, r) in enumerate(rows):
            mine = result[s * block : (s + 1) * block]
            if earlier_ref is None:
                out_ref[h, r, :block] = mine.astype(BF16)
            else:
                past = earlier_ref[h, r].astype(F32)[:block]
                parts = [jnp.where(front, mine, past), jnp.where(front, past, mine)]
                out_ref[h, r] = jnp.concatenate(parts, axis=0).astype(BF16)
        return carry

    lax.fori_loop(0, steps, step, 0, unroll=6)


def finish(flag, cols, prepared, own, others, weights, earlier=None):
    half, _, width = own.shape
    shape = (2, half, padded(cols // 2, 16) if earlier is None else cols, width)
    extra = [] if earlier is None else [earlier]
    size = own.size * 2
    return pl.pallas_call(
        functools.partial(finish_kernel, cols=cols, sources=len(others)),
        out_shape=jax.ShapeDtypeStruct(shape, BF16),
        in_specs=[pl.BlockSpec(memory_space=pltpu.SMEM)] + whole(6 + len(others) + len(extra)),
        out_specs=pl.BlockSpec(memory_space=VMEM),
        compiler_params=params(),
        cost_estimate=cost(26 * size * width, 10 * size, 5 * size),
        name="finish",
    )(flag, *prepared, own, *others, *weights, *extra)


def layer_norm(values):
    centered = values - jnp.mean(values, axis=-1, keepdims=True)
    variance = jnp.mean(centered * centered, axis=-1, keepdims=True)
    return centered * lax.rsqrt(variance + 1e-05)


def any_mesh(pair, chain_lengths, in_weight, out_weight, trans_in, trans_out):
    tile_rows, tile_cols, width = pair.shape
    hidden_units = trans_out.shape[0]
    row_count = lax.axis_size("row")
    col_count = lax.axis_size("col")
    outer = row_count // 2
    tokens = tile_rows * row_count
    valid_count = tokens - chain_lengths[chain_lengths.shape[0] - 1]
    row_id = lax.axis_index("row")
    col_id = lax.axis_index("col")
    line_id = row_id // 2

    def along_line(value, step, targets):
        perm = [(2 * (t - step) + b, 2 * t + b) for t in targets for b in range(2)]
        return lax.ppermute(value, "row", perm)

    row_pos = row_id * tile_rows + jnp.arange(tile_rows, dtype=jnp.int32)
    col_pos = col_id * tile_cols + jnp.arange(tile_cols, dtype=jnp.int32)
    pair_mask = ((row_pos < valid_count)[:, None] & (col_pos < valid_count)[None, :]).astype(
        jnp.float32
    )[:, :, None]
    normed = layer_norm(pair.astype(jnp.float32)).astype(jnp.bfloat16).reshape(-1, width)

    def gated(offset):
        block = jnp.dot(
            normed,
            in_weight[:, offset * width : (offset + 2) * width],
            preferred_element_type=jnp.float32,
        ).reshape(tile_rows, tile_cols, 2 * width)
        value = jax.nn.sigmoid(block[..., :width]) * block[..., width:] * pair_mask
        return value.astype(jnp.bfloat16)

    right_ops = gated(2)
    from_left, from_right = {0: right_ops}, {0: right_ops}
    for step in range(1, outer):
        from_left[step] = along_line(from_left[step - 1], 1, range(step, outer))
        from_right[step] = along_line(from_right[step - 1], -1, range(0, outer - step))
    left_ops = gated(0)
    left_other = lax.ppermute(left_ops, "row", [(i, i ^ 1) for i in range(row_count)])
    lefts = jnp.concatenate([left_ops, left_other], axis=0)

    partials = []
    for source in range(outer):
        block = right_ops
        for step in range(1, outer):
            if source + step < outer:
                block = jnp.where(line_id == source + step, from_left[step], block)
            if source - step >= 0:
                block = jnp.where(line_id == source - step, from_right[step], block)
        partials.append(
            jnp.einsum("ikc,jkc->ijc", lefts, block, preferred_element_type=jnp.float32)
        )
    partial = jnp.stack(partials)
    share = outer // col_count
    mine = lax.dynamic_slice_in_dim(partial, col_id * share, share, 0)
    for hop in range(1, col_count):
        target = (col_id + hop) % col_count
        passed = lax.dynamic_slice_in_dim(partial, target * share, share, 0)
        mine = mine + lax.ppermute(
            passed, "col", [(c, (c + hop) % col_count) for c in range(col_count)]
        )
    tri_normed = layer_norm(mine).astype(jnp.bfloat16)
    own_part = tri_normed[:, :tile_rows]
    other_part = lax.ppermute(
        tri_normed[:, tile_rows:], "row", [(i, i ^ 1) for i in range(row_count)]
    )
    even = row_id % 2 == 0
    both = jnp.stack(
        [jnp.where(even, own_part, other_part), jnp.where(even, other_part, own_part)], axis=1
    )
    tri_normed = both.transpose(2, 0, 1, 3, 4).reshape(-1, width)

    out_gate = jax.nn.sigmoid(
        jnp.dot(normed, in_weight[:, 4 * width :], preferred_element_type=jnp.float32)
    )
    update = jnp.dot(tri_normed, out_weight, preferred_element_type=jnp.float32)
    updated = pair.astype(jnp.float32).reshape(-1, width) + out_gate * update
    trans_normed = layer_norm(updated).astype(jnp.bfloat16)
    expanded = jnp.dot(trans_normed, trans_in, preferred_element_type=jnp.float32)
    hidden = (jax.nn.silu(expanded[:, :hidden_units]) * expanded[:, hidden_units:]).astype(
        jnp.bfloat16
    )
    result = updated + jnp.dot(hidden, trans_out, preferred_element_type=jnp.float32)
    return result.reshape(tile_rows, tile_cols, width).astype(jnp.bfloat16)


def per_device(pair, chain_lengths, in_weight, out_weight, trans_in, trans_out):
    if (lax.axis_size("row"), lax.axis_size("col")) != (8, 2):
        return any_mesh(pair, chain_lengths, in_weight, out_weight, trans_in, trans_out)
    return two_by_four(pair, chain_lengths, in_weight, out_weight, trans_in, trans_out)


def two_by_four(pair, chain_lengths, in_weight, out_weight, trans_in, trans_out):
    tile_rows, tile_cols, width = pair.shape
    half = tile_rows // 2
    tokens = tile_rows * lax.axis_size("row")
    valid_count = tokens - chain_lengths[chain_lengths.shape[0] - 1]
    row_id, core = lax.axis_index("row"), lax.axis_index("col")
    place, side = row_id // 2, row_id % 2
    keeper = place // 2

    def among(value, moves):
        return lax.ppermute(value, "row", [(2 * s + b, 2 * t + b) for s, t in moves for b in range(2)])

    def across(value):
        return lax.ppermute(value, "row", [(i, i ^ 1) for i in range(8)])

    def to_core(value, places, keep):
        perm = []
        for z, towards in zip(places, keep):
            target = z // 2 if towards else 1 - z // 2
            perm += [(4 * z + 2 * b + 1 - target, 4 * z + 2 * b + target) for b in range(2)]
        return lax.ppermute(value, ("row", "col"), perm)

    def give_back(value, swap):
        perm = []
        for s, t in ((1, 0), (2, 3)):
            away = 1 - t // 2
            source = 1 - away if swap else away
            perm += [(4 * s + 2 * b + source, 4 * t + 2 * (b ^ swap) + away) for b in range(2)]
        return lax.ppermute(value, ("row", "col"), perm)

    def side_to_side(value, places, holders):
        perm = []
        for z, holder in zip(places, holders):
            perm += [(4 * z + 2 * b + holder, 4 * z + 2 * (1 - b) + holder) for b in range(2)]
        return lax.ppermute(value, ("row", "col"), perm)

    def by_side(block, axis):
        return jnp.where(side == 0, block, jnp.roll(block, width // 2, axis))

    def after(value, *others):
        return lax.optimization_barrier((value, *others))[0]

    def scalars(*values):
        return jnp.stack([jnp.asarray(v).astype(jnp.int32) for v in values])

    is_keeper = core == keeper
    inner = (place == 1) | (place == 2)
    where = scalars(valid_count, row_id * tile_rows, core * tile_cols, side)
    folded = pair.reshape(2, half, tile_cols, width)
    cross = [(1, 2), (2, 1)]
    everyone, inners = range(4), (1, 2)

    def phase(moves, finished):
        values = lax.optimization_barrier(tuple(v for _, v in moves) + tuple(finished))
        return [send(v) for (send, _), v in zip(moves, values)]

    def hop(moves):
        return lambda value: among(value, moves)

    def either(at_inner, at_end):
        return jnp.where(inner, at_inner, at_end)

    swap = hop([(0, 1), (1, 0), (2, 3), (3, 2)])
    right_own, right_far = project(where, folded, in_weight, 2)
    one = phase([(swap, right_own), (hop(cross), right_own), (across, right_far)], ())
    mate_own, near_own, right_beside = one
    order = jnp.where(is_keeper, place % 2, place // 2)
    weights = [
        by_side(out_weight, 0).T * BF16(0.5),
        jnp.where(jnp.arange(trans_in.shape[1])[:, None] < trans_out.shape[0], BF16(0.5), BF16(1.0))
        * trans_in.T,
        trans_out.T,
    ]
    gate_weight = in_weight[:, 4 * width :].T * BF16(0.5)
    left_own, left_far = project(where, folded, in_weight, 0)
    two = phase(
        [(swap, either(near_own, right_beside)), (hop(cross), right_beside), (across, left_far)],
        one + weights + [gate_weight],
    )
    prepared = [prepare(scalars(f), after(folded, *one), gate_weight) for f in (order, 1 - order)]
    mate_beside, near_beside, left_beside = two
    three = phase(
        [(swap, either(near_beside, left_own)), (hop(cross), mate_own)],
        (near_beside, left_beside, *prepared[0], *prepared[1]),
    )
    guest_own, far_own = three

    left = left_major(left_own, left_beside)
    plain, outer = scalars(side, 0), scalars(side, jnp.where(inner, 0, 1))
    (home,) = triangle(plain, left, [[right_own], [right_beside]])
    home_rest = to_core(home, everyone, [True] * 4)
    (mate,) = triangle(plain, left, [[mate_own], [mate_beside]])
    mate_rest = to_core(mate, inners, [True] * 2)
    four = phase(
        [(swap, either(right_beside, left_beside)), (hop(cross), mate_beside)], three + [home, mate]
    )
    guest_beside, far_beside = four

    (away,) = triangle(
        outer,
        left,
        [[after(near_own, far_own, mate)], [near_beside], [mate_beside], [guest_own]],
    )
    away_rest = to_core(away, everyone, [False] * 4)
    role = scalars(jnp.where(is_keeper, 0, 1))
    first = fold(half, role, home, home_rest, away, away_rest)
    first_other = across(first[1])
    mate_block = fold(half, role, mate, mate_rest)
    mate_other = side_to_side(mate_block[1], inners, (0, 1))

    late, lent_own, lent_beside = triangle(
        outer,
        left,
        [[after(far_own, mate_other)], [far_beside], [mate_own], [guest_beside]],
        [[guest_own], [guest_beside]],
    )
    lent_rest = to_core(lent_own, inners, [False] * 2), to_core(lent_beside, inners, [True] * 2)
    late_rest = to_core(late, everyone, [True, False, False, True])
    (lent,) = fold(half, role, lent_beside, lent_rest[1], lent_own, lent_rest[0])
    given = give_back(lent, 0), give_back(after(lent, first_other), 1)
    late_block = fold(half, role, late, late_rest)
    late_other = side_to_side(late_block[1], everyone, (0, 1, 0, 1))

    earlier = finish(
        scalars(order), tile_cols, prepared[0], after(first[0], lent), [first_other], weights
    )
    own = jnp.where(
        inner & is_keeper, mate_block[0], jnp.where(inner | is_keeper, late_block[0], given[0])
    )
    others = [mate_other, late_other, given[1]]
    result = finish(scalars(1 - order), tile_cols, prepared[1], own, others, weights, earlier)
    return result.reshape(tile_rows, tile_cols, width)


def solution(mesh):
    placed = (P(("crops", "row"), "col", None), P("crops"), P(), P(), P(), P())
    return jax.shard_map(
        per_device,
        mesh=mesh,
        in_specs=placed,
        out_specs=P(("crops", "row"), "col", None),
        check_vma=False,
    )
```

```python
import functools

import jax
import jax.numpy as jnp
from jax import lax
from jax.experimental import pallas as pl
from jax.experimental.pallas import tpu as pltpu
from jax.sharding import PartitionSpec as P

VMEM = pltpu.VMEM
BF16, F32 = jnp.bfloat16, jnp.float32
CHUNK = 16


def whole(count):
    return [pl.BlockSpec(memory_space=VMEM)] * count


def params():
    return pltpu.CompilerParams(vmem_limit_bytes=20 << 20)


def cost(flops, moved, transcendentals=0):
    return pl.CostEstimate(flops=flops, bytes_accessed=moved, transcendentals=transcendentals)


def twice_sigmoid(halved):
    return jnp.tanh(halved) + 1.0


def norm_chans(values):
    centered = values - jnp.mean(values, axis=0, keepdims=True)
    variance = jnp.mean(centered * centered, axis=0, keepdims=True)
    return centered * lax.rsqrt(variance + 1e-05)


def padded(count, unit):
    return -(-count // unit) * unit


def project_kernel(where_ref, pair_hbm, weight_ref, own_ref, far_ref, pair_ref, both_ref, sems, first):
    valid, row0, col0, side = (where_ref[i] for i in range(4))
    _, half, cols, width = pair_ref.shape
    chans = width // 2
    tail = cols - width
    count = sems.shape[0]
    size = -(-half // count)
    spans = [(k * size, min(size, half - k * size)) for k in range(count)]
    loads = [
        pltpu.make_async_copy(
            pair_hbm.at[:, pl.ds(start, length)], pair_ref.at[:, pl.ds(start, length)], sems.at[k]
        )
        for k, (start, length) in enumerate(spans)
    ]
    for load in loads:
        load.start()

    for i in range(2):
        block = weight_ref[:, (first + i) * width : (first + i + 1) * width].astype(F32)
        block = jnp.where(side == 0, block, pltpu.roll(block, chans, 1))
        both_ref[i * width : (i + 1) * width] = (block.T * 0.5).astype(BF16)

    lane = lax.broadcasted_iota(jnp.int32, (1, 3 * width), 1)
    in_tail = lane >= 2 * width
    ends = jnp.where(in_tail, 2 * width + chans, width)
    is_first = jnp.where(lane < ends, 1, 0)
    token = jnp.where(in_tail, lane % chans + width, lane % width) + col0
    gap = jnp.zeros((chans - tail, width), F32)

    def step(r, carry):
        first, second = (pair_ref[h, r].astype(F32) for h in range(2))
        tokens = jnp.concatenate(
            [first[:width], second[:width], first[width:], gap, second[width:], gap], axis=0
        )
        normed = norm_chans(tokens.T).astype(BF16)
        both = jnp.dot(both_ref[...], normed, preferred_element_type=F32)
        limits = [jnp.where(row0 + h * half + r < valid, valid, 0) for h in range(2)]
        keep = jnp.where(token < limits[1] + is_first * (limits[0] - limits[1]), 1.0, 0.0)
        out = (twice_sigmoid(both[:width]) * both[width:] * keep).astype(BF16)
        own_ref[r] = out[:chans]
        far_ref[r] = out[chans:]
        return carry

    for load, (start, length) in zip(loads, spans):
        load.wait()
        lax.fori_loop(start, start + length, step, 0, unroll=3)


def project(where, pair, weight, first):
    _, half, cols, width = pair.shape
    piece = jax.ShapeDtypeStruct((half, width // 2, 3 * width), BF16)
    return pl.pallas_call(
        functools.partial(project_kernel, first=first),
        out_shape=(piece, piece),
        in_specs=[
            pl.BlockSpec(memory_space=pltpu.SMEM),
            pl.BlockSpec(memory_space=pl.ANY),
            pl.BlockSpec(memory_space=VMEM),
        ],
        out_specs=whole(2),
        scratch_shapes=[
            VMEM(pair.shape, BF16),
            VMEM((2 * width, width), BF16),
            pltpu.SemaphoreType.DMA((4,)),
        ],
        compiler_params=params(),
        cost_estimate=cost(4 * pair.size * width, 4 * pair.size, pair.size),
        name="project",
    )(where, pair, weight)


def channel_major(pieces, left):
    half, chans, lanes = pieces[0].shape
    width = lanes // 3
    main, rest = [], []
    for piece in pieces:
        tail = piece[:, :, 2 * width :]
        turned = jnp.concatenate([tail[:, :, width // 2 :], tail[:, :, : width // 2]], axis=2)
        main += [piece[:, :, :width], piece[:, :, width : 2 * width]]
        rest += [tail, turned]
        if left:
            gap = jnp.zeros((padded(2 * half, 16) - 2 * half, chans, width), BF16)
            main.append(gap)
            rest.append(gap)
    rest = jnp.concatenate(rest, axis=0)
    if left:
        low = lax.broadcasted_iota(jnp.int32, rest.shape, 2) < width // 2
        rest = jnp.where(low, rest, jnp.zeros_like(rest))
    main = jnp.swapaxes(jnp.concatenate(main, axis=0), 0, 1)
    return main, jnp.swapaxes(rest, 0, 1)


def left_kernel(own_ref, beside_ref, out_ref):
    width = own_ref.shape[2] // 3
    main, rest = channel_major([own_ref[...], beside_ref[...]], True)
    out_ref[:, :, :width] = main
    out_ref[:, :, width:] = rest


def left_major(own, beside):
    half, chans, lanes = own.shape
    rows, deep = 2 * padded(2 * half, 16), lanes // 3 * 2
    piece = pl.BlockSpec((half, CHUNK, lanes), lambda c: (0, c, 0))
    return pl.pallas_call(
        left_kernel,
        grid=(chans // CHUNK,),
        out_shape=jax.ShapeDtypeStruct((chans, rows, deep), BF16),
        in_specs=[piece, piece],
        out_specs=pl.BlockSpec((CHUNK, rows, deep), lambda c: (c, 0, 0)),
        compiler_params=params(),
        cost_estimate=cost(0, 8 * own.size),
        name="left_major",
    )(own, beside)


def triangle_kernel(flag_ref, left_ref, *refs, counts, guests, options):
    pieces, refs = [], list(refs)
    for count in counts:
        parts = [refs.pop(0)[...] for _ in range(count)]
        pieces.append(parts[0] if count == 1 else jnp.concatenate(parts, axis=0))
    outs, work = refs[: 1 + guests], refs[1 + guests :]
    visitors, rights = pieces[:guests], pieces[guests:]
    own, beside = rights[:2]
    if options == 2:
        plain = flag_ref[1] == 0
        own = jnp.where(plain, own, rights[2])
        beside = jnp.where(plain, beside, rights[3])
    width = own.shape[2] // 3
    even = flag_ref[0] == 0
    right_ref = work[0]
    main, rest = channel_major(
        [jnp.where(even, own, beside), jnp.where(even, beside, own)], False
    )
    rows = main.shape[1]

    @pl.when(pl.program_id(0) == 0)
    def _():
        right_ref[...] = jnp.zeros_like(right_ref)

    right_ref[:, :rows, :width] = main
    right_ref[:, :rows, width:] = rest
    if guests:
        guest_ref = work[1]
        main, rest = channel_major(visitors, True)
        guest_ref[:, :, :width] = main
        guest_ref[:, :, width:] = rest

    def product(rows):
        dims = (((1,), (1,)), ((), ()))
        return lax.dot_general(rows, right_ref[c], dims, preferred_element_type=F32).astype(BF16)

    for c in range(CHUNK):
        outs[0][c] = product(left_ref[c])
        if guests:
            lent = product(guest_ref[c])
            part = lent.shape[0] // guests
            for g in range(guests):
                outs[1 + g][c] = lent[g * part : (g + 1) * part]


def triangle(flags, left, pieces, guests=()):
    chans, rows, deep = left.shape
    lanes, half = deep // 2 * 3, sum(part.shape[0] for part in pieces[0])
    options, cols = len(pieces) // 2, padded(4 * half, 128)

    def spec(part, option):
        def at(c, flag_ref):
            return (0, c if option is None else jnp.where(flag_ref[1] == option, c, 0), 0)

        return pl.BlockSpec((part.shape[0], CHUNK, lanes), at)

    def block(height, depth):
        return pl.BlockSpec((CHUNK, height, depth), lambda c, flag_ref: (c, 0, 0))

    specs = [spec(part, None) for piece in guests for part in piece]
    for i, piece in enumerate(pieces):
        specs += [spec(part, i // 2 if options == 2 else None) for part in piece]
    heights = [rows] + [rows // 2] * len(guests)
    work = [VMEM((CHUNK, cols, deep), BF16)]
    if guests:
        work.append(VMEM((CHUNK, rows, deep), BF16))
    everything = list(guests) + list(pieces)
    return pl.pallas_call(
        functools.partial(
            triangle_kernel,
            counts=[len(piece) for piece in everything],
            guests=len(guests),
            options=options,
        ),
        grid_spec=pltpu.PrefetchScalarGridSpec(
            num_scalar_prefetch=1,
            grid=(chans // CHUNK,),
            in_specs=[block(rows, deep)] + specs,
            out_specs=[block(h, cols) for h in heights],
            scratch_shapes=work,
        ),
        out_shape=[jax.ShapeDtypeStruct((chans, h, cols), BF16) for h in heights],
        compiler_params=params(),
        cost_estimate=cost(2 * chans * sum(heights) * cols * deep, 10 * half * chans * lanes),
        name="triangle",
    )(flags, left, *[part for piece in everything for part in piece])


def fold_kernel(role_ref, *refs, outputs, half):
    outs, work_ref = refs[-1 - outputs : -1], refs[-1]
    cols = outs[0].shape[1]
    parts = refs[: -1 - outputs]
    c = pl.program_id(0)
    options = len(parts) // 2
    for option in range(options):

        @pl.when((options == 1) | (role_ref[0] == option))
        def _(option=option):
            total = parts[2 * option][...].astype(F32) + parts[2 * option + 1][...].astype(F32)
            at = pl.ds(pl.multiple_of(c * CHUNK, CHUNK), CHUNK)
            work_ref[:, at, :] = jnp.swapaxes(total.astype(BF16), 0, 1)

    @pl.when(c == pl.num_programs(0) - 1)
    def _():
        pitch = work_ref.shape[0] // outputs
        for o, out_ref in enumerate(outs):

            def turn(r, carry, o=o, out_ref=out_ref):
                at = o * pitch + r
                stacked = jnp.concatenate([work_ref[at], work_ref[at + half]], axis=0)
                out_ref[r] = stacked.T[:cols]
                return carry

            lax.fori_loop(0, half, turn, 0, unroll=True)


def fold(half, role, *parts):
    chans, rows, cols = parts[0].shape
    outputs = rows // padded(2 * half, 16)
    out = jax.ShapeDtypeStruct((half, padded(4 * half, 16), 2 * chans), BF16)

    def block(option):
        return pl.BlockSpec(
            (CHUNK, rows, cols),
            lambda c, role_ref: (
                c if len(parts) == 2 else jnp.where(role_ref[0] == option, c, 0), 0, 0
            ),
        )

    return pl.pallas_call(
        functools.partial(fold_kernel, outputs=outputs, half=half),
        grid_spec=pltpu.PrefetchScalarGridSpec(
            num_scalar_prefetch=1,
            grid=(chans // CHUNK,),
            in_specs=[block(i // 2) for i in range(len(parts))],
            out_specs=[pl.BlockSpec(out.shape, lambda c, role_ref: (0, 0, 0))] * outputs,
            scratch_shapes=[VMEM((rows, chans, cols), BF16)],
        ),
        out_shape=[out] * outputs,
        compiler_params=params(),
        cost_estimate=cost(0, 6 * parts[0].size),
        name="fold",
    )(role, *parts)


def prepare_kernel(flag_ref, pair_ref, gate_w_ref, pair_out_ref, gate_ref):
    _, half, cols, width = pair_ref.shape
    block = cols // 2
    front = flag_ref[0] == 0

    def step(i, carry):
        first = jnp.minimum(2 * i, half - 2)
        pair = []
        for h, r in [(h, first + e) for h in range(2) for e in range(2)]:
            row = pair_ref[h, r].astype(F32)
            pair.append(jnp.where(front, row[:block], row[block:]))
        pair = jnp.concatenate(pair, axis=0).T
        normed = norm_chans(pair).astype(BF16)
        pair_out_ref[i, :, : 4 * block] = pair.astype(BF16)
        gate = jnp.dot(gate_w_ref[...], normed, preferred_element_type=F32)
        gate_ref[i, :, : 4 * block] = twice_sigmoid(gate)
        return carry

    lax.fori_loop(0, pair_out_ref.shape[0], step, 0, unroll=4)


def prepare(flag, pair, gate_w):
    _, half, cols, width = pair.shape
    shape = ((half + 1) // 2, width, padded(2 * cols, 128))
    return pl.pallas_call(
        prepare_kernel,
        out_shape=(jax.ShapeDtypeStruct(shape, BF16), jax.ShapeDtypeStruct(shape, F32)),
        in_specs=[pl.BlockSpec(memory_space=pltpu.SMEM)] + whole(2),
        out_specs=whole(2),
        compiler_params=params(),
        cost_estimate=cost(pair.size * width, 6 * pair.size, pair.size // 2),
        name="prepare",
    )(flag, pair, gate_w)


def finish_kernel(flag_ref, pair_ref, gate_ref, own_ref, other_ref, *refs, cols):
    out_w_ref, in_ref, back_ref = refs[:3]
    earlier_ref, out_ref = refs[3] if len(refs) == 5 else None, refs[-1]
    steps, width, _ = pair_ref.shape
    half = own_ref.shape[0]
    block, chans = cols // 2, width // 2
    hidden_units = back_ref.shape[1]
    front = flag_ref[0] == 0

    def step(i, carry):
        first = jnp.minimum(2 * i, half - 2)
        rows = [(h, first + e) for h in range(2) for e in range(2)]
        turned = [[ref[first + e].T[:, :block] for ref in (own_ref, other_ref)] for e in range(2)]
        tri = [
            jnp.concatenate([t[h * chans : (h + 1) * chans] for t in turned[e]], axis=0)
            for h in range(2)
            for e in range(2)
        ]
        tri_normed = norm_chans(jnp.concatenate(tri, axis=1).astype(F32)).astype(BF16)
        pair = pair_ref[i, :, : 4 * block].astype(F32)
        update = jnp.dot(out_w_ref[...], tri_normed, preferred_element_type=F32)
        updated = pair + gate_ref[i, :, : 4 * block] * update
        trans_normed = norm_chans(updated).astype(BF16)
        expanded = jnp.dot(in_ref[...], trans_normed, preferred_element_type=F32)
        swish, linear = expanded[:hidden_units], expanded[hidden_units:]
        hidden = (swish * twice_sigmoid(swish) * linear).astype(BF16)
        result = updated + jnp.dot(back_ref[...], hidden, preferred_element_type=F32)
        result = result.T
        for s, (h, r) in enumerate(rows):
            mine = result[s * block : (s + 1) * block]
            if earlier_ref is None:
                out_ref[h, r, :block] = mine.astype(BF16)
            else:
                past = earlier_ref[h, r].astype(F32)[:block]
                parts = [jnp.where(front, mine, past), jnp.where(front, past, mine)]
                out_ref[h, r] = jnp.concatenate(parts, axis=0).astype(BF16)
        return carry

    lax.fori_loop(0, steps, step, 0, unroll=6)


def finish(flag, cols, prepared, own, other, weights, earlier=None):
    half, _, width = own.shape
    shape = (2, half, padded(cols // 2, 16) if earlier is None else cols, width)
    extra = [] if earlier is None else [earlier]
    size = own.size * 2
    return pl.pallas_call(
        functools.partial(finish_kernel, cols=cols),
        out_shape=jax.ShapeDtypeStruct(shape, BF16),
        in_specs=[pl.BlockSpec(memory_space=pltpu.SMEM)] + whole(7 + len(extra)),
        out_specs=pl.BlockSpec(memory_space=VMEM),
        compiler_params=params(),
        cost_estimate=cost(26 * size * width, 10 * size, 5 * size),
        name="finish",
    )(flag, *prepared, own, other, *weights, *extra)


def layer_norm(values):
    centered = values - jnp.mean(values, axis=-1, keepdims=True)
    variance = jnp.mean(centered * centered, axis=-1, keepdims=True)
    return centered * lax.rsqrt(variance + 1e-05)


def any_mesh(pair, chain_lengths, in_weight, out_weight, trans_in, trans_out):
    tile_rows, tile_cols, width = pair.shape
    hidden_units = trans_out.shape[0]
    row_count = lax.axis_size("row")
    col_count = lax.axis_size("col")
    outer = row_count // 2
    tokens = tile_rows * row_count
    valid_count = tokens - chain_lengths[chain_lengths.shape[0] - 1]
    row_id = lax.axis_index("row")
    col_id = lax.axis_index("col")
    line_id = row_id // 2

    def along_line(value, step, targets):
        perm = [(2 * (t - step) + b, 2 * t + b) for t in targets for b in range(2)]
        return lax.ppermute(value, "row", perm)

    row_pos = row_id * tile_rows + jnp.arange(tile_rows, dtype=jnp.int32)
    col_pos = col_id * tile_cols + jnp.arange(tile_cols, dtype=jnp.int32)
    pair_mask = ((row_pos < valid_count)[:, None] & (col_pos < valid_count)[None, :]).astype(
        jnp.float32
    )[:, :, None]
    normed = layer_norm(pair.astype(jnp.float32)).astype(jnp.bfloat16).reshape(-1, width)

    def gated(offset):
        block = jnp.dot(
            normed,
            in_weight[:, offset * width : (offset + 2) * width],
            preferred_element_type=jnp.float32,
        ).reshape(tile_rows, tile_cols, 2 * width)
        value = jax.nn.sigmoid(block[..., :width]) * block[..., width:] * pair_mask
        return value.astype(jnp.bfloat16)

    right_ops = gated(2)
    from_left, from_right = {0: right_ops}, {0: right_ops}
    for step in range(1, outer):
        from_left[step] = along_line(from_left[step - 1], 1, range(step, outer))
        from_right[step] = along_line(from_right[step - 1], -1, range(0, outer - step))
    left_ops = gated(0)
    left_other = lax.ppermute(left_ops, "row", [(i, i ^ 1) for i in range(row_count)])
    lefts = jnp.concatenate([left_ops, left_other], axis=0)

    partials = []
    for source in range(outer):
        block = right_ops
        for step in range(1, outer):
            if source + step < outer:
                block = jnp.where(line_id == source + step, from_left[step], block)
            if source - step >= 0:
                block = jnp.where(line_id == source - step, from_right[step], block)
        partials.append(
            jnp.einsum("ikc,jkc->ijc", lefts, block, preferred_element_type=jnp.float32)
        )
    partial = jnp.stack(partials)
    share = outer // col_count
    mine = lax.dynamic_slice_in_dim(partial, col_id * share, share, 0)
    for hop in range(1, col_count):
        target = (col_id + hop) % col_count
        passed = lax.dynamic_slice_in_dim(partial, target * share, share, 0)
        mine = mine + lax.ppermute(
            passed, "col", [(c, (c + hop) % col_count) for c in range(col_count)]
        )
    tri_normed = layer_norm(mine).astype(jnp.bfloat16)
    own_part = tri_normed[:, :tile_rows]
    other_part = lax.ppermute(
        tri_normed[:, tile_rows:], "row", [(i, i ^ 1) for i in range(row_count)]
    )
    even = row_id % 2 == 0
    both = jnp.stack(
        [jnp.where(even, own_part, other_part), jnp.where(even, other_part, own_part)], axis=1
    )
    tri_normed = both.transpose(2, 0, 1, 3, 4).reshape(-1, width)

    out_gate = jax.nn.sigmoid(
        jnp.dot(normed, in_weight[:, 4 * width :], preferred_element_type=jnp.float32)
    )
    update = jnp.dot(tri_normed, out_weight, preferred_element_type=jnp.float32)
    updated = pair.astype(jnp.float32).reshape(-1, width) + out_gate * update
    trans_normed = layer_norm(updated).astype(jnp.bfloat16)
    expanded = jnp.dot(trans_normed, trans_in, preferred_element_type=jnp.float32)
    hidden = (jax.nn.silu(expanded[:, :hidden_units]) * expanded[:, hidden_units:]).astype(
        jnp.bfloat16
    )
    result = updated + jnp.dot(hidden, trans_out, preferred_element_type=jnp.float32)
    return result.reshape(tile_rows, tile_cols, width).astype(jnp.bfloat16)


def per_device(pair, chain_lengths, in_weight, out_weight, trans_in, trans_out):
    if (lax.axis_size("row"), lax.axis_size("col")) != (8, 2):
        return any_mesh(pair, chain_lengths, in_weight, out_weight, trans_in, trans_out)
    return two_by_four(pair, chain_lengths, in_weight, out_weight, trans_in, trans_out)


def two_by_four(pair, chain_lengths, in_weight, out_weight, trans_in, trans_out):
    tile_rows, tile_cols, width = pair.shape
    half = tile_rows // 2
    tokens = tile_rows * lax.axis_size("row")
    valid_count = tokens - chain_lengths[chain_lengths.shape[0] - 1]
    row_id, core = lax.axis_index("row"), lax.axis_index("col")
    place, side = row_id // 2, row_id % 2
    keeper = place // 2

    def among(value, moves):
        return lax.ppermute(value, "row", [(2 * s + b, 2 * t + b) for s, t in moves for b in range(2)])

    def across(value):
        return lax.ppermute(value, "row", [(i, i ^ 1) for i in range(8)])

    def to_core(value, places, keep):
        perm = []
        for z, towards in zip(places, keep):
            target = z // 2 if towards else 1 - z // 2
            perm += [(4 * z + 2 * b + 1 - target, 4 * z + 2 * b + target) for b in range(2)]
        return lax.ppermute(value, ("row", "col"), perm)

    def give_back(value, swap):
        perm = []
        for s, t in ((1, 0), (2, 3)):
            away = 1 - t // 2
            source = 1 - away if swap else away
            perm += [(4 * s + 2 * b + source, 4 * t + 2 * (b ^ swap) + away) for b in range(2)]
        return lax.ppermute(value, ("row", "col"), perm)

    def side_to_side(value, places, holders):
        perm = []
        for z, holder in zip(places, holders):
            perm += [(4 * z + 2 * b + holder, 4 * z + 2 * (1 - b) + holder) for b in range(2)]
        return lax.ppermute(value, ("row", "col"), perm)

    def by_side(block, axis):
        return jnp.where(side == 0, block, jnp.roll(block, width // 2, axis))

    def after(value, *others):
        return lax.optimization_barrier((value, *others))[0]

    def scalars(*values):
        return jnp.stack([jnp.asarray(v).astype(jnp.int32) for v in values])

    is_keeper = core == keeper
    inner = (place == 1) | (place == 2)
    where = scalars(valid_count, row_id * tile_rows, core * tile_cols, side)
    folded = pair.reshape(2, half, tile_cols, width)
    cross = [(1, 2), (2, 1)]
    everyone, inners = range(4), (1, 2)

    def phase(moves, finished):
        values = lax.optimization_barrier(tuple(v for _, v in moves) + tuple(finished))
        return [send(v) for (send, _), v in zip(moves, values)]

    def hop(moves):
        return lambda value: among(value, moves)

    def either(at_inner, at_end):
        return jnp.where(inner, at_inner, at_end)

    swap = hop([(0, 1), (1, 0), (2, 3), (3, 2)])
    right_own, right_far = project(where, folded, in_weight, 2)
    one = phase([(swap, right_own), (hop(cross), right_own), (across, right_far)], ())
    mate_own, near_own, right_beside = one
    order = jnp.where(is_keeper, place % 2, place // 2)
    weights = [
        by_side(out_weight, 0).T * BF16(0.5),
        jnp.where(jnp.arange(trans_in.shape[1])[:, None] < trans_out.shape[0], BF16(0.5), BF16(1.0))
        * trans_in.T,
        trans_out.T,
    ]
    gate_weight = in_weight[:, 4 * width :].T * BF16(0.5)
    left_own, left_far = project(where, folded, in_weight, 0)
    two = phase(
        [(swap, either(near_own, right_beside)), (hop(cross), right_beside), (across, left_far)],
        one + weights + [gate_weight],
    )
    prepared = [prepare(scalars(f), after(folded, *one), gate_weight) for f in (order, 1 - order)]
    mate_beside, near_beside, left_beside = two
    three = phase(
        [(swap, either(near_beside, left_own)), (hop(cross), mate_own)],
        (near_beside, left_beside, *prepared[0], *prepared[1]),
    )
    guest_own, far_own = three

    left = left_major(left_own, left_beside)
    plain, outer = scalars(side, 0), scalars(side, jnp.where(inner, 0, 1))
    (home,) = triangle(plain, left, [[right_own], [right_beside]])
    home_rest = to_core(home, everyone, [True] * 4)
    (mate,) = triangle(plain, left, [[mate_own], [mate_beside]])
    mate_rest = to_core(mate, inners, [True] * 2)
    four = phase(
        [(swap, either(right_beside, left_beside)), (hop(cross), mate_beside)], three + [home, mate]
    )
    guest_beside, far_beside = four

    (away,) = triangle(
        outer,
        left,
        [[after(near_own, far_own, mate)], [near_beside], [mate_beside], [guest_own]],
    )
    away_rest = to_core(away, everyone, [False] * 4)
    role = scalars(jnp.where(is_keeper, 0, 1))
    first = fold(half, role, home, home_rest, away, away_rest)
    first_other = across(first[1])
    mate_block = fold(half, role, mate, mate_rest)
    mate_other = side_to_side(mate_block[1], inners, (0, 1))

    late, lent_own, lent_beside = triangle(
        outer,
        left,
        [[after(far_own, mate_other)], [far_beside], [mate_own], [guest_beside]],
        [[guest_own], [guest_beside]],
    )
    lent_rest = to_core(lent_own, inners, [False] * 2), to_core(lent_beside, inners, [True] * 2)
    late_rest = to_core(late, everyone, [True, False, False, True])
    (lent,) = fold(half, role, lent_beside, lent_rest[1], lent_own, lent_rest[0])
    given = give_back(lent, 0), give_back(lent, 1)
    late_block = fold(half, role, late, late_rest)
    late_other = side_to_side(late_block[1], everyone, (0, 1, 0, 1))

    earlier = finish(
        scalars(order), tile_cols, prepared[0], after(first[0], lent), first_other, weights
    )
    own, other = (
        jnp.where(inner & is_keeper, early, jnp.where(inner | is_keeper, end, back))
        for early, end, back in zip((mate_block[0], mate_other), (late_block[0], late_other), given)
    )
    result = finish(scalars(1 - order), tile_cols, prepared[1], own, other, weights, earlier)
    return result.reshape(tile_rows, tile_cols, width)


def solution(mesh):
    placed = (P(("crops", "row"), "col", None), P("crops"), P(), P(), P(), P())
    return jax.shard_map(
        per_device,
        mesh=mesh,
        in_specs=placed,
        out_specs=P(("crops", "row"), "col", None),
        check_vma=False,
    )
```
